32 devices in a mesh: shard: 4 (over y, x), ctx: 2 (over core), tp: 4 (over z).
Axes of the slice: x: 2, y: 2, z: 4, core: 2. Of those that a mesh axis runs over, the one named last changes fastest.
Arguments:
- hidden: bfloat16 [3, 4, 1024, 2048], P(None, 'shard', ('ctx', 'tp')), may hold values from -6 to 6
- segments: int32 [3, 4, 1024], P(None, 'shard'), may hold values from 0 to 15, never falling along the last dimension, each value on 1 to 512 neighbouring positions
- cotangent: bfloat16 [3, 4, 1024, 2048], P(None, 'shard', ('ctx', 'tp')), may hold values from -6 to 6
- attn_gain: bfloat16 [2048], P(('shard', 'ctx', 'tp')), may hold values from 0.5 to 1.5
- q_weight: bfloat16 [2048, 3072], P(('shard', 'ctx'), 'tp'), may hold values from -0.125 to 0.125
- latent_weight: bfloat16 [2048, 576], P(('shard', 'ctx', 'tp')), may hold values from -0.125 to 0.125
- latent_gain: bfloat16 [512], P(('shard', 'ctx', 'tp')), may hold values from 0.5 to 1.5
- expand_weight: bfloat16 [512, 4096], P(('shard', 'ctx'), 'tp'), may hold values from -0.25 to 0.25
- out_weight: bfloat16 [2048, 2048], P('tp', ('shard', 'ctx')), may hold values from -0.5 to 0.5
- mlp_gain: bfloat16 [2048], P(('shard', 'ctx', 'tp')), may hold values from 0.5 to 1.5
- gate_weight: bfloat16 [2048, 10944], P(('shard', 'ctx'), 'tp'), may hold values from -0.125 to 0.125
- up_weight: bfloat16 [2048, 10944], P(('shard', 'ctx'), 'tp'), may hold values from -0.125 to 0.125
- down_weight: bfloat16 [10944, 2048], P('tp', ('shard', 'ctx')), may hold values from -0.0546875 to 0.0546875
Outputs:
- output: bfloat16 [3, 4, 1024, 2048], P(None, 'shard', ('ctx', 'tp'))
- input_grad: bfloat16 [3, 4, 1024, 2048], P(None, 'shard', ('ctx', 'tp'))
- attn_gain_grad: float32 [2048], P(('shard', 'ctx', 'tp'))
- q_weight_grad: float32 [2048, 3072], P(('shard', 'ctx'), 'tp')
- latent_weight_grad: float32 [2048, 576], P(('shard', 'ctx', 'tp'))
- latent_gain_grad: float32 [512], P(('shard', 'ctx', 'tp'))
- expand_weight_grad: float32 [512, 4096], P(('shard', 'ctx'), 'tp')
- out_weight_grad: float32 [2048, 2048], P('tp', ('shard', 'ctx'))
- mlp_gain_grad: float32 [2048], P(('shard', 'ctx', 'tp'))
- gate_weight_grad: float32 [2048, 10944], P(('shard', 'ctx'), 'tp')
- up_weight_grad: float32 [2048, 10944], P(('shard', 'ctx'), 'tp')
- down_weight_grad: float32 [10944, 2048], P('tp', ('shard', 'ctx'))
The draws below stay inside these ranges and needn't reach their ends.
Inputs may be any that keep to these rules, and one draw needn't show every extreme that they name: `segments`: segment numbers never fall along a sequence; 0 marks padding; a segment holds at most 512 tokens.
All inputs are finite; a program needn't handle non-finite values.
Results may differ from the reference program's by a relative error of at most 0.023.
Values may be sent and summed in bfloat16 or wider, within the bound.
No kernel may reach another device: no remote copies, remote signals or barrier semaphores. Data moves between devices by JAX's collectives and lax.ppermute only.
A program may use at most 232 MiB of HBM per device.

```python
import math
import jax
import jax.numpy as jnp
import numpy as np
from jax import lax

D = 2048
HEADS = 16
NOPE = 128
ROPE = 64
VHEAD = 128
KVRANK = 512
FF = 10944
SEQ_LEN = 1024
MICRO = 3
DOCS = 16
SEQS = 4
DOC_MOST = 512


def level_of(key, dims, pieces, low, top_value):
    loudness = 1.0
    for dim, blocks in pieces:
        draws = jax.random.uniform(jax.random.fold_in(jax.random.fold_in(key, 6), dim), (blocks,), jnp.float32, low / len(pieces), top_value / len(pieces))
        loudness = loudness * jnp.repeat(jnp.exp(draws), dims[dim] // blocks).reshape((-1,) + (1,) * (len(dims) - 1 - dim))
    return loudness


def split_up(number_of, total, most, slope):
    loads = [(1 << 20) // math.isqrt(grade ** slope) + 1 for grade in range(2, number_of + 1)]
    surplus, given = total - most - (number_of - 1), [1] * (number_of - 1)
    while surplus > 0:
        candidates = [i for i in range(number_of - 1) if given[i] < most]
        whole, budget = sum([loads[i] for i in candidates]), surplus
        for i in candidates:
            extra = min(most - given[i], max(1, budget * loads[i] // whole), surplus)
            given[i] = given[i] + extra
            surplus = surplus - extra
    return np.array([most] + given)


def uneven_parts(key, count, total, limit, slope):
    if count == 2:
        one = jax.random.randint(key, (), max(1, total - limit), min(limit, total - 1) + 1)
        return jnp.stack([one, total - one])
    lengths = jnp.asarray(split_up(count, total, limit, slope), jnp.int32)
    pairs = (count - 1) // 2
    giver, receiver = lengths[1:1 + 2 * pairs:2], lengths[2:2 + 2 * pairs:2]
    room = jnp.minimum(giver - 1, limit - receiver)
    moved = jax.random.randint(jax.random.fold_in(key, 1), (pairs,), 0, 1 << 20) % (room + 1)
    lengths = lengths.at[1:1 + 2 * pairs:2].set(giver - moved).at[2:2 + 2 * pairs:2].set(receiver + moved)
    return lengths[jax.random.permutation(jax.random.fold_in(key, 2), count)]


def scatter_about(rng, extent, width, limit, pieces=(), held_as=jnp.bfloat16):
    array = jax.random.normal(rng, extent, jnp.float32) * width
    if len(pieces) > 0:
        array = level_of(rng, extent, pieces, -0.22, 0.18) * array
    return jnp.clip(array, min=-limit, max=limit).astype(held_as)


def setup_inputs(seed: int = 0) -> dict:
    streams_of = jax.random.split(jax.random.key(seed), 14)
    hidden = scatter_about(streams_of[0], (MICRO, SEQS, SEQ_LEN, D), 1.0, 6.0, ((1, 4), (2, 8)))
    segments = jax.vmap(lambda own: jnp.searchsorted(jnp.cumsum(uneven_parts(own, DOCS, SEQ_LEN, DOC_MOST, 2)), jnp.arange(SEQ_LEN), side="right"))(jax.random.split(streams_of[1], MICRO * SEQS)).reshape((MICRO, SEQS, SEQ_LEN)).astype(jnp.int32)
    cotangent = scatter_about(streams_of[2], (MICRO, SEQS, SEQ_LEN, D), 1.0, 6.0, ((1, 4), (2, 8)))
    attn_gain = jnp.clip(1.0 + 0.1 * jax.random.normal(streams_of[3], (D,), jnp.float32), 0.5, 1.5).astype(jnp.bfloat16)
    q_weight = scatter_about(streams_of[4], (D, HEADS * (NOPE + ROPE)), D ** -0.5, 0.125, ((0, 8), (1, 4)))
    latent_weight = scatter_about(streams_of[5], (D, KVRANK + ROPE), D ** -0.5, 0.125, ((0, 32),))
    latent_gain = jnp.clip(1.0 + 0.1 * jax.random.normal(streams_of[6], (KVRANK,), jnp.float32), 0.5, 1.5).astype(jnp.bfloat16)
    expand_weight = scatter_about(streams_of[7], (KVRANK, HEADS * (NOPE + VHEAD)), KVRANK ** -0.5, 0.25, ((0, 8), (1, 4)))
    out_weight = scatter_about(streams_of[8], (HEADS * VHEAD, D), (HEADS * VHEAD // 16) ** -0.5, 0.5, ((0, 4), (1, 8)))
    mlp_gain = jnp.clip(1.0 + 0.1 * jax.random.normal(streams_of[9], (D,), jnp.float32), 0.5, 1.5).astype(jnp.bfloat16)
    gate_weight = scatter_about(streams_of[10], (D, FF), D ** -0.5, 0.125, ((0, 8), (1, 4)))
    up_weight = scatter_about(streams_of[11], (D, FF), D ** -0.5, 0.125, ((0, 8), (1, 4)))
    down_weight = scatter_about(streams_of[12], (FF, D), FF ** -0.5, 0.0546875, ((0, 4), (1, 8)))
    return dict(hidden=hidden, segments=segments, cotangent=cotangent, attn_gain=attn_gain, q_weight=q_weight, latent_weight=latent_weight, latent_gain=latent_gain, expand_weight=expand_weight, out_weight=out_weight, mlp_gain=mlp_gain, gate_weight=gate_weight, up_weight=up_weight, down_weight=down_weight)


@jax.custom_vjp
def low(v):
    return lax.optimization_barrier(v.astype(jnp.bfloat16)).astype(jnp.float32)

@jax.custom_vjp
def low_back(v):
    return v

def low_keep(v):
    return (low(v), None)

def low_pass(kept, grad):
    return (grad,)

def back_keep(v):
    return (v, None)

def back_low(kept, grad):
    return (low(grad),)
low.defvjp(low_keep, low_pass)
low_back.defvjp(back_keep, back_low)
EPSILON = 1e-06
THETA_BASE = 10000.0
NEG_FILL = -1e+30
HIGHEST = lax.Precision.HIGHEST

def matmul(left, right):
    return jnp.dot(left, right, preferred_element_type=jnp.float32, precision=HIGHEST)

def normed(values, gain_vec):
    return values * lax.rsqrt(lax.optimization_barrier(jnp.mean(values * values, axis=-1, keepdims=True)) + EPSILON) * gain_vec

def positions(segment_ids):
    length = segment_ids.shape[0]
    index_row = jnp.arange(length, dtype=jnp.int32)
    begins = jnp.concatenate([jnp.ones((1,), jnp.bool_), segment_ids[1:] != segment_ids[:-1]])
    return index_row - lax.cummax(jnp.where(begins, index_row, 0), axis=0)

def rotary_table(places_in):
    half_width = ROPE // 2
    freqs = THETA_BASE ** (-2.0 * jnp.arange(half_width, dtype=jnp.float32) / ROPE)
    angles = places_in.astype(jnp.float32)[:, None] * freqs[None, :]
    return (jnp.cos(angles), jnp.sin(angles))

def rotate(values, cos_table, sin_table):
    half_width = values.shape[-1] // 2
    first_half = values[..., :half_width]
    second_half = values[..., half_width:]
    return jnp.concatenate([first_half * cos_table - second_half * sin_table, second_half * cos_table + first_half * sin_table], axis=-1)

def layer(inputs, seg_row, params):
    gain_one, w_query, w_latent, gain_kv, w_expand, w_out, gain_two, w_gate, w_up, w_down = params
    length = inputs.shape[0]
    cos_table, sin_table = rotary_table(positions(seg_row))
    normed_one = low(normed(inputs, gain_one))
    query_lin = low_back(matmul(normed_one, w_query)).reshape(length, HEADS, NOPE + ROPE)
    queries = low(jnp.concatenate([query_lin[..., :NOPE], rotate(query_lin[..., NOPE:], cos_table[:, None, :], sin_table[:, None, :])], axis=-1))
    latent_raw = low_back(matmul(normed_one, w_latent))
    latent_all = low(normed(latent_raw[:, :KVRANK], gain_kv))
    rope_all = low(rotate(latent_raw[:, KVRANK:], cos_table, sin_table))
    expanded = low(low_back(matmul(latent_all, w_expand))).reshape(length, HEADS, NOPE + VHEAD)
    keys_all = jnp.concatenate([expanded[..., :NOPE], jnp.broadcast_to(rope_all[:, None, :], (length, HEADS, ROPE))], axis=-1)
    values_all = expanded[..., NOPE:]
    block_rows = min(1024, length)
    key_index = jnp.arange(length, dtype=jnp.int32)
    softmax_scale = (NOPE + ROPE) ** (-0.5)

    def attend(first_idx):
        query_block = lax.dynamic_slice_in_dim(queries, first_idx, block_rows, 0)
        query_index = first_idx + jnp.arange(block_rows, dtype=jnp.int32)
        seg_query = lax.dynamic_slice_in_dim(seg_row, first_idx, block_rows, 0)
        same_doc = (seg_query[:, None] == seg_row[None, :]) & (key_index[None, :] <= query_index[:, None]) & (seg_row[None, :] != 0)
        allowed = same_doc | (key_index[None, :] == query_index[:, None])
        scores = low_back(jnp.einsum('qhd,khd->hqk', query_block, keys_all, precision=HIGHEST)) * softmax_scale
        scores = jnp.where(allowed[None], scores, NEG_FILL)
        probs = jax.nn.softmax(scores, axis=-1)
        return low_back(low(jnp.einsum('hqk,khd->qhd', low(probs), values_all, precision=HIGHEST)))
    block_starts = jnp.arange(length // block_rows, dtype=jnp.int32) * block_rows
    att_flat = lax.map(jax.checkpoint(attend), block_starts).reshape(length, HEADS * VHEAD)
    middle = inputs + low_back(matmul(att_flat, w_out))
    normed_two = low(normed(middle, gain_two))
    gate_val = low_back(matmul(normed_two, w_gate))
    up_val = low_back(matmul(normed_two, w_up))
    hidden_act = low(jax.nn.silu(gate_val) * up_val)
    return middle + low_back(matmul(hidden_act, w_down))

def reference(hidden, segments, cotangent, attn_gain, q_weight, latent_weight, latent_gain, expand_weight, out_weight, mlp_gain, gate_weight, up_weight, down_weight):
    weights = (attn_gain, q_weight, latent_weight, latent_gain, expand_weight, out_weight, mlp_gain, gate_weight, up_weight, down_weight)
    params = tuple((weight.astype(jnp.float32) for weight in weights))
    seq_count = MICRO * SEQS
    inputs_all = hidden.astype(jnp.float32).reshape(seq_count, SEQ_LEN, D)
    seg_all = segments.reshape(seq_count, SEQ_LEN).astype(jnp.int32)

    def whole(inputs_in, params_in):

        def one_seq(sample):
            return layer(sample[0], sample[1], params_in)
        return lax.map(jax.checkpoint(one_seq), (inputs_in, seg_all))
    result, pullback = jax.vjp(whole, inputs_all, params)
    grad_inputs, grad_params = pullback(cotangent.astype(jnp.float32).reshape(seq_count, SEQ_LEN, D))
    out_shape = (MICRO, SEQS, SEQ_LEN, D)
    return (result.reshape(out_shape).astype(jnp.bfloat16), grad_inputs.reshape(out_shape).astype(jnp.bfloat16), grad_params[0], grad_params[1], grad_params[2], grad_params[3], grad_params[4], grad_params[5], grad_params[6], grad_params[7], grad_params[8], grad_params[9])
```

```python
import functools

import jax
import jax.numpy as jnp
from jax import lax
from jax.experimental import pallas as pl
from jax.experimental.pallas import tpu as pltpu
from jax.sharding import PartitionSpec as P

NOPE = 128
ROPE = 64
VHEAD = 128
KVRANK = 512
DOC_MOST = 512
LANES = 128

EPSILON = 1e-06
THETA_BASE = 10000.0
NEG_FILL = -1e30

f32 = jnp.float32
bf16 = jnp.bfloat16


def norm_scale(values):
    return lax.rsqrt(jnp.mean(values * values, axis=-1, keepdims=True) + EPSILON)


def norm_back(values, factor, gain_vec, grad_out):
    scaled = grad_out * gain_vec
    grad_in = factor * scaled - values * factor**3 * jnp.mean(
        scaled * values, axis=-1, keepdims=True
    )
    return (grad_in, jnp.sum(grad_out * values * factor, axis=0))


def rotate(values, cos_table, sin_table):
    half_width = values.shape[-1] // 2
    first_half = values[..., :half_width]
    second_half = values[..., half_width:]
    return jnp.concatenate(
        [
            first_half * cos_table - second_half * sin_table,
            second_half * cos_table + first_half * sin_table,
        ],
        axis=-1,
    )


def dot(left, right, kind=f32):
    return jnp.dot(left, right, preferred_element_type=f32).astype(kind)


def dot_rt(left, right, kind=f32):
    return lax.dot_general(
        left, right, (((1,), (1,)), ((), ())), preferred_element_type=f32
    ).astype(kind)


def dot_lt(left, right, kind=f32):
    return lax.dot_general(
        left, right, (((0,), (0,)), ((), ())), preferred_element_type=f32
    ).astype(kind)


def add16(*terms):
    total = terms[0].astype(f32)
    for term in terms[1:]:
        total = total + term.astype(f32)
    return total.astype(bf16)


def after(value, *others):
    return lax.optimization_barrier((value, *others))[0]


def swap_core(value):
    return lax.ppermute(value, "ctx", [(0, 1), (1, 0)])


def swap_x(value):
    return lax.ppermute(value, "shard", [(i, i ^ 1) for i in range(4)])


def swap_y(value):
    return lax.ppermute(value, "shard", [(i, i ^ 2) for i in range(4)])


def step_z(value):
    size = lax.axis_size("tp")
    return lax.ppermute(value, "tp", [(i, (i + 1) % size) for i in range(size)])


def gather_z(value):
    pieces = [value]
    for _ in range(lax.axis_size("tp") - 1):
        pieces.append(step_z(pieces[-1]))
    return pieces


def gather_xfirst(value):
    one = swap_x(value)
    return [value, one, swap_y(value), swap_y(one)]


def gather_yfirst(value):
    two = swap_y(value)
    return [value, swap_x(value), two, swap_x(two)]


def scatter_yfirst(blocks, last=bf16):
    three, two = swap_y(blocks[3]), swap_y(blocks[2])
    other = swap_x(add16(blocks[1], three))
    total = blocks[0].astype(f32) + two.astype(f32) + other.astype(f32)
    return total.astype(last)


def scatter_xfirst(blocks, last=bf16):
    three, one = swap_x(blocks[3]), swap_x(blocks[1])
    other = swap_y(add16(blocks[2], three))
    total = blocks[0].astype(f32) + one.astype(f32) + other.astype(f32)
    return total.astype(last)


def scatter_z(block_of, last=bf16, add=add16):
    size = lax.axis_size("tp")
    total = block_of(1)
    for j in range(2, size):
        total = add(step_z(total), block_of(j))
    return (step_z(total).astype(f32) + block_of(0).astype(f32)).astype(last)


def in_order(core, mine, other, axis):
    return jnp.where(
        core == 0,
        jnp.concatenate([mine, other], axis=axis),
        jnp.concatenate([other, mine], axis=axis),
    )


def swap_halves(values, lane):
    return jnp.where(
        lane % ROPE < ROPE // 2,
        pltpu.roll(values, LANES - ROPE // 2, 1),
        pltpu.roll(values, ROPE // 2, 1),
    )


def window_mask(start, base, rows, width, seg_query, seg_key):
    query_index = base + lax.broadcasted_iota(jnp.int32, (rows, width), 0)
    key_index = start + lax.broadcasted_iota(jnp.int32, (rows, width), 1)
    same_doc = (seg_query == seg_key) & (key_index <= query_index) & (seg_key != 0)
    return same_doc | (key_index == query_index)


def head_operands(q_ref, kv_ref, rope_key, slot, window, head, heads, cos_table, sin_table):
    rows = q_ref.shape[2]
    lane = lax.broadcasted_iota(jnp.int32, (rows, LANES), 1)
    first = heads * NOPE + head // 2 * LANES
    rope_lin = q_ref[slot, 0, :, first : first + LANES]
    turned = rope_lin * cos_table + swap_halves(rope_lin, lane) * sin_table
    turned = jnp.where(lane // ROPE == head % 2, turned, 0.0)
    plain = q_ref[slot, 0, :, head * NOPE : (head + 1) * NOPE]
    query = jnp.concatenate([plain, turned], axis=1).astype(bf16)
    at = head * (NOPE + VHEAD)
    key = jnp.concatenate([kv_ref[0, window, at : at + NOPE], rope_key], axis=1)
    value = kv_ref[0, window, at + NOPE : at + NOPE + VHEAD]
    return query, key, value


def attend_kernel(
    heads, width, scale, place, q_ref, kv_ref, kr_ref, segq_ref, segk_ref, cos_ref, sin_ref, o_ref
):
    slots, rows = q_ref.shape[0], q_ref.shape[2]
    for slot in range(slots):
        start = pl.multiple_of(place[slot, 0], rows)
        window = pl.ds(start, width)
        allowed = window_mask(
            start,
            place[slot, 1],
            rows,
            width,
            segq_ref[0, slot * rows : (slot + 1) * rows, :],
            segk_ref[0, slot : slot + 1, :],
        )
        rope_key = kr_ref[0, window, :]
        for head in range(heads):
            query, key, value = head_operands(
                q_ref, kv_ref, rope_key, slot, window, head, heads, cos_ref[slot, 0], sin_ref[slot, 0]
            )
            scores = jnp.where(allowed, dot_rt(query, key) * scale, NEG_FILL)
            expd = jnp.exp(scores - jnp.max(scores, axis=-1, keepdims=True))
            probs = expd / jnp.sum(expd, axis=-1, keepdims=True)
            o_ref[slot, 0, :, head * VHEAD : (head + 1) * VHEAD] = dot(
                probs.astype(bf16), value, bf16
            )


def attend_back_kernel(
    heads,
    width,
    scale,
    place,
    q_ref,
    kv_ref,
    kr_ref,
    segq_ref,
    segk_ref,
    cos_ref,
    sin_ref,
    do_ref,
    dq_ref,
    dkv_ref,
    dkr_ref,
    total,
):
    slots, rows = q_ref.shape[0], q_ref.shape[2]
    lane = lax.broadcasted_iota(jnp.int32, (rows, LANES), 1)

    @pl.when(pl.program_id(1) == 0)
    def _():
        dkr_ref[...] = jnp.zeros_like(dkr_ref)

    total[...] = jnp.zeros_like(total)
    for slot in range(slots):
        start = pl.multiple_of(place[slot, 0], rows)
        window = pl.ds(start, width)
        allowed = window_mask(
            start,
            place[slot, 1],
            rows,
            width,
            segq_ref[0, slot * rows : (slot + 1) * rows, :],
            segk_ref[0, slot : slot + 1, :],
        )
        rope_key = kr_ref[0, window, :]
        rope_grads = None
        for head in range(heads):
            query, key, value = head_operands(
                q_ref, kv_ref, rope_key, slot, window, head, heads, cos_ref[slot, 0], sin_ref[slot, 0]
            )
            grad_mixed = do_ref[slot, 0, :, head * VHEAD : (head + 1) * VHEAD]
            scores = jnp.where(allowed, dot_rt(query, key) * scale, NEG_FILL)
            expd = jnp.exp(scores - jnp.max(scores, axis=-1, keepdims=True))
            probs = expd / jnp.sum(expd, axis=-1, keepdims=True)
            grad_probs = dot_rt(grad_mixed, value)
            inner = jnp.sum(probs * grad_probs, axis=-1, keepdims=True)
            grad_scores = (scale * probs * (grad_probs - inner)).astype(bf16)
            grad_query = dot(grad_scores, key)
            grad_key = dot_lt(grad_scores, query)
            at = head * (NOPE + VHEAD)
            total[window, at : at + NOPE] += grad_key[:, :NOPE]
            dkr_ref[0, window, :] += grad_key[:, NOPE:]
            total[window, at + NOPE : at + NOPE + VHEAD] += dot_lt(probs.astype(bf16), grad_mixed)
            dq_ref[slot, 0, :, head * NOPE : (head + 1) * NOPE] = grad_query[:, :NOPE].astype(bf16)
            if head % 2 == 0:
                rope_grads = jnp.where(lane < ROPE, grad_query[:, NOPE:], 0.0)
            else:
                rope_grads = jnp.where(lane < ROPE, rope_grads, grad_query[:, NOPE:])
            if head % 2 == 1 or head == heads - 1:
                turned = rope_grads * cos_ref[slot, 0] - swap_halves(rope_grads, lane) * sin_ref[slot, 0]
                first = heads * NOPE + head // 2 * LANES
                dq_ref[slot, 0, :, first : first + LANES] = turned.astype(bf16)
    dkv_ref[0] = total[...].astype(bf16)


def attention_specs(heads, slots, rows, length, width, q_width):
    return [
        pl.BlockSpec((slots, 1, rows, q_width), lambda m, j, place: (0, m, 0, j)),
        pl.BlockSpec((1, length, heads * (NOPE + VHEAD)), lambda m, j, place: (m, 0, j)),
        pl.BlockSpec((1, length, LANES), lambda m, j, place: (m, 0, 0)),
        pl.BlockSpec((1, slots * rows, 1), lambda m, j, place: (m, 0, 0)),
        pl.BlockSpec((1, slots, width), lambda m, j, place: (m, 0, 0)),
        pl.BlockSpec((slots, 1, rows, LANES), lambda m, j, place: (0, m, 0, 0)),
        pl.BlockSpec((slots, 1, rows, LANES), lambda m, j, place: (0, m, 0, 0)),
    ]


def attend(heads, groups, width, scale, place, q_lin, kv, rope_keys, seg_query, seg_key, cos, sin):
    slots, micro, rows, q_all = q_lin.shape
    length = kv.shape[1]
    return pl.pallas_call(
        functools.partial(attend_kernel, heads, width, scale),
        out_shape=jax.ShapeDtypeStruct((slots, micro, rows, groups * heads * VHEAD), bf16),
        grid_spec=pltpu.PrefetchScalarGridSpec(
            num_scalar_prefetch=1,
            grid=(micro, groups),
            in_specs=attention_specs(heads, slots, rows, length, width, q_all // groups),
            out_specs=pl.BlockSpec(
                (slots, 1, rows, heads * VHEAD), lambda m, j, place: (0, m, 0, j)
            ),
        ),
        compiler_params=pltpu.CompilerParams(
            dimension_semantics=("arbitrary", "arbitrary"), vmem_limit_bytes=40 << 20
        ),
        cost_estimate=pl.CostEstimate(
            flops=2 * slots * rows * micro * groups * heads * width * 384,
            transcendentals=slots * rows * micro * groups * heads * width,
            bytes_accessed=2 * kv.size + 6 * q_lin.size,
        ),
        name="attend",
    )(place, q_lin, kv, rope_keys, seg_query, seg_key, cos, sin)


def attend_back(
    heads, groups, width, scale, place, q_lin, kv, rope_keys, seg_query, seg_key, cos, sin, d_o
):
    slots, micro, rows, q_all = q_lin.shape
    length = kv.shape[1]
    q_width = q_all // groups
    kv_width = heads * (NOPE + VHEAD)
    return pl.pallas_call(
        functools.partial(attend_back_kernel, heads, width, scale),
        out_shape=(
            jax.ShapeDtypeStruct(q_lin.shape, bf16),
            jax.ShapeDtypeStruct(kv.shape, bf16),
            jax.ShapeDtypeStruct((micro, length, LANES), f32),
        ),
        grid_spec=pltpu.PrefetchScalarGridSpec(
            num_scalar_prefetch=1,
            grid=(micro, groups),
            in_specs=attention_specs(heads, slots, rows, length, width, q_width)
            + [pl.BlockSpec((slots, 1, rows, heads * VHEAD), lambda m, j, place: (0, m, 0, j))],
            out_specs=[
                pl.BlockSpec((slots, 1, rows, q_width), lambda m, j, place: (0, m, 0, j)),
                pl.BlockSpec((1, length, kv_width), lambda m, j, place: (m, 0, j)),
                pl.BlockSpec((1, length, LANES), lambda m, j, place: (m, 0, 0)),
            ],
            scratch_shapes=[pltpu.VMEM((length, kv_width), f32)],
        ),
        compiler_params=pltpu.CompilerParams(
            dimension_semantics=("arbitrary", "arbitrary"), vmem_limit_bytes=40 << 20
        ),
        cost_estimate=pl.CostEstimate(
            flops=2 * slots * rows * micro * groups * heads * width * 1024,
            transcendentals=slots * rows * micro * groups * heads * width,
            bytes_accessed=4 * kv.size + 8 * q_lin.size,
        ),
        name="attend_back",
    )(place, q_lin, kv, rope_keys, seg_query, seg_key, cos, sin, d_o)


def shards(
    hidden,
    segments,
    cotangent,
    attn_gain,
    q_weight,
    latent_weight,
    latent_gain,
    expand_weight,
    out_weight,
    mlp_gain,
    gate_weight,
    up_weight,
    down_weight,
):
    micro, _, rows, width = hidden.shape
    length = segments.shape[2]
    tp_size, cores = lax.axis_size("tp"), lax.axis_size("ctx")
    shard, core, place_z = lax.axis_index("shard"), lax.axis_index("ctx"), lax.axis_index("tp")
    span = rows * tp_size
    own = micro * rows
    block = width // 4
    slice_rows = q_weight.shape[0]
    heads_here = q_weight.shape[1] // (NOPE + ROPE)
    split = heads_here % cores == 0
    heads = heads_here // cores if split else heads_here
    slots = cores if split else 1
    rope_width = -(-heads * ROPE // LANES) * LANES
    q_width = heads * NOPE + rope_width
    scale = (NOPE + ROPE) ** (-0.5)
    hidden_here = gate_weight.shape[1]
    part = -(-hidden_here // (cores * LANES)) * LANES
    window = min(length, -(-(DOC_MOST + rows) // LANES) * LANES)

    def features(values):
        size = values.shape[-1] // 4
        return jnp.concatenate(
            [
                lax.dynamic_slice_in_dim(values, (shard ^ k) * size, size, values.ndim - 1)
                for k in range(4)
            ],
            axis=-1,
        )

    def mine(values, axis):
        return lax.dynamic_index_in_dim(values, core, axis, keepdims=False)

    def others(values, axis):
        return lax.dynamic_index_in_dim(values, 1 - core, axis, keepdims=False)

    def halves(values, axis, pick, joined):
        del axis
        return in_order(core, mine(values, pick), swap_core(others(values, pick)), joined)

    small_rows = latent_weight.shape[0]
    gain_rows, latent_gains = attn_gain.shape[0], latent_gain.shape[0]
    kv_cols = latent_weight.shape[1]
    gains_row = jnp.concatenate([attn_gain, mlp_gain, latent_gain])
    gains_row = jnp.pad(gains_row, (0, kv_cols - gains_row.shape[0]))
    small = jnp.concatenate([latent_weight, jnp.pad(gains_row[None], ((0, 15), (0, 0)))])
    line = jnp.zeros((tp_size, small_rows + 16, kv_cols), bf16)
    for j, piece in enumerate(gather_z(small)):
        line = lax.dynamic_update_index_in_dim(line, piece, (place_z - j) % tp_size, 0)
    plane = jnp.stack(gather_xfirst(line))
    small_all = in_order(core, plane[:, None], swap_core(plane)[:, None], 1)
    w_latent = small_all[:, :, :, :small_rows].reshape(width, kv_cols)
    gain_all = small_all[:, :, :, small_rows].astype(f32)
    gain_one = gain_all[..., :gain_rows].reshape(width)
    gain_two = gain_all[..., gain_rows : 2 * gain_rows].reshape(width)
    gain_kv = features(
        gain_all[..., 2 * gain_rows : 2 * gain_rows + latent_gains].reshape(KVRANK)
    )

    down_pad = jnp.pad(down_weight, ((0, cores * part - hidden_here), (0, 0)))
    down_piece = halves(down_pad.reshape(cores, part, slice_rows), 0, 0, 1)
    half_part = part // 2 // 16 * 16
    down_top = gather_xfirst(down_piece[:half_part])
    down_low = gather_yfirst(down_piece[half_part:])
    w_down = jnp.concatenate(
        [jnp.concatenate(down_top, axis=1), jnp.concatenate(down_low, axis=1)], axis=0
    )

    def q_order(values):
        groups = values.shape[1] // (heads * (NOPE + ROPE))
        by_head = values.reshape(values.shape[0], groups, heads, NOPE + ROPE)
        plain = by_head[..., :NOPE].reshape(values.shape[0], groups, heads * NOPE)
        rope = by_head[..., NOPE:].reshape(values.shape[0], groups, heads * ROPE)
        rope = jnp.pad(rope, ((0, 0), (0, 0), (0, rope_width - heads * ROPE)))
        return jnp.concatenate([plain, rope], axis=-1)

    def q_disorder(values):
        lead = values.shape[:2]
        plain = values[..., : heads * NOPE].reshape(*lead, heads, NOPE)
        rope = values[..., heads * NOPE : heads * (NOPE + ROPE)].reshape(*lead, heads, ROPE)
        return jnp.concatenate([plain, rope], axis=-1).reshape(lead[0], -1)

    q_local = q_order(q_weight)
    expand_rows = expand_weight.shape[0]
    kv_width = heads * (NOPE + VHEAD)
    expand_local = expand_weight.reshape(expand_rows, -1, kv_width)
    out_local = out_weight.reshape(-1, heads * VHEAD, slice_rows)
    if split:
        q_piece = halves(q_local, 0, 1, 0)
        expand_piece = halves(expand_local, 0, 1, 0)
        out_piece = halves(out_local, 1, 0, 1)
    else:
        q_piece = in_order(core, q_local[:, 0], swap_core(q_local[:, 0]), 0)
        expand_piece = in_order(core, expand_local[:, 0], swap_core(expand_local[:, 0]), 0)
        out_piece = in_order(core, out_local[0], swap_core(out_local[0]), 1)
    q_line = jnp.concatenate(gather_z(q_piece), axis=1)
    expand_line = jnp.concatenate(gather_z(expand_piece), axis=1)
    out_line = jnp.concatenate(gather_z(out_piece), axis=0)
    q_blocks = gather_xfirst(q_line)
    expand_blocks = gather_yfirst(expand_line)
    out_blocks = gather_yfirst(out_line)
    w_query = jnp.concatenate(q_blocks, axis=0)
    w_expand = jnp.concatenate(expand_blocks, axis=0)
    w_expand = jnp.concatenate(
        [
            lax.dynamic_slice_in_dim(w_expand, (shard ^ k) * (KVRANK // 4), KVRANK // 4, 0)
            for k in range(4)
        ],
        axis=0,
    )
    w_out = jnp.concatenate(out_blocks, axis=1)

    def hidden_piece(weight):
        padded = jnp.pad(weight, ((0, 0), (0, cores * part - hidden_here)))
        return halves(padded.reshape(slice_rows, cores, part), 0, 1, 0)

    gate_piece, up_piece = lax.optimization_barrier(
        (hidden_piece(gate_weight), hidden_piece(up_weight), q_blocks[3], out_blocks[3])
    )[:2]
    w_gate = jnp.concatenate(gather_xfirst(gate_piece), axis=0)
    w_up = jnp.concatenate(gather_yfirst(up_piece), axis=0)

    seg_all = segments[:, 0]
    bases = [core * span + place_z * rows, (1 - core) * span + place_z * rows][:slots]
    starts = [jnp.maximum(base + rows - window, 0) for base in bases]
    place = jnp.stack([jnp.stack([a, b]) for a, b in zip(starts, bases)]).astype(jnp.int32)
    seg_query = jnp.concatenate(
        [lax.dynamic_slice_in_dim(seg_all, base, rows, 1) for base in bases], axis=1
    )
    seg_key = jnp.stack(
        [lax.dynamic_slice_in_dim(seg_all, start, window, 1) for start in starts], axis=1
    )
    query_index = jnp.concatenate([base + jnp.arange(rows, dtype=jnp.int32) for base in bases])
    first_index = jnp.sum(
        (seg_all[:, None, :] < seg_query[:, :, None]).astype(jnp.int32), axis=-1
    )
    positions = (query_index[None] - first_index).reshape(micro, slots, rows)
    positions = positions.transpose(1, 0, 2)
    freqs = THETA_BASE ** (-2.0 * jnp.arange(ROPE // 2, dtype=f32) / ROPE)
    angles = positions.astype(f32)[..., None] * freqs
    cos_rows, sin_rows = jnp.cos(angles), jnp.sin(angles)
    cos_own = cos_rows[0].reshape(own, ROPE // 2)
    sin_own = sin_rows[0].reshape(own, ROPE // 2)
    cos_lanes = jnp.concatenate([cos_rows] * 4, axis=-1)
    sin_lanes = jnp.concatenate([-sin_rows, sin_rows] * 2, axis=-1)
    attention = (heads, tp_size, window, scale, place)
    tables = (seg_query[..., None], seg_key, cos_lanes, sin_lanes)

    inputs = features(hidden.reshape(own, width)).astype(f32)
    factor_one = norm_scale(inputs)
    normed_own = (inputs * factor_one * gain_one).astype(bf16)
    normed_chip = normed_own
    if split:
        normed_chip = jnp.concatenate([normed_own, swap_core(normed_own)])
    latent_raw = dot(normed_own, w_latent)
    latent_part = latent_raw[:, :KVRANK]
    factor_latent = norm_scale(latent_part)
    latent_own = (latent_part * factor_latent * gain_kv).astype(bf16)
    rope_own = rotate(latent_raw[:, KVRANK:], cos_own, sin_own).astype(bf16)
    latent_pack = jnp.concatenate([latent_own, rope_own], axis=1).reshape(micro, rows, kv_cols)
    latent_half = jnp.zeros((micro, span, kv_cols), bf16)
    for j, piece in enumerate(gather_z(latent_pack)):
        latent_half = lax.dynamic_update_slice_in_dim(
            latent_half, piece, (place_z - j) % tp_size * rows, 1
        )
    latent_full = in_order(core, latent_half, swap_core(latent_half), 1)
    latent_all = latent_full[..., :KVRANK].reshape(micro * length, KVRANK)
    rope_keys = jnp.concatenate([latent_full[..., KVRANK:]] * 2, axis=-1)

    q_lin = dot(normed_chip, w_query).reshape(slots, micro, rows, tp_size * q_width)
    kv_all = dot(latent_all, w_expand, bf16).reshape(micro, length, tp_size * kv_width)
    mixed = attend(*attention, q_lin, kv_all, rope_keys, *tables)
    mixed = mixed.reshape(slots * own, tp_size * heads * VHEAD)
    if split:
        mixed_out = dot(mixed, w_out, bf16)
        middle = inputs + mixed_out[:own].astype(f32) + swap_core(mixed_out[own:]).astype(f32)
    else:
        middle = inputs + dot(mixed, w_out)
    factor_two = norm_scale(middle)
    normed_two = (middle * factor_two * gain_two).astype(bf16)

    def to_group(values):
        pieces = []
        for piece in gather_z(values):
            pieces += [piece, swap_core(piece)]
        return jnp.concatenate(pieces)

    grad_own = features(cotangent.reshape(own, width))
    grad_all = to_group(after(grad_own, q_line, expand_line, out_line))
    normed_all = to_group(normed_two)
    grad_act = dot_rt(grad_all, w_down)
    gate_val = dot(normed_all, w_gate)
    up_val = dot(normed_all, w_up)
    sigma = jax.nn.sigmoid(gate_val)
    swish = gate_val * sigma
    hidden_act = (swish * up_val).astype(bf16)
    grad_gate = (grad_act * up_val * sigma * (1.0 + gate_val * (1.0 - sigma))).astype(bf16)
    grad_up = (grad_act * swish).astype(bf16)

    def rows_of(values, j):
        return values[2 * own * j : 2 * own * (j + 1)]

    def from_group(product):
        def block_of(j):
            both = lax.optimization_barrier(product(j))
            return add16(both[:own], swap_core(both[own:]))

        return scatter_z(block_of, f32)

    grad_normed_two = from_group(
        lambda j: (
            dot_rt(rows_of(grad_gate, j), w_gate) + dot_rt(rows_of(grad_up, j), w_up)
        ).astype(bf16)
    )
    down_out = from_group(lambda j: dot(rows_of(hidden_act, j), w_down, bf16))
    output = (middle + down_out).astype(bf16)

    def columns(values, k):
        return values[:, block * k : block * (k + 1)]

    gate_back = scatter_yfirst(
        [dot_lt(columns(normed_all, k), grad_gate, bf16) for k in range(4)]
    )
    up_back = scatter_xfirst([dot_lt(columns(normed_all, k), grad_up, bf16) for k in range(4)])
    down_blocks = [dot_lt(hidden_act, columns(grad_all, k), bf16) for k in range(4)]
    down_back = jnp.concatenate(
        [
            scatter_yfirst([piece[:half_part] for piece in down_blocks]),
            scatter_xfirst([piece[half_part:] for piece in down_blocks]),
        ]
    )

    def hidden_grad(value):
        by_core = value.reshape(cores, slice_rows, part)
        both = in_order(core, mine(by_core, 0), swap_core(others(by_core, 0)), 1)
        return both[:, :hidden_here].astype(f32)

    grad_wgate, grad_wup = hidden_grad(gate_back), hidden_grad(up_back)
    by_core = down_back.reshape(part, cores, slice_rows)
    grad_wdown = in_order(core, mine(by_core, 1), swap_core(others(by_core, 1)), 0)
    grad_wdown = grad_wdown[:hidden_here].astype(f32)

    grad_mid_norm, grad_gain_two = norm_back(middle, factor_two, gain_two, grad_normed_two)
    grad_middle = grad_own.astype(f32) + grad_mid_norm
    grad_attn = grad_middle.astype(bf16)
    if split:
        grad_attn = jnp.concatenate([grad_attn, swap_core(grad_attn)])
    grad_mixed = dot_rt(grad_attn, w_out, bf16)
    grad_qlin, grad_kv, grad_ropes = attend_back(
        *attention,
        q_lin,
        kv_all,
        rope_keys,
        *tables,
        grad_mixed.reshape(slots, micro, rows, tp_size * heads * VHEAD),
    )
    grad_qlin = grad_qlin.reshape(slots * own, tp_size * q_width)
    grad_kv = grad_kv.reshape(micro * length, tp_size * kv_width)

    grad_latent = jnp.concatenate(
        [
            dot_rt(grad_kv, w_expand, bf16).reshape(micro, length, KVRANK),
            (grad_ropes[..., :ROPE] + grad_ropes[..., ROPE:]).astype(bf16),
        ],
        axis=-1,
    ).reshape(micro, cores, span, kv_cols)
    latent_sum = add16(mine(grad_latent, 1), swap_core(others(grad_latent, 1)))
    grad_latent_own = scatter_z(
        lambda j: lax.dynamic_slice_in_dim(latent_sum, (place_z - j) % tp_size * rows, rows, 1), f32
    ).reshape(own, kv_cols)
    grad_latent_part, grad_gain_latent = norm_back(
        latent_part, factor_latent, gain_kv, grad_latent_own[:, :KVRANK]
    )
    grad_raw = jnp.concatenate(
        [grad_latent_part, rotate(grad_latent_own[:, KVRANK:], cos_own, -sin_own)], axis=-1
    ).astype(bf16)
    grad_normed_one = dot_rt(grad_raw, w_latent)
    if split:
        query_back = dot_rt(grad_qlin, w_query, bf16)
        grad_normed_one = (
            grad_normed_one
            + query_back[:own].astype(f32)
            + swap_core(query_back[own:]).astype(f32)
        )
    else:
        grad_normed_one = grad_normed_one + dot_rt(grad_qlin, w_query)
    grad_in_norm, grad_gain_one = norm_back(inputs, factor_one, gain_one, grad_normed_one)
    input_grad = (grad_middle + grad_in_norm).astype(bf16)

    out_back = scatter_xfirst([dot_lt(mixed, columns(grad_attn, k), bf16) for k in range(4)])
    query_back = scatter_yfirst(
        [dot_lt(columns(normed_chip, k), grad_qlin, bf16) for k in range(4)]
    )
    latent_block = KVRANK // 4
    expand_back = scatter_xfirst(
        [
            dot_lt(
                lax.dynamic_slice_in_dim(latent_all, (shard ^ k) * latent_block, latent_block, 1),
                grad_kv,
                bf16,
            )
            for k in range(4)
        ]
    )
    out_here = scatter_z(
        lambda j: out_back[heads * VHEAD * j : heads * VHEAD * (j + 1)]
    )
    query_here = scatter_z(lambda j: query_back[:, q_width * j : q_width * (j + 1)])
    expand_here = scatter_z(lambda j: expand_back[:, kv_width * j : kv_width * (j + 1)])
    out_cores = out_here.reshape(heads * VHEAD, cores, slice_rows)
    query_cores = query_here.reshape(cores, slice_rows, q_width)
    expand_cores = expand_here.reshape(cores, expand_rows, kv_width)
    if split:
        grad_wout = in_order(core, mine(out_cores, 1), swap_core(others(out_cores, 1)), 0)
        grad_wquery = in_order(
            core, mine(query_cores, 0)[:, None], swap_core(others(query_cores, 0))[:, None], 1
        )
        grad_wexpand = in_order(core, mine(expand_cores, 0), swap_core(others(expand_cores, 0)), 1)
    else:
        grad_wout = mine(out_cores, 1).astype(f32) + swap_core(others(out_cores, 1)).astype(f32)
        grad_wquery = mine(query_cores, 0).astype(f32) + swap_core(others(query_cores, 0)).astype(
            f32
        )
        grad_wquery = grad_wquery[:, None]
        grad_wexpand = mine(expand_cores, 0).astype(f32) + swap_core(
            others(expand_cores, 0)
        ).astype(f32)
    grad_wquery = q_disorder(grad_wquery).astype(f32)
    grad_wout, grad_wexpand = grad_wout.astype(f32), grad_wexpand.astype(f32)

    def scatter_small(values, add):
        kept = add(mine(values, 1), swap_core(others(values, 1)))
        three, two = swap_y(kept[3]), swap_y(kept[2])
        kept = add(add(kept[0], two), swap_x(add(kept[1], three)))
        return scatter_z(
            lambda j: lax.dynamic_index_in_dim(
                kept, (place_z - j) % tp_size, 0, keepdims=False
            ),
            f32,
            add,
        )

    grad_wlatent = dot_lt(normed_own, grad_raw, bf16)
    grad_wlatent = scatter_small(
        grad_wlatent.reshape(4, cores, tp_size, small_rows, kv_cols), add16
    )
    gain_grads = scatter_small(
        jnp.concatenate(
            [
                grad_gain_one.reshape(4, cores, tp_size, gain_rows),
                grad_gain_two.reshape(4, cores, tp_size, gain_rows),
                features(grad_gain_latent).reshape(4, cores, tp_size, latent_gains),
            ],
            axis=-1,
        ),
        jnp.add,
    )
    like = (micro, 1, rows, width)
    return (
        features(output).reshape(like),
        features(input_grad).reshape(like),
        gain_grads[:gain_rows],
        grad_wquery,
        grad_wlatent,
        gain_grads[2 * gain_rows :],
        grad_wexpand,
        grad_wout,
        gain_grads[gain_rows : 2 * gain_rows],
        grad_wgate,
        grad_wup,
        grad_wdown,
    )


def solution(mesh):
    tokens = P(None, "shard", ("ctx", "tp"), None)
    everywhere = P(("shard", "ctx", "tp"))
    down_split = P(("shard", "ctx"), "tp")
    up_split = P("tp", ("shard", "ctx"))
    whole_rows = P(("shard", "ctx", "tp"), None)
    return jax.shard_map(
        shards,
        mesh=mesh,
        in_specs=(
            tokens,
            P(None, "shard", None),
            tokens,
            everywhere,
            down_split,
            whole_rows,
            everywhere,
            down_split,
            up_split,
            everywhere,
            down_split,
            down_split,
            up_split,
        ),
        out_specs=(
            tokens,
            tokens,
            everywhere,
            down_split,
            whole_rows,
            everywhere,
            down_split,
            up_split,
            everywhere,
            down_split,
            down_split,
            up_split,
        ),
        check_vma=False,
    )
```

```python
import functools

import jax
import jax.numpy as jnp
from jax import lax
from jax.experimental import pallas as pl
from jax.experimental.pallas import tpu as pltpu
from jax.sharding import PartitionSpec as P

NOPE = 128
ROPE = 64
VHEAD = 128
KVRANK = 512
DOC_MOST = 512
LANES = 128

EPSILON = 1e-06
THETA_BASE = 10000.0
NEG_FILL = -1e30

f32 = jnp.float32
bf16 = jnp.bfloat16


def norm_scale(values):
    return lax.rsqrt(jnp.mean(values * values, axis=-1, keepdims=True) + EPSILON)


def norm_back(values, factor, gain_vec, grad_out):
    scaled = grad_out * gain_vec
    grad_in = factor * scaled - values * factor**3 * jnp.mean(
        scaled * values, axis=-1, keepdims=True
    )
    return (grad_in, jnp.sum(grad_out * values * factor, axis=0))


def rotate(values, cos_table, sin_table):
    half_width = values.shape[-1] // 2
    first_half = values[..., :half_width]
    second_half = values[..., half_width:]
    return jnp.concatenate(
        [
            first_half * cos_table - second_half * sin_table,
            second_half * cos_table + first_half * sin_table,
        ],
        axis=-1,
    )


def dot(left, right, kind=f32):
    return jnp.dot(left, right, preferred_element_type=f32).astype(kind)


def dot_rt(left, right, kind=f32):
    return lax.dot_general(
        left, right, (((1,), (1,)), ((), ())), preferred_element_type=f32
    ).astype(kind)


def dot_lt(left, right, kind=f32):
    return lax.dot_general(
        left, right, (((0,), (0,)), ((), ())), preferred_element_type=f32
    ).astype(kind)


def add16(*terms):
    total = terms[0].astype(f32)
    for term in terms[1:]:
        total = total + term.astype(f32)
    return total.astype(bf16)


def after(value, *others):
    return lax.optimization_barrier((value, *others))[0]


class Line:
    def __init__(self):
        self.last = None

    def send(self, move, value, *needs, free=False):
        if self.last is not None and not free:
            needs = (*needs, self.last)
        if needs:
            value = after(value, *needs)
        self.last = move(value)
        return self.last


def swap_core(value):
    return lax.ppermute(value, "ctx", [(0, 1), (1, 0)])


def swap_x(value):
    return lax.ppermute(value, "shard", [(i, i ^ 1) for i in range(4)])


def swap_y(value):
    return lax.ppermute(value, "shard", [(i, i ^ 2) for i in range(4)])


def step_z(value):
    size = lax.axis_size("tp")
    return lax.ppermute(value, "tp", [(i, (i + 1) % size) for i in range(size)])


def gather_xy(line_x, line_y, x_first, y_first):
    ax = line_x.send(swap_x, x_first)
    by = line_y.send(swap_y, y_first)
    ay = line_y.send(swap_y, x_first)
    bx = line_x.send(swap_x, y_first)
    axy = line_y.send(swap_y, ax)
    byx = line_x.send(swap_x, by)
    return [x_first, ax, ay, axy], [y_first, bx, by, byx]


def scatter_yfirst(line_x, line_y, blocks, last=bf16):
    three, two = line_y.send(swap_y, blocks[3]), line_y.send(swap_y, blocks[2])
    other = line_x.send(swap_x, add16(blocks[1], three))
    total = blocks[0].astype(f32) + two.astype(f32) + other.astype(f32)
    return total.astype(last)


def scatter_xfirst(line_x, line_y, blocks, last=bf16):
    three, one = line_x.send(swap_x, blocks[3]), line_x.send(swap_x, blocks[1])
    other = line_y.send(swap_y, add16(blocks[2], three))
    total = blocks[0].astype(f32) + one.astype(f32) + other.astype(f32)
    return total.astype(last)


def scatter_z(line_z, block_of, last=bf16, add=add16):
    size = lax.axis_size("tp")
    total = block_of(1)
    for j in range(2, size):
        total = add(line_z.send(step_z, total), block_of(j))
    return (line_z.send(step_z, total).astype(f32) + block_of(0).astype(f32)).astype(last)


def in_order(core, mine, other, axis):
    return jnp.where(
        core == 0,
        jnp.concatenate([mine, other], axis=axis),
        jnp.concatenate([other, mine], axis=axis),
    )


def assemble(sources, moves, shapes, place):
    depth = min(32, len(moves))

    def kernel(place_ref, *refs):
        given, made, sems = refs[: len(sources)], refs[len(sources) : -1], refs[-1]
        flight = []
        for i, (src, row, rows, column, columns, dst, to_row, to_column) in enumerate(moves):
            if i >= depth:
                flight[i - depth].wait()
            if not isinstance(to_row, int):
                to_row = pl.multiple_of(to_row[1](place_ref), to_row[0])
            copy = pltpu.make_async_copy(
                given[src].at[pl.ds(row, rows), pl.ds(column, columns)],
                made[dst].at[pl.ds(to_row, rows), pl.ds(to_column, columns)],
                sems.at[i % depth],
            )
            copy.start()
            flight.append(copy)
        for copy in flight[-depth:]:
            copy.wait()

    return pl.pallas_call(
        kernel,
        out_shape=[jax.ShapeDtypeStruct(shape, bf16) for shape in shapes],
        grid_spec=pltpu.PrefetchScalarGridSpec(
            num_scalar_prefetch=1,
            in_specs=[pl.BlockSpec(memory_space=pl.ANY)] * len(sources),
            out_specs=[pl.BlockSpec(memory_space=pltpu.VMEM)] * len(shapes),
            scratch_shapes=[pltpu.SemaphoreType.DMA((depth,))],
        ),
        compiler_params=pltpu.CompilerParams(vmem_limit_bytes=48 << 20),
        cost_estimate=pl.CostEstimate(
            flops=0,
            transcendentals=0,
            bytes_accessed=4 * sum(a * b for a, b in shapes),
        ),
        name="assemble",
    )(place, *sources)


def lay_out_kernel(places, *refs):
    pieces, (latent, rope) = refs[:-2], refs[-2:]
    rows = pieces[0].shape[1]
    for i, piece in enumerate(pieces):
        at = pl.ds(pl.multiple_of(places[i], rows), rows)
        latent[:, at, :] = piece[:, :, :KVRANK]
        keys = piece[:, :, KVRANK:]
        rope[:, at, :] = jnp.concatenate([keys, keys], axis=-1)


def lay_out(places, pieces, length):
    micro = pieces[0].shape[0]
    in_vmem = pl.BlockSpec(memory_space=pltpu.VMEM)
    return pl.pallas_call(
        lay_out_kernel,
        out_shape=[
            jax.ShapeDtypeStruct((micro, length, KVRANK), bf16),
            jax.ShapeDtypeStruct((micro, length, 2 * ROPE), bf16),
        ],
        grid_spec=pltpu.PrefetchScalarGridSpec(
            num_scalar_prefetch=1,
            in_specs=[in_vmem] * len(pieces),
            out_specs=[in_vmem] * 2,
        ),
        cost_estimate=pl.CostEstimate(
            flops=0, transcendentals=0, bytes_accessed=4 * micro * length * (KVRANK + 2 * ROPE)
        ),
        name="lay_out",
    )(places, *pieces)


def swap_halves(values, lane):
    return jnp.where(
        lane % ROPE < ROPE // 2,
        pltpu.roll(values, LANES - ROPE // 2, 1),
        pltpu.roll(values, ROPE // 2, 1),
    )


def window_mask(start, base, rows, width, seg_query, seg_key):
    query_index = base + lax.broadcasted_iota(jnp.int32, (rows, width), 0)
    key_index = start + lax.broadcasted_iota(jnp.int32, (rows, width), 1)
    same_doc = (seg_query == seg_key) & (key_index <= query_index) & (seg_key != 0)
    return same_doc | (key_index == query_index)


def head_operands(q_ref, kv_ref, rope_key, slot, window, head, heads, cos_table, sin_table):
    rows = q_ref.shape[2]
    lane = lax.broadcasted_iota(jnp.int32, (rows, LANES), 1)
    first = heads * NOPE + head // 2 * LANES
    rope_lin = q_ref[slot, 0, :, first : first + LANES]
    turned = rope_lin * cos_table + swap_halves(rope_lin, lane) * sin_table
    turned = jnp.where(lane // ROPE == head % 2, turned, 0.0)
    plain = q_ref[slot, 0, :, head * NOPE : (head + 1) * NOPE]
    query = jnp.concatenate([plain, turned], axis=1).astype(bf16)
    at = head * (NOPE + VHEAD)
    key = jnp.concatenate([kv_ref[0, window, at : at + NOPE], rope_key], axis=1)
    value = kv_ref[0, window, at + NOPE : at + NOPE + VHEAD]
    return query, key, value


def attend_kernel(
    heads, width, scale, place, q_ref, kv_ref, kr_ref, segq_ref, segk_ref, cos_ref, sin_ref, o_ref
):
    slots, rows = q_ref.shape[0], q_ref.shape[2]
    for slot in range(slots):
        start = pl.multiple_of(place[slot, 0], rows)
        window = pl.ds(start, width)
        allowed = window_mask(
            start,
            place[slot, 1],
            rows,
            width,
            segq_ref[0, slot * rows : (slot + 1) * rows, :],
            segk_ref[0, slot : slot + 1, :],
        )
        rope_key = kr_ref[0, window, :]
        for head in range(heads):
            query, key, value = head_operands(
                q_ref, kv_ref, rope_key, slot, window, head, heads, cos_ref[slot, 0], sin_ref[slot, 0]
            )
            scores = jnp.where(allowed, dot_rt(query, key) * scale, NEG_FILL)
            expd = jnp.exp(scores - jnp.max(scores, axis=-1, keepdims=True))
            probs = expd / jnp.sum(expd, axis=-1, keepdims=True)
            o_ref[slot, 0, :, head * VHEAD : (head + 1) * VHEAD] = dot(
                probs.astype(bf16), value, bf16
            )


def attend_back_kernel(
    heads,
    width,
    scale,
    place,
    q_ref,
    kv_ref,
    kr_ref,
    segq_ref,
    segk_ref,
    cos_ref,
    sin_ref,
    do_ref,
    dq_ref,
    dkv_ref,
    dkr_ref,
    total,
):
    slots, rows = q_ref.shape[0], q_ref.shape[2]
    lane = lax.broadcasted_iota(jnp.int32, (rows, LANES), 1)

    @pl.when(pl.program_id(1) == 0)
    def _():
        dkr_ref[...] = jnp.zeros_like(dkr_ref)

    total[...] = jnp.zeros_like(total)
    for slot in range(slots):
        start = pl.multiple_of(place[slot, 0], rows)
        window = pl.ds(start, width)
        allowed = window_mask(
            start,
            place[slot, 1],
            rows,
            width,
            segq_ref[0, slot * rows : (slot + 1) * rows, :],
            segk_ref[0, slot : slot + 1, :],
        )
        rope_key = kr_ref[0, window, :]
        rope_grads = None
        for head in range(heads):
            query, key, value = head_operands(
                q_ref, kv_ref, rope_key, slot, window, head, heads, cos_ref[slot, 0], sin_ref[slot, 0]
            )
            grad_mixed = do_ref[slot, 0, :, head * VHEAD : (head + 1) * VHEAD]
            scores = jnp.where(allowed, dot_rt(query, key) * scale, NEG_FILL)
            expd = jnp.exp(scores - jnp.max(scores, axis=-1, keepdims=True))
            probs = expd / jnp.sum(expd, axis=-1, keepdims=True)
            grad_probs = dot_rt(grad_mixed, value)
            inner = jnp.sum(probs * grad_probs, axis=-1, keepdims=True)
            grad_scores = (scale * probs * (grad_probs - inner)).astype(bf16)
            grad_query = dot(grad_scores, key)
            grad_key = dot_lt(grad_scores, query)
            at = head * (NOPE + VHEAD)
            total[window, at : at + NOPE] += grad_key[:, :NOPE]
            dkr_ref[0, window, :] += grad_key[:, NOPE:]
            total[window, at + NOPE : at + NOPE + VHEAD] += dot_lt(probs.astype(bf16), grad_mixed)
            dq_ref[slot, 0, :, head * NOPE : (head + 1) * NOPE] = grad_query[:, :NOPE].astype(bf16)
            if head % 2 == 0:
                rope_grads = jnp.where(lane < ROPE, grad_query[:, NOPE:], 0.0)
            else:
                rope_grads = jnp.where(lane < ROPE, rope_grads, grad_query[:, NOPE:])
            if head % 2 == 1 or head == heads - 1:
                turned = rope_grads * cos_ref[slot, 0] - swap_halves(rope_grads, lane) * sin_ref[slot, 0]
                first = heads * NOPE + head // 2 * LANES
                dq_ref[slot, 0, :, first : first + LANES] = turned.astype(bf16)
    dkv_ref[0] = total[...].astype(bf16)


def attention_specs(heads, slots, rows, length, width, q_width):
    return [
        pl.BlockSpec((slots, 1, rows, q_width), lambda m, j, place: (0, m, 0, j)),
        pl.BlockSpec((1, length, heads * (NOPE + VHEAD)), lambda m, j, place: (m, 0, j)),
        pl.BlockSpec((1, length, LANES), lambda m, j, place: (m, 0, 0)),
        pl.BlockSpec((1, slots * rows, 1), lambda m, j, place: (m, 0, 0)),
        pl.BlockSpec((1, slots, width), lambda m, j, place: (m, 0, 0)),
        pl.BlockSpec((slots, 1, rows, LANES), lambda m, j, place: (0, m, 0, 0)),
        pl.BlockSpec((slots, 1, rows, LANES), lambda m, j, place: (0, m, 0, 0)),
    ]


def attend(heads, groups, width, scale, place, q_lin, kv, rope_keys, seg_query, seg_key, cos, sin):
    slots, micro, rows, q_all = q_lin.shape
    length = kv.shape[1]
    return pl.pallas_call(
        functools.partial(attend_kernel, heads, width, scale),
        out_shape=jax.ShapeDtypeStruct((slots, micro, rows, groups * heads * VHEAD), bf16),
        grid_spec=pltpu.PrefetchScalarGridSpec(
            num_scalar_prefetch=1,
            grid=(micro, groups),
            in_specs=attention_specs(heads, slots, rows, length, width, q_all // groups),
            out_specs=pl.BlockSpec(
                (slots, 1, rows, heads * VHEAD), lambda m, j, place: (0, m, 0, j)
            ),
        ),
        compiler_params=pltpu.CompilerParams(
            dimension_semantics=("arbitrary", "arbitrary"), vmem_limit_bytes=40 << 20
        ),
        cost_estimate=pl.CostEstimate(
            flops=2 * slots * rows * micro * groups * heads * width * 384,
            transcendentals=slots * rows * micro * groups * heads * width,
            bytes_accessed=2 * kv.size + 6 * q_lin.size,
        ),
        name="attend",
    )(place, q_lin, kv, rope_keys, seg_query, seg_key, cos, sin)


def attend_back(
    heads, groups, width, scale, place, q_lin, kv, rope_keys, seg_query, seg_key, cos, sin, d_o
):
    slots, micro, rows, q_all = q_lin.shape
    length = kv.shape[1]
    q_width = q_all // groups
    kv_width = heads * (NOPE + VHEAD)
    return pl.pallas_call(
        functools.partial(attend_back_kernel, heads, width, scale),
        out_shape=(
            jax.ShapeDtypeStruct(q_lin.shape, bf16),
            jax.ShapeDtypeStruct(kv.shape, bf16),
            jax.ShapeDtypeStruct((micro, length, LANES), f32),
        ),
        grid_spec=pltpu.PrefetchScalarGridSpec(
            num_scalar_prefetch=1,
            grid=(micro, groups),
            in_specs=attention_specs(heads, slots, rows, length, width, q_width)
            + [pl.BlockSpec((slots, 1, rows, heads * VHEAD), lambda m, j, place: (0, m, 0, j))],
            out_specs=[
                pl.BlockSpec((slots, 1, rows, q_width), lambda m, j, place: (0, m, 0, j)),
                pl.BlockSpec((1, length, kv_width), lambda m, j, place: (m, 0, j)),
                pl.BlockSpec((1, length, LANES), lambda m, j, place: (m, 0, 0)),
            ],
            scratch_shapes=[pltpu.VMEM((length, kv_width), f32)],
        ),
        compiler_params=pltpu.CompilerParams(
            dimension_semantics=("arbitrary", "arbitrary"), vmem_limit_bytes=40 << 20
        ),
        cost_estimate=pl.CostEstimate(
            flops=2 * slots * rows * micro * groups * heads * width * 1024,
            transcendentals=slots * rows * micro * groups * heads * width,
            bytes_accessed=4 * kv.size + 8 * q_lin.size,
        ),
        name="attend_back",
    )(place, q_lin, kv, rope_keys, seg_query, seg_key, cos, sin, d_o)


def spans(total, step):
    return [(at, min(step, total - at)) for at in range(0, total, step)]


def feed_kernel(part, rows, offset, place, *refs):
    given, refs = refs[:20], refs[20:]
    refs = refs[4:] if offset else refs
    back_own, back_other, out_own, out_other, act_all, hid_all, norm_all, grad_all = refs[:8]
    w_hid, w_down, norm, grad, d_act, act, hid, sems = refs[8:]
    norm_own, norm_other, grad_own, grad_other = given[:4]
    slice_rows = given[4].shape[0]

    def at_core(i):
        core = place[0] if i < 4 else 1 - place[0]
        return pl.ds(pl.multiple_of((2 * (i % 4) + core) * slice_rows, slice_rows), slice_rows)

    early = [
        pltpu.make_async_copy(grad_own, grad.at[pl.ds(0, rows)], sems.at[0]),
        pltpu.make_async_copy(grad_other, grad.at[pl.ds(rows, rows)], sems.at[1]),
    ] + [
        pltpu.make_async_copy(given[12 + i], w_down.at[at_core(i)], sems.at[2 + i])
        for i in range(8)
    ]
    later = [
        pltpu.make_async_copy(norm_own, norm.at[pl.ds(0, rows)], sems.at[10]),
        pltpu.make_async_copy(norm_other, norm.at[pl.ds(rows, rows)], sems.at[11]),
    ] + [
        pltpu.make_async_copy(given[4 + i], w_hid.at[at_core(i)], sems.at[12 + i])
        for i in range(8)
    ]
    for copy in early + later:
        copy.start()
    for copy in early:
        copy.wait()

    def for_chunks(total, body):
        whole = total // 256

        def step(i, carry):
            body(pl.multiple_of(i * 256, 256), 256)
            return carry

        lax.fori_loop(0, whole, step, 0)
        if total % 256:
            body(whole * 256, total % 256)

    def act_back(start, size):
        d_act[:, pl.ds(start, size)] = dot(grad[...], w_down[:, pl.ds(start, size)])

    for_chunks(part, act_back)
    for copy in later:
        copy.wait()

    def forward(start, size):
        gate = dot(norm[...], w_hid[:, pl.ds(start, size)])
        up_at = start + part
        if not isinstance(start, int):
            up_at = pl.multiple_of(up_at, LANES)
        up = dot(norm[...], w_hid[:, pl.ds(up_at, size)])
        back = d_act[:, pl.ds(start, size)]
        sigma = jax.nn.sigmoid(gate)
        swish = gate * sigma
        act[:, pl.ds(start, size)] = (swish * up).astype(bf16)
        hid[:, pl.ds(start, size)] = (
            back * up * sigma * (1.0 + gate * (1.0 - sigma))
        ).astype(bf16)
        hid[:, pl.ds(up_at, size)] = (back * swish).astype(bf16)

    for_chunks(part, forward)
    here = pl.ds(offset * 2 * rows, 2 * rows)
    saves = [
        pltpu.make_async_copy(source, target.at[here], sems.at[20 + i])
        for i, (source, target) in enumerate(
            ((act, act_all), (hid, hid_all), (norm, norm_all), (grad, grad_all))
        )
    ]
    for copy in saves:
        copy.start()

    def backward(start, size):
        back = dot_rt(hid[...], w_hid[pl.ds(start, size), :], bf16)
        back_own[:, pl.ds(start, size)] = back[:rows]
        back_other[:, pl.ds(start, size)] = back[rows:]
        out = dot_rt(act[...], w_down[pl.ds(start, size), :], bf16)
        out_own[:, pl.ds(start, size)] = out[:rows]
        out_other[:, pl.ds(start, size)] = out[rows:]

    for_chunks(w_hid.shape[0], backward)
    for copy in saves:
        copy.wait()


def feed(place, offset, blocks, tokens, hidden_pieces, down_pieces, whole):
    rows, width = tokens[0].shape
    part = down_pieces[0].shape[1]
    anywhere = pl.BlockSpec(memory_space=pl.ANY)
    in_vmem = pl.BlockSpec(memory_space=pltpu.VMEM)
    total = 2 * rows * blocks
    operands = [*tokens, *hidden_pieces, *down_pieces, *whole]
    return pl.pallas_call(
        functools.partial(feed_kernel, part, rows, offset),
        out_shape=[jax.ShapeDtypeStruct((rows, width), bf16)] * 4
        + [
            jax.ShapeDtypeStruct((total, columns), bf16)
            for columns in (part, 2 * part, width, width)
        ],
        grid_spec=pltpu.PrefetchScalarGridSpec(
            num_scalar_prefetch=1,
            in_specs=[anywhere] * len(operands),
            out_specs=[in_vmem] * 4 + [anywhere] * 4,
            scratch_shapes=[
                pltpu.VMEM((width, 2 * part), bf16),
                pltpu.VMEM((width, part), bf16),
                pltpu.VMEM((2 * rows, width), bf16),
                pltpu.VMEM((2 * rows, width), bf16),
                pltpu.VMEM((2 * rows, part), f32),
                pltpu.VMEM((2 * rows, part), bf16),
                pltpu.VMEM((2 * rows, 2 * part), bf16),
                pltpu.SemaphoreType.DMA((24,)),
            ],
        ),
        input_output_aliases={21 + i: 4 + i for i in range(len(whole))},
        compiler_params=pltpu.CompilerParams(vmem_limit_bytes=58 << 20),
        cost_estimate=pl.CostEstimate(
            flops=2 * 2 * rows * width * part * 6,
            transcendentals=2 * rows * part,
            bytes_accessed=2 * (3 * width * part + 2 * rows * (6 * width + 3 * part)),
        ),
        name="feed",
    )(place, *operands)


def pack_kernel(part, place, gate, up, down, hid_mine, hid_other, down_mine, down_other):
    slice_rows, hidden_here = gate.shape
    rest = hidden_here - part

    def put(at, low, high, value):
        low[:, at : at + part] = value[:, :part]
        if rest < part:
            edge = rest // LANES * LANES
            high[:, at + edge : at + part] = jnp.zeros((slice_rows, part - edge), bf16)
        high[:, at : at + rest] = value[:, part:]

    def write(hid_low, hid_high, down_low, down_high):
        put(0, hid_low, hid_high, gate[...])
        put(part, hid_low, hid_high, up[...])
        put(0, down_low, down_high, down[...].T)

    @pl.when(place[0] == 0)
    def _():
        write(hid_mine, hid_other, down_mine, down_other)

    @pl.when(place[0] != 0)
    def _():
        write(hid_other, hid_mine, down_other, down_mine)


def pack(place, part, gate, up, down):
    slice_rows = gate.shape[0]
    in_vmem = pl.BlockSpec(memory_space=pltpu.VMEM)
    return pl.pallas_call(
        functools.partial(pack_kernel, part),
        out_shape=[jax.ShapeDtypeStruct((slice_rows, n * part), bf16) for n in (2, 2, 1, 1)],
        grid_spec=pltpu.PrefetchScalarGridSpec(
            num_scalar_prefetch=1, in_specs=[in_vmem] * 3, out_specs=[in_vmem] * 4
        ),
        compiler_params=pltpu.CompilerParams(vmem_limit_bytes=48 << 20),
        cost_estimate=pl.CostEstimate(
            flops=0, transcendentals=0, bytes_accessed=24 * slice_rows * part
        ),
        name="pack",
    )(place, gate, up, down)


def weight_grad_kernel(blocks, place, left, right_ref, *refs):
    outs, (turned, buffer, sems) = refs[:-3], refs[-3:]
    slice_rows, tokens = outs[0].shape[0], turned.shape[1]

    def fetch(i):
        half, k = blocks[i]
        core = place[0] if half == 0 else 1 - place[0]
        start = pl.multiple_of((2 * k + core) * slice_rows, slice_rows)
        return pltpu.make_async_copy(
            left.at[:, pl.ds(start, slice_rows)], buffer.at[i % 2], sems.at[i % 2]
        )

    @pl.when(pl.program_id(0) == 0)
    def _():
        fetch(0).start()
        for i in range(len(outs)):
            fetch(i).wait()
            if i + 1 < len(outs):
                fetch(i + 1).start()

            def turn(j, carry, i=i):
                at = pl.ds(pl.multiple_of(j * 256, 256), 256)
                turned[pl.ds(i * slice_rows, slice_rows), at] = buffer[i % 2, at, :].T
                return carry

            lax.fori_loop(0, tokens // 256, turn, 0)

    for half in range(0, len(outs), 4):
        rows = pl.ds(half * slice_rows, 4 * slice_rows)
        grads = dot(turned[rows, :], right_ref[...], bf16)
        for i in range(4):
            outs[half + i][...] = grads[i * slice_rows : (i + 1) * slice_rows]


def weight_grad(place, blocks, slice_rows, left, right):
    tokens, columns = right.shape
    count = len(blocks)
    return pl.pallas_call(
        functools.partial(weight_grad_kernel, blocks),
        out_shape=[jax.ShapeDtypeStruct((slice_rows, columns), bf16)] * count,
        grid_spec=pltpu.PrefetchScalarGridSpec(
            num_scalar_prefetch=1,
            grid=(-(-columns // 256),),
            in_specs=[
                pl.BlockSpec(memory_space=pl.ANY),
                pl.BlockSpec((tokens, 256), lambda n, place: (0, n)),
            ],
            out_specs=[pl.BlockSpec((slice_rows, 256), lambda n, place: (0, n))] * count,
            scratch_shapes=[
                pltpu.VMEM((count * slice_rows, tokens), bf16),
                pltpu.VMEM((2, tokens, slice_rows), bf16),
                pltpu.SemaphoreType.DMA((2,)),
            ],
        ),
        compiler_params=pltpu.CompilerParams(
            dimension_semantics=("arbitrary",), vmem_limit_bytes=48 << 20
        ),
        cost_estimate=pl.CostEstimate(
            flops=2 * tokens * columns * count * slice_rows,
            transcendentals=0,
            bytes_accessed=2 * (tokens * columns + count * slice_rows * (tokens + columns)),
        ),
        name="weight_grad",
    )(place, left, right)


def shards(
    hidden,
    segments,
    cotangent,
    attn_gain,
    q_weight,
    latent_weight,
    latent_gain,
    expand_weight,
    out_weight,
    mlp_gain,
    gate_weight,
    up_weight,
    down_weight,
):
    micro, _, rows, width = hidden.shape
    length = segments.shape[2]
    tp_size, cores = lax.axis_size("tp"), lax.axis_size("ctx")
    shard, core, place_z = lax.axis_index("shard"), lax.axis_index("ctx"), lax.axis_index("tp")
    span = rows * tp_size
    own = micro * rows
    block = width // 4
    slice_rows = q_weight.shape[0]
    heads_here = q_weight.shape[1] // (NOPE + ROPE)
    split = heads_here % cores == 0
    heads = heads_here // cores if split else heads_here
    slots = cores if split else 1
    rope_width = -(-heads * ROPE // LANES) * LANES
    q_width = heads * NOPE + rope_width
    scale = (NOPE + ROPE) ** (-0.5)
    hidden_here = gate_weight.shape[1]
    part = -(-hidden_here // (cores * LANES)) * LANES
    window = min(length, -(-(DOC_MOST + rows) // LANES) * LANES)

    line_x, line_y, line_z, line_c = Line(), Line(), Line(), Line()

    def features(values):
        size = values.shape[-1] // 4
        return jnp.concatenate(
            [
                lax.dynamic_slice_in_dim(values, (shard ^ k) * size, size, values.ndim - 1)
                for k in range(4)
            ],
            axis=-1,
        )

    def columns(values, k):
        return values[:, block * k : block * (k + 1)]

    def mine(values, axis):
        return lax.dynamic_index_in_dim(values, core, axis, keepdims=False)

    def others(values, axis):
        return lax.dynamic_index_in_dim(values, 1 - core, axis, keepdims=False)

    def to_core(value):
        return line_c.send(swap_core, value)

    small_rows = latent_weight.shape[0]
    gain_rows, latent_gains = attn_gain.shape[0], latent_gain.shape[0]
    kv_cols = latent_weight.shape[1]
    gains_row = jnp.concatenate([attn_gain, mlp_gain, latent_gain])
    gains_row = jnp.pad(gains_row, (0, kv_cols - gains_row.shape[0]))
    small = jnp.concatenate([latent_weight, jnp.pad(gains_row[None], ((0, 15), (0, 0)))])
    small_all = lax.all_gather(small, ("shard", "ctx", "tp"), axis=0)
    devices = 4 * cores * tp_size

    def own_first(values):
        size = values.shape[0] // 4
        return jnp.concatenate(
            [lax.dynamic_slice_in_dim(values, (shard ^ k) * size, size, 0) for k in range(4)]
        )

    w_latent = own_first(small_all[:, :small_rows].reshape(width, kv_cols))
    gain_all = small_all[:, small_rows].astype(f32)
    gain_one = own_first(gain_all[:, :gain_rows].reshape(width))
    gain_two = own_first(gain_all[:, gain_rows : 2 * gain_rows].reshape(width))
    gain_kv = gain_all[:, 2 * gain_rows : 2 * gain_rows + latent_gains].reshape(KVRANK)
    del devices

    def q_order(values):
        groups = values.shape[1] // (heads * (NOPE + ROPE))
        by_head = values.reshape(values.shape[0], groups, heads, NOPE + ROPE)
        plain = by_head[..., :NOPE].reshape(values.shape[0], groups, heads * NOPE)
        rope = by_head[..., NOPE:].reshape(values.shape[0], groups, heads * ROPE)
        rope = jnp.pad(rope, ((0, 0), (0, 0), (0, rope_width - heads * ROPE)))
        return jnp.concatenate([plain, rope], axis=-1)

    def q_disorder(values):
        lead = values.shape[:2]
        plain = values[..., : heads * NOPE].reshape(*lead, heads, NOPE)
        rope = values[..., heads * NOPE : heads * (NOPE + ROPE)].reshape(*lead, heads, ROPE)
        return jnp.concatenate([plain, rope], axis=-1).reshape(lead[0], -1)

    expand_rows = expand_weight.shape[0]
    kv_width = heads * (NOPE + VHEAD)
    out_width = heads * VHEAD
    stack = slice_rows // expand_rows
    blocks_kv = kv_width // LANES
    expand_cols = -(-blocks_kv // stack)
    groups = cores if split else 1

    def expand_stack(values):
        tiles = [values[:, LANES * i : LANES * (i + 1)] for i in range(blocks_kv)]
        tiles += [jnp.zeros_like(tiles[0])] * (expand_cols * stack - blocks_kv)
        return jnp.concatenate(
            [jnp.concatenate(tiles[stack * i : stack * (i + 1)]) for i in range(expand_cols)],
            axis=1,
        )

    q_local = q_order(q_weight)
    out_local = out_weight.T
    packs = jnp.stack(
        [
            jnp.concatenate(
                [
                    q_local[:, g],
                    out_local[:, out_width * g : out_width * (g + 1)],
                    expand_stack(expand_weight[:, kv_width * g : kv_width * (g + 1)]),
                ],
                axis=1,
            )
            for g in range(groups)
        ]
    )
    pack_mine, pack_other = (mine(packs, 0), others(packs, 0)) if split else (packs[0], packs[0])
    attn_piece = jnp.concatenate([pack_mine, to_core(pack_other)])

    shift = jnp.stack([core, shard]).astype(jnp.int32)

    tokens = ()

    def now(value):
        return after(value, *tokens) if tokens else value

    def send(line, move, value, free=False):
        return line.send(move, now(value), free=free)

    def close(*arrived):
        nonlocal tokens
        tokens = arrived

    attn_z, held = [attn_piece], {}
    wanted = []
    for j in range(tp_size):
        lead, tail = (1, 2) if j % 2 == 0 else (2, 1)
        wanted.append((j, lead, 0, lead == 1, True))
        wanted.append((j, tail, 0, tail == 1, False))
        wanted.append((j, 3, lead, lead == 2, False))

    def attention_round():
        for j, piece in enumerate(attn_z):
            held.setdefault((j, 0), piece)
        keys, arrived = [], []
        for over_x in (True, False):
            ready = [w for w in wanted if w[3] == over_x and (w[0], w[2]) in held]
            ready.sort(key=lambda w: not w[4])
            if ready:
                j, k, source = ready[0][:3]
                wanted.remove(ready[0])
                line, move = (line_x, swap_x) if over_x else (line_y, swap_y)
                arrived.append(send(line, move, held[j, source]))
                keys.append((j, k))
        held.update(zip(keys, arrived))
        if len(attn_z) < tp_size:
            attn_z.append(send(line_z, step_z, attn_z[-1]))
            arrived.append(attn_z[-1])
        return arrived

    close(*attention_round())
    hid_a, hid_other, down_a, down_other = pack(
        now(shift), part, gate_weight, up_weight, down_weight
    )
    grad_own = features(now(cotangent).reshape(own, width))
    inputs16 = features(now(hidden).reshape(own, width))
    inputs = inputs16.astype(f32)
    seg_all = now(segments)[:, 0]
    bases = [core * span + place_z * rows, (1 - core) * span + place_z * rows][:slots]
    starts = [jnp.maximum(base + rows - window, 0) for base in bases]
    place = jnp.stack([jnp.stack([a, b]) for a, b in zip(starts, bases)]).astype(jnp.int32)
    seg_query = jnp.concatenate(
        [lax.dynamic_slice_in_dim(seg_all, base, rows, 1) for base in bases], axis=1
    )
    seg_key = jnp.stack(
        [lax.dynamic_slice_in_dim(seg_all, start, window, 1) for start in starts], axis=1
    )
    query_index = jnp.concatenate([base + jnp.arange(rows, dtype=jnp.int32) for base in bases])
    first_index = jnp.sum(
        (seg_all[:, None, :] < seg_query[:, :, None]).astype(jnp.int32), axis=-1
    )
    positions = (query_index[None] - first_index).reshape(micro, slots, rows)
    positions = positions.transpose(1, 0, 2)
    freqs = THETA_BASE ** (-2.0 * jnp.arange(ROPE // 2, dtype=f32) / ROPE)
    angles = positions.astype(f32)[..., None] * freqs
    cos_rows, sin_rows = jnp.cos(angles), jnp.sin(angles)
    cos_own = cos_rows[0].reshape(own, ROPE // 2)
    sin_own = sin_rows[0].reshape(own, ROPE // 2)
    cos_lanes = jnp.concatenate([cos_rows] * 4, axis=-1)
    sin_lanes = jnp.concatenate([-sin_rows, sin_rows] * 2, axis=-1)
    attention = (heads, tp_size, window, scale, place)
    tables = (seg_query[..., None], seg_key, cos_lanes, sin_lanes)

    close(*attention_round(), hid_a, grad_own, inputs16)
    for _ in range(tp_size - 3):
        close(*attention_round())
    half_own = own // 2
    grad_half = send(line_z, step_z, grad_own[:half_own])
    hid_b = send(line_c, swap_core, hid_other)
    factor_one = norm_scale(now(inputs))
    normed_own = (inputs * factor_one * gain_one).astype(bf16)
    latent_raw = dot(normed_own, w_latent)
    latent_part = latent_raw[:, :KVRANK]
    factor_latent = norm_scale(latent_part)
    latent_own = (latent_part * factor_latent * gain_kv).astype(bf16)
    rope_own = rotate(latent_raw[:, KVRANK:], cos_own, sin_own).astype(bf16)
    latent_pack = jnp.concatenate([latent_own, rope_own], axis=1).reshape(micro, rows, kv_cols)
    close(*attention_round(), latent_pack, grad_half, hid_b)
    normed_chip = normed_own
    if split:
        normed_chip = jnp.concatenate([normed_own, send(line_c, swap_core, normed_own)])
    down_b = send(line_c, swap_core, down_other)
    grad_half = jnp.concatenate([grad_half, send(line_z, step_z, grad_own[half_own:])])
    grad_z = [grad_own, grad_half]
    while len(wanted) > 2:
        close(*attention_round(), normed_chip, grad_half, down_b)
    latent_z, latent_far = [latent_pack], [send(line_c, swap_core, latent_pack)]

    def latents_ahead(count):
        for _ in range(count):
            latent_z.append(send(line_z, step_z, latent_z[-1]))
            latent_far.append(to_core(latent_z[-1]))

    latents_ahead(2)
    close(*attention_round(), latent_z[-1], latent_far[0])
    attn_xy = [[held[j, k] for k in range(4)] for j in range(tp_size)]

    hid_a1, hid_b2 = send(line_x, swap_x, hid_a), send(line_y, swap_y, hid_b)
    latents_ahead(tp_size - 3)
    q_cols, out_cols = q_width, q_width + out_width

    def core_row(k, half):
        def row(ref):
            at = ref[0] if half == 0 else 1 - ref[0]
            return (2 * k + at) * slice_rows

        return (slice_rows, row)

    def expand_row(k, half):
        def row(ref):
            at = ref[0] if half == 0 else 1 - ref[0]
            return (2 * (ref[1] ^ k) + at) * expand_rows

        return (expand_rows, row)

    moves = []
    for j in range(tp_size):
        for k in range(4):
            for half in range(2):
                source, top = 4 * j + k, half * slice_rows
                moves.append(
                    (source, top, slice_rows, 0, q_width, 0, core_row(k, half), j * q_width)
                )
                moves.append(
                    (source, top, slice_rows, q_cols, out_width, 1, core_row(k, half), j * out_width)
                )
                for i in range(blocks_kv):
                    moves.append(
                        (
                            source,
                            top + i % stack * expand_rows,
                            expand_rows,
                            out_cols + i // stack * LANES,
                            LANES,
                            2,
                            expand_row(k, half),
                            j * kv_width + i * LANES,
                        )
                    )
    w_query, w_out, w_expand = assemble(
        [piece for pieces in attn_xy for piece in pieces],
        moves,
        [(width, tp_size * q_width), (width, tp_size * out_width), (KVRANK, tp_size * kv_width)],
        now(shift),
    )
    q_lin = dot(normed_chip, w_query).reshape(slots, micro, rows, tp_size * q_width)
    close(hid_a1, hid_b2, latent_z[-1], q_lin)

    hid_b1, hid_a2 = send(line_x, swap_x, hid_b), send(line_y, swap_y, hid_a)
    more = (tp_size - 2) // 2

    def grads_ahead(count):
        for _ in range(count):
            grad_z.append(send(line_z, step_z, grad_z[-1]))

    latent_rows = [
        [(at * span + (place_z - j) % tp_size * rows) for j in range(tp_size)]
        for at in (core, 1 - core)
    ]
    latent_all, rope_keys = lay_out(
        jnp.stack([row for each in latent_rows for row in each]).astype(jnp.int32),
        [now(piece) for piece in latent_z + latent_far],
        length,
    )
    latent_all = latent_all.reshape(micro * length, KVRANK)
    grads_ahead(more)
    kv_all = dot(latent_all, w_expand, bf16).reshape(micro, length, tp_size * kv_width)
    mixed = attend(*attention, q_lin, kv_all, rope_keys, *tables)
    mixed = mixed.reshape(slots * own, tp_size * out_width)
    grad_far = [to_core(grad_z[0])]
    close(hid_b1, hid_a2, grad_z[-1], grad_far[-1], mixed)

    hid_b3, hid_a3 = send(line_x, swap_x, hid_b2), send(line_y, swap_y, hid_a1)
    grads_ahead(tp_size - 2 - more)
    mixed = now(mixed)
    if split:
        mixed_out = dot_rt(mixed, w_out, bf16)
        middle = inputs + mixed_out[:own].astype(f32) + to_core(mixed_out[own:]).astype(f32)
    else:
        middle = inputs + dot_rt(mixed, w_out)
    factor_two = norm_scale(middle)
    normed_two = (middle * factor_two * gain_two).astype(bf16)
    grad_far.append(send(line_c, swap_core, grad_z[1]))
    close(hid_b3, hid_a3, grad_z[-1], grad_far[-1], normed_two)

    down_a1, down_b2 = send(line_x, swap_x, down_a), send(line_y, swap_y, down_b)
    down_b1 = send(line_x, swap_x, down_b, free=True)
    down_a2 = send(line_y, swap_y, down_a, free=True)
    down_b3, down_a3 = send(line_x, swap_x, down_b2), send(line_y, swap_y, down_a1)
    norm_z = [normed_two, send(line_z, step_z, normed_two)]
    norm_far = [send(line_c, swap_core, normed_two)]
    for piece in grad_z[2:]:
        grad_far.append(send(line_c, swap_core, piece, free=True))
    close(down_b3, down_a3, norm_z[-1], norm_far[-1], grad_far[-1])

    hidden_pieces = [hid_a, hid_a1, hid_a2, hid_a3, hid_b, hid_b1, hid_b2, hid_b3]
    down_pieces = [down_a, down_a1, down_a2, down_a3, down_b, down_b1, down_b2, down_b3]
    whole, back_parts, out_parts = [], [], []

    class Ring:
        def __init__(self, parts):
            self.parts, self.at, self.total, self.seen = parts, 0, None, {}

        def block(self, j):
            if j not in self.seen:
                own_part, far_part = self.parts[j]
                self.seen[j] = add16(own_part, send(line_c, swap_core, far_part))
            return self.seen[j]

        def step(self):
            if self.at == tp_size - 1:
                return ()
            self.at += 1
            total = self.block(self.at)
            if self.total is not None:
                total = add16(total, self.total)
            self.total = send(line_z, step_z, total)
            return (self.total,)

        def result(self):
            while self.step():
                pass
            return self.total.astype(f32) + self.block(0).astype(f32)

    back_ring, out_ring = Ring(back_parts), Ring(out_parts)
    for j in range(tp_size):
        arrived = []
        if len(norm_z) < tp_size:
            norm_z.append(send(line_z, step_z, norm_z[-1]))
            arrived.append(norm_z[-1])
        elif back_ring.at + 1 < len(back_parts):
            arrived += back_ring.step()
        if j + 1 < tp_size:
            norm_far.append(send(line_c, swap_core, norm_z[j + 1]))
            arrived.append(norm_far[-1])
        made = feed(
            now(shift),
            j,
            tp_size,
            [norm_z[j], norm_far[j], grad_z[j], grad_far[j]],
            hidden_pieces,
            down_pieces,
            whole,
        )
        back_parts.append(made[:2])
        out_parts.append(made[2:4])
        whole = made[4:]
        close(*arrived, made[0])
    act_all, hidden_all, normed_all, grad_all = whole

    first, second = ((0, 3), (0, 2), (1, 3), (1, 1)), ((0, 1), (0, 0), (1, 2), (1, 0))
    arrived = []
    while back_ring.at < tp_size - 1:
        arrived += back_ring.step()
    hid_grads = dict(
        zip(first, weight_grad(now(shift), first, slice_rows, normed_all, hidden_all))
    )
    grad_normed_two = back_ring.result()
    close(*arrived, hid_grads[first[0]], grad_normed_two)

    half_ring = (tp_size - 1) // 2
    own3 = send(line_y, swap_y, hid_grads[0, 3])
    far3 = send(line_x, swap_x, hid_grads[1, 3])
    arrived = [own3, far3]
    for _ in range(half_ring):
        arrived += out_ring.step()
    hid_grads.update(
        zip(second, weight_grad(now(shift), second, slice_rows, normed_all, hidden_all))
    )
    close(*arrived, hid_grads[second[0]])

    own2 = send(line_y, swap_y, hid_grads[0, 2])
    far1 = send(line_x, swap_x, hid_grads[1, 1])
    arrived = [own2, far1]
    for _ in range(half_ring):
        arrived += out_ring.step()
    blocks = first + second
    down_grads = dict(
        zip(blocks, weight_grad(now(shift), blocks, slice_rows, grad_all, act_all))
    )
    own1, far2 = add16(hid_grads[0, 1], own3), add16(hid_grads[1, 2], far3)
    close(*arrived, down_grads[blocks[0]], own1, far2)

    own1, far2 = send(line_x, swap_x, own1), send(line_y, swap_y, far2)
    down3 = send(line_y, swap_y, down_grads[0, 3], free=True)
    downf3 = send(line_x, swap_x, down_grads[1, 3], free=True)
    arrived = [own1, far2, down3, downf3]
    hid_own = add16(hid_grads[0, 0], own2, own1)
    hid_other = add16(hid_grads[1, 0], far1, far2)

    grad_mid_norm, grad_gain_two = norm_back(middle, factor_two, gain_two, now(grad_normed_two))
    grad_middle = grad_own.astype(f32) + grad_mid_norm
    grad_attn = grad_middle.astype(bf16)
    if split:
        grad_attn = jnp.concatenate([grad_attn, to_core(grad_attn)])
    grad_mixed = dot(grad_attn, w_out, bf16)
    out_blocks = [dot_lt(columns(grad_attn, k), mixed, bf16) for k in range(4)]
    down1, downf2 = add16(down_grads[0, 1], down3), add16(down_grads[1, 2], downf3)
    close(*arrived, grad_mixed, down1, downf2, *out_blocks)

    down2 = send(line_y, swap_y, down_grads[0, 2])
    downf1 = send(line_x, swap_x, down_grads[1, 1])
    down1 = send(line_x, swap_x, down1, free=True)
    downf2 = send(line_y, swap_y, downf2, free=True)
    hid_far = send(line_c, swap_core, hid_other)
    output = (middle + out_ring.result()).astype(bf16)
    grad_qlin, grad_kv, grad_ropes = attend_back(
        heads,
        tp_size,
        window,
        scale,
        now(place),
        q_lin,
        kv_all,
        rope_keys,
        *tables,
        grad_mixed.reshape(slots, micro, rows, tp_size * out_width),
    )
    grad_qlin = grad_qlin.reshape(slots * own, tp_size * q_width)
    grad_kv = grad_kv.reshape(micro * length, tp_size * kv_width)
    close(down2, downf1, down1, downf2, hid_far, grad_ropes)

    def stage_one(blocks):
        middle_row = blocks[0].shape[0] // 2
        top, low = zip(*((each[:middle_row], each[middle_row:]) for each in blocks))
        return (
            top,
            low,
            send(line_y, swap_y, top[3], free=True),
            send(line_x, swap_x, low[3], free=True),
            send(line_y, swap_y, top[2], free=True),
            send(line_x, swap_x, low[1], free=True),
        )

    def stage_two(top, low, top3, low3, top2, low1):
        top1 = send(line_x, swap_x, add16(top[1], top3), free=True)
        low2 = send(line_y, swap_y, add16(low[2], low3), free=True)
        return top, low, top2, low1, top1, low2

    def stage_sum(top, low, top2, low1, top1, low2):
        return jnp.concatenate([add16(top[0], top2, top1), add16(low[0], low1, low2)])

    out_stage = stage_one(out_blocks)
    latent_block = KVRANK // 4
    kv_now = now(grad_kv)
    expand_blocks = [
        dot_lt(
            lax.dynamic_slice_in_dim(latent_all, (shard ^ k) * latent_block, latent_block, 1),
            kv_now,
            bf16,
        )
        for k in range(4)
    ]
    grad_latent = jnp.concatenate(
        [
            dot_rt(kv_now, w_expand, bf16).reshape(micro, length, KVRANK),
            (grad_ropes[..., :ROPE] + grad_ropes[..., ROPE:]).astype(bf16),
        ],
        axis=-1,
    ).reshape(micro, cores, span, kv_cols)
    close(*out_stage[2:], grad_latent, *expand_blocks)

    out_stage = stage_two(*out_stage)
    expand_stage = stage_one(expand_blocks)
    latent_sum = add16(mine(grad_latent, 1), send(line_c, swap_core, others(grad_latent, 1)))
    qlin_now = now(grad_qlin)
    query_blocks = [dot_lt(columns(normed_chip, k), qlin_now, bf16) for k in range(4)]
    close(*out_stage[4:], *expand_stage[2:], latent_sum, *query_blocks)

    query_stage = stage_one(query_blocks)
    expand_stage = stage_two(*expand_stage)
    grad_latent_own = scatter_z(
        line_z,
        lambda j: lax.dynamic_slice_in_dim(
            now(latent_sum), (place_z - j) % tp_size * rows, rows, 1
        ),
        f32,
    ).reshape(own, kv_cols)
    out_back = stage_sum(*out_stage)
    if split:
        query_part = dot_rt(now(grad_qlin), w_query, bf16)
        grad_normed_one = query_part[:own].astype(f32) + to_core(query_part[own:]).astype(f32)
    else:
        grad_normed_one = dot_rt(now(grad_qlin), w_query)
    close(*query_stage[2:], *expand_stage[4:], grad_latent_own)

    query_stage = stage_two(*query_stage)
    down_own = add16(down_grads[0, 0], down2, down1)
    down_other = add16(down_grads[1, 0], downf1, downf2)
    down_far = to_core(down_other)
    grad_wgate, grad_wup, grad_wdown = (
        in_order(core, near, far, 1)[:, :hidden_here].astype(f32)
        for near, far in (
            (hid_own[:, :part], hid_far[:, :part]),
            (hid_own[:, part:], hid_far[:, part:]),
            (down_own, down_far),
        )
    )
    grad_wdown = grad_wdown.T

    out_here = scatter_z(line_z, lambda j: out_back[:, out_width * j : out_width * (j + 1)])
    expand_back = stage_sum(*expand_stage)
    expand_here = scatter_z(line_z, lambda j: expand_back[:, kv_width * j : kv_width * (j + 1)])
    query_back = stage_sum(*query_stage)
    query_here = scatter_z(line_z, lambda j: query_back[:, q_width * j : q_width * (j + 1)])
    out_cores = out_here.reshape(cores, slice_rows, out_width)
    query_cores = query_here.reshape(cores, slice_rows, q_width)
    expand_cores = expand_here.reshape(cores, expand_rows, kv_width)

    def finish(by_core):
        kept, given = mine(by_core, 0), to_core(others(by_core, 0))
        if split:
            return in_order(core, kept[:, None], given[:, None], 1).astype(f32)
        return (kept.astype(f32) + given.astype(f32))[:, None]

    grad_wout = finish(out_cores).reshape(slice_rows, -1).T
    grad_wexpand = finish(expand_cores).reshape(expand_rows, -1)
    grad_wquery = q_disorder(finish(query_cores))

    grad_latent_part, grad_gain_latent = norm_back(
        latent_part, factor_latent, gain_kv, grad_latent_own[:, :KVRANK]
    )
    grad_raw = jnp.concatenate(
        [grad_latent_part, rotate(grad_latent_own[:, KVRANK:], cos_own, -sin_own)], axis=-1
    ).astype(bf16)
    grad_normed_one = grad_normed_one + dot_rt(grad_raw, w_latent)
    grad_in_norm, grad_gain_one = norm_back(inputs, factor_one, gain_one, grad_normed_one)
    input_grad = (grad_middle + grad_in_norm).astype(bf16)

    core_rows = width // 4 // cores

    def core_features(values, at, size):
        return jnp.concatenate(
            [
                lax.dynamic_slice_in_dim(values, (cores * k + at) * size, size, values.ndim - 1)
                for k in range(4)
            ],
            axis=-1,
        )

    def gains_of(at):
        pieces = [
            core_features(grads, at, grads.shape[0] // (4 * cores)).reshape(4, tp_size, -1)
            for grads in (grad_gain_one, grad_gain_two, features(grad_gain_latent))
        ]
        return jnp.concatenate(pieces, axis=-1)

    def over_all(kept, given, rounded):
        kept = kept.astype(f32) + swap_core(given.astype(rounded)).astype(f32)
        sent = kept.astype(rounded)
        total = kept[0]
        for k in (1, 2, 3):
            gone = lax.ppermute(sent[k], "shard", [(i, i ^ k) for i in range(4)])
            total = total + gone.astype(f32)
        sent = total.astype(rounded)
        here = lax.dynamic_index_in_dim(total, place_z, 0, keepdims=False)
        for j in range(1, tp_size):
            gone = lax.dynamic_index_in_dim(sent, (place_z + j) % tp_size, 0, keepdims=False)
            gone = lax.ppermute(gone, "tp", [(i, (i + j) % tp_size) for i in range(tp_size)])
            here = here + gone.astype(f32)
        return here

    grad_wlatent = over_all(
        *(
            dot_lt(core_features(normed_own, at, core_rows), grad_raw).reshape(
                4, tp_size, small_rows, kv_cols
            )
            for at in (core, 1 - core)
        ),
        bf16,
    )
    gain_grads = over_all(gains_of(core), gains_of(1 - core), f32)
    like = (micro, 1, rows, width)
    return (
        features(output).reshape(like),
        features(input_grad).reshape(like),
        gain_grads[:gain_rows],
        grad_wquery,
        grad_wlatent,
        gain_grads[2 * gain_rows :],
        grad_wexpand,
        grad_wout,
        gain_grads[gain_rows : 2 * gain_rows],
        grad_wgate,
        grad_wup,
        grad_wdown,
    )


def solution(mesh):
    tokens = P(None, "shard", ("ctx", "tp"), None)
    everywhere = P(("shard", "ctx", "tp"))
    down_split = P(("shard", "ctx"), "tp")
    up_split = P("tp", ("shard", "ctx"))
    whole_rows = P(("shard", "ctx", "tp"), None)
    return jax.shard_map(
        shards,
        mesh=mesh,
        in_specs=(
            tokens,
            P(None, "shard", None),
            tokens,
            everywhere,
            down_split,
            whole_rows,
            everywhere,
            down_split,
            up_split,
            everywhere,
            down_split,
            down_split,
            up_split,
        ),
        out_specs=(
            tokens,
            tokens,
            everywhere,
            down_split,
            whole_rows,
            everywhere,
            down_split,
            up_split,
            everywhere,
            down_split,
            down_split,
            up_split,
        ),
        check_vma=False,
    )
```

```python
import functools

import jax
import jax.numpy as jnp
from jax import lax
from jax.experimental import pallas as pl
from jax.experimental.pallas import tpu as pltpu
from jax.sharding import PartitionSpec as P

NOPE = 128
ROPE = 64
VHEAD = 128
KVRANK = 512
DOC_MOST = 512
LANES = 128

EPSILON = 1e-06
THETA_BASE = 10000.0
NEG_FILL = -1e30

f32 = jnp.float32
bf16 = jnp.bfloat16


def norm_scale(values):
    return lax.rsqrt(jnp.mean(values * values, axis=-1, keepdims=True) + EPSILON)


def norm_back(values, factor, gain_vec, grad_out):
    scaled = grad_out * gain_vec
    grad_in = factor * scaled - values * factor**3 * jnp.mean(
        scaled * values, axis=-1, keepdims=True
    )
    return (grad_in, jnp.sum(grad_out * values * factor, axis=0))


def rotate(values, cos_table, sin_table):
    half_width = values.shape[-1] // 2
    first_half = values[..., :half_width]
    second_half = values[..., half_width:]
    return jnp.concatenate(
        [
            first_half * cos_table - second_half * sin_table,
            second_half * cos_table + first_half * sin_table,
        ],
        axis=-1,
    )


def dot(left, right, kind=f32):
    return jnp.dot(left, right, preferred_element_type=f32).astype(kind)


def dot_rt(left, right, kind=f32):
    return lax.dot_general(
        left, right, (((1,), (1,)), ((), ())), preferred_element_type=f32
    ).astype(kind)


def dot_lt(left, right, kind=f32):
    return lax.dot_general(
        left, right, (((0,), (0,)), ((), ())), preferred_element_type=f32
    ).astype(kind)


def add16(*terms):
    total = terms[0].astype(f32)
    for term in terms[1:]:
        total = total + term.astype(f32)
    return total.astype(bf16)


def after(value, *others):
    return lax.optimization_barrier((value, *others))[0]


class Line:
    def __init__(self):
        self.last = None

    def send(self, move, value, *needs, free=False):
        if self.last is not None and not free:
            needs = (*needs, self.last)
        if needs:
            value = after(value, *needs)
        self.last = move(value)
        return self.last


def swap_core(value):
    return lax.ppermute(value, "ctx", [(0, 1), (1, 0)])


def swap_x(value):
    return lax.ppermute(value, "shard", [(i, i ^ 1) for i in range(4)])


def swap_y(value):
    return lax.ppermute(value, "shard", [(i, i ^ 2) for i in range(4)])


def step_z(value):
    size = lax.axis_size("tp")
    return lax.ppermute(value, "tp", [(i, (i + 1) % size) for i in range(size)])


def gather_xy(line_x, line_y, x_first, y_first):
    ax = line_x.send(swap_x, x_first)
    by = line_y.send(swap_y, y_first)
    ay = line_y.send(swap_y, x_first)
    bx = line_x.send(swap_x, y_first)
    axy = line_y.send(swap_y, ax)
    byx = line_x.send(swap_x, by)
    return [x_first, ax, ay, axy], [y_first, bx, by, byx]


def scatter_yfirst(line_x, line_y, blocks, last=bf16):
    three, two = line_y.send(swap_y, blocks[3]), line_y.send(swap_y, blocks[2])
    other = line_x.send(swap_x, add16(blocks[1], three))
    total = blocks[0].astype(f32) + two.astype(f32) + other.astype(f32)
    return total.astype(last)


def scatter_xfirst(line_x, line_y, blocks, last=bf16):
    three, one = line_x.send(swap_x, blocks[3]), line_x.send(swap_x, blocks[1])
    other = line_y.send(swap_y, add16(blocks[2], three))
    total = blocks[0].astype(f32) + one.astype(f32) + other.astype(f32)
    return total.astype(last)


def scatter_z(line_z, block_of, last=bf16, add=add16):
    size = lax.axis_size("tp")
    total = block_of(1)
    for j in range(2, size):
        total = add(line_z.send(step_z, total), block_of(j))
    return (line_z.send(step_z, total).astype(f32) + block_of(0).astype(f32)).astype(last)


def in_order(core, mine, other, axis):
    return jnp.where(
        core == 0,
        jnp.concatenate([mine, other], axis=axis),
        jnp.concatenate([other, mine], axis=axis),
    )


def assemble(sources, moves, shapes, place):
    depth = min(32, len(moves))

    def kernel(place_ref, *refs):
        given, made, sems = refs[: len(sources)], refs[len(sources) : -1], refs[-1]
        flight = []
        for i, (src, row, rows, column, columns, dst, to_row, to_column) in enumerate(moves):
            if i >= depth:
                flight[i - depth].wait()
            if not isinstance(to_row, int):
                to_row = pl.multiple_of(to_row[1](place_ref), to_row[0])
            copy = pltpu.make_async_copy(
                given[src].at[pl.ds(row, rows), pl.ds(column, columns)],
                made[dst].at[pl.ds(to_row, rows), pl.ds(to_column, columns)],
                sems.at[i % depth],
            )
            copy.start()
            flight.append(copy)
        for copy in flight[-depth:]:
            copy.wait()

    return pl.pallas_call(
        kernel,
        out_shape=[jax.ShapeDtypeStruct(shape, bf16) for shape in shapes],
        grid_spec=pltpu.PrefetchScalarGridSpec(
            num_scalar_prefetch=1,
            in_specs=[pl.BlockSpec(memory_space=pl.ANY)] * len(sources),
            out_specs=[pl.BlockSpec(memory_space=pltpu.VMEM)] * len(shapes),
            scratch_shapes=[pltpu.SemaphoreType.DMA((depth,))],
        ),
        compiler_params=pltpu.CompilerParams(vmem_limit_bytes=48 << 20),
        cost_estimate=pl.CostEstimate(
            flops=0,
            transcendentals=0,
            bytes_accessed=4 * sum(a * b for a, b in shapes),
        ),
        name="assemble",
    )(place, *sources)


def lay_out_kernel(places, *refs):
    given, (latent, rope) = refs[:-2], refs[-2:]
    micro, rows = latent.shape[0], given[0].shape[1]
    pieces = [each[i : i + micro] for each in given for i in range(0, each.shape[0], micro)]
    for place, piece in zip(range(len(pieces)), pieces):
        at = pl.ds(pl.multiple_of(places[place], rows), rows)
        latent[:, at, :] = piece[:, :, :KVRANK]
        keys = piece[:, :, KVRANK:]
        rope[:, at, :] = jnp.concatenate([keys, keys], axis=-1)


def lay_out(places, pieces, micro, length):
    in_vmem = pl.BlockSpec(memory_space=pltpu.VMEM)
    return pl.pallas_call(
        lay_out_kernel,
        out_shape=[
            jax.ShapeDtypeStruct((micro, length, KVRANK), bf16),
            jax.ShapeDtypeStruct((micro, length, 2 * ROPE), bf16),
        ],
        grid_spec=pltpu.PrefetchScalarGridSpec(
            num_scalar_prefetch=1,
            in_specs=[in_vmem] * len(pieces),
            out_specs=[in_vmem] * 2,
        ),
        cost_estimate=pl.CostEstimate(
            flops=0, transcendentals=0, bytes_accessed=4 * micro * length * (KVRANK + 2 * ROPE)
        ),
        name="lay_out",
    )(places, *pieces)


SENT_BLOCKS = (((3, 0), (2, 0)), ((3, 1), (1, 1)), ((1, 0), (0, 0), (2, 1), (0, 1)))


def swap_halves(values, lane):
    return jnp.where(
        lane % ROPE < ROPE // 2,
        pltpu.roll(values, LANES - ROPE // 2, 1),
        pltpu.roll(values, ROPE // 2, 1),
    )


def window_mask(start, base, rows, width, seg_query, seg_key):
    query_index = base + lax.broadcasted_iota(jnp.int32, (rows, width), 0)
    key_index = start + lax.broadcasted_iota(jnp.int32, (rows, width), 1)
    same_doc = (seg_query == seg_key) & (key_index <= query_index) & (seg_key != 0)
    return same_doc | (key_index == query_index)


def head_operands(q_ref, kv_ref, rope_key, slot, window, head, heads, cos_table, sin_table):
    rows = q_ref.shape[2]
    lane = lax.broadcasted_iota(jnp.int32, (rows, LANES), 1)
    first = heads * NOPE + head // 2 * LANES
    rope_lin = q_ref[slot, 0, :, first : first + LANES]
    turned = rope_lin * cos_table + swap_halves(rope_lin, lane) * sin_table
    turned = jnp.where(lane // ROPE == head % 2, turned, 0.0)
    plain = q_ref[slot, 0, :, head * NOPE : (head + 1) * NOPE]
    query = jnp.concatenate([plain, turned], axis=1).astype(bf16)
    at = head * (NOPE + VHEAD)
    key = jnp.concatenate([kv_ref[0, window, at : at + NOPE], rope_key], axis=1)
    value = kv_ref[0, window, at + NOPE : at + NOPE + VHEAD]
    return query, key, value


def attend_kernel(
    heads, width, scale, place, q_ref, kv_ref, kr_ref, segq_ref, segk_ref, cos_ref, sin_ref, o_ref
):
    slots, rows = q_ref.shape[0], q_ref.shape[2]
    for slot in range(slots):
        start = pl.multiple_of(place[slot, 0], rows)
        window = pl.ds(start, width)
        allowed = window_mask(
            start,
            place[slot, 1],
            rows,
            width,
            segq_ref[0, slot * rows : (slot + 1) * rows, :],
            segk_ref[0, slot : slot + 1, :],
        )
        rope_key = kr_ref[0, window, :]
        for head in range(heads):
            query, key, value = head_operands(
                q_ref, kv_ref, rope_key, slot, window, head, heads, cos_ref[slot, 0], sin_ref[slot, 0]
            )
            scores = jnp.where(allowed, dot_rt(query, key) * scale, NEG_FILL)
            expd = jnp.exp(scores - jnp.max(scores, axis=-1, keepdims=True))
            probs = expd / jnp.sum(expd, axis=-1, keepdims=True)
            o_ref[slot, 0, :, head * VHEAD : (head + 1) * VHEAD] = dot(
                probs.astype(bf16), value, bf16
            )


def attend_back_kernel(
    heads,
    width,
    scale,
    groups,
    place,
    q_ref,
    kv_ref,
    kr_ref,
    segq_ref,
    segk_ref,
    cos_ref,
    sin_ref,
    do_ref,
    norm_ref,
    latent_ref,
    wq_ref,
    wkv_ref,
    *refs,
):
    slots, rows = q_ref.shape[0], q_ref.shape[2]
    q_width, kv_width = q_ref.shape[3], kv_ref.shape[2]
    query_outs, expand_outs, latent_outs = refs[:3], refs[3:6], refs[6:8]
    parts, (total, rope_total, kv_grads, q_grads, expand_grads) = refs[8:-5], refs[-5:]
    group, m = pl.program_id(0), pl.program_id(1)
    micro = pl.num_programs(1)
    lane = lax.broadcasted_iota(jnp.int32, (rows, LANES), 1)
    q_first = pl.multiple_of(group * q_width, LANES)
    kv_first = pl.multiple_of(group * kv_width, LANES)

    def q_rows(slot):
        return pl.ds(pl.multiple_of((slot * micro + m) * rows, rows), rows)

    @pl.when(group == 0)
    def _():
        rope_total[m] = jnp.zeros(rope_total.shape[1:], f32)

    total[...] = jnp.zeros_like(total)
    for slot in range(slots):
        start = pl.multiple_of(place[slot, 0], rows)
        window = pl.ds(start, width)
        allowed = window_mask(
            start,
            place[slot, 1],
            rows,
            width,
            segq_ref[0, slot * rows : (slot + 1) * rows, :],
            segk_ref[0, slot : slot + 1, :],
        )
        rope_key = kr_ref[0, window, :]
        rope_grads = None
        for head in range(heads):
            query, key, value = head_operands(
                q_ref, kv_ref, rope_key, slot, window, head, heads, cos_ref[slot, 0], sin_ref[slot, 0]
            )
            grad_mixed = do_ref[slot, 0, :, head * VHEAD : (head + 1) * VHEAD]
            scores = jnp.where(allowed, dot_rt(query, key) * scale, NEG_FILL)
            expd = jnp.exp(scores - jnp.max(scores, axis=-1, keepdims=True))
            probs = expd / jnp.sum(expd, axis=-1, keepdims=True)
            grad_probs = dot_rt(grad_mixed, value)
            inner = jnp.sum(probs * grad_probs, axis=-1, keepdims=True)
            grad_scores = (scale * probs * (grad_probs - inner)).astype(bf16)
            grad_query = dot(grad_scores, key)
            grad_key = dot_lt(grad_scores, query)
            at = head * (NOPE + VHEAD)
            total[window, at : at + NOPE] += grad_key[:, :NOPE]
            rope_total[m, window, :] += grad_key[:, NOPE:]
            total[window, at + NOPE : at + NOPE + VHEAD] += dot_lt(probs.astype(bf16), grad_mixed)
            q_grads[q_rows(slot), pl.ds(q_first + head * NOPE, NOPE)] = grad_query[:, :NOPE].astype(
                bf16
            )
            if head % 2 == 0:
                rope_grads = jnp.where(lane < ROPE, grad_query[:, NOPE:], 0.0)
            else:
                rope_grads = jnp.where(lane < ROPE, rope_grads, grad_query[:, NOPE:])
            if head % 2 == 1 or head == heads - 1:
                turned = rope_grads * cos_ref[slot, 0] - swap_halves(rope_grads, lane) * sin_ref[slot, 0]
                first = q_first + heads * NOPE + head // 2 * LANES
                q_grads[q_rows(slot), pl.ds(first, LANES)] = turned.astype(bf16)
    kv_grads[m, :, pl.ds(kv_first, kv_width)] = total[...].astype(bf16)

    @pl.when(m == micro - 1)
    def _():
        grads = dot_lt(norm_ref[...], q_grads[:, pl.ds(q_first, q_width)], bf16)
        size = grads.shape[0] // 8
        for out, blocks in zip(query_outs, SENT_BLOCKS):
            for i, (k, half) in enumerate(blocks):
                out[i * size : (i + 1) * size, :] = grads[(2 * k + half) * size :][:size]
        back = kv_grads[:, :, pl.ds(kv_first, kv_width)]
        expand_grads[...] = dot_lt(
            latent_ref[...], back.reshape(latent_ref.shape[0], kv_width), bf16
        )
        size = expand_grads.shape[0] // 8
        shard = place[slots, 0]
        for out, blocks in zip(expand_outs, SENT_BLOCKS):
            for i, (k, half) in enumerate(blocks):
                at = pl.multiple_of((2 * (shard ^ k) + half) * size, size)
                out[i * size : (i + 1) * size, :] = expand_grads[pl.ds(at, size), :]

    @pl.when(group == groups - 1)
    def _():
        span = latent_outs[0].shape[1]
        for out, half in zip(latent_outs, (place[slots, 1], 1 - place[slots, 1])):
            at = pl.ds(pl.multiple_of(half * span, span), span)
            out[0, :, :KVRANK] = dot_rt(kv_grads[m, at, :], wkv_ref[...], bf16)
            ropes = rope_total[m, at, :]
            ropes = ropes + pltpu.roll(ropes, ROPE, 1)
            out[0, :, KVRANK:] = ropes[:, :ROPE].astype(bf16)
        for slot, out in enumerate(parts):
            out[0] = dot_rt(q_grads[q_rows(slot), :], wq_ref[...], bf16)


def attention_specs(heads, slots, rows, length, width, q_width, order):
    def at(*index):
        return lambda a, b, place: tuple(
            {"m": (a, b)[order], "j": (a, b)[1 - order]}.get(i, i) for i in index
        )

    return [
        pl.BlockSpec((slots, 1, rows, q_width), at(0, "m", 0, "j")),
        pl.BlockSpec((1, length, heads * (NOPE + VHEAD)), at("m", 0, "j")),
        pl.BlockSpec((1, length, LANES), at("m", 0, 0)),
        pl.BlockSpec((1, slots * rows, 1), at("m", 0, 0)),
        pl.BlockSpec((1, slots, width), at("m", 0, 0)),
        pl.BlockSpec((slots, 1, rows, LANES), at(0, "m", 0, 0)),
        pl.BlockSpec((slots, 1, rows, LANES), at(0, "m", 0, 0)),
    ]


def attend(heads, groups, width, scale, place, q_lin, kv, rope_keys, seg_query, seg_key, cos, sin):
    slots, micro, rows, q_all = q_lin.shape
    length = kv.shape[1]
    return pl.pallas_call(
        functools.partial(attend_kernel, heads, width, scale),
        out_shape=jax.ShapeDtypeStruct((slots, micro, rows, groups * heads * VHEAD), bf16),
        grid_spec=pltpu.PrefetchScalarGridSpec(
            num_scalar_prefetch=1,
            grid=(micro, groups),
            in_specs=attention_specs(heads, slots, rows, length, width, q_all // groups, 0),
            out_specs=pl.BlockSpec(
                (slots, 1, rows, heads * VHEAD), lambda m, j, place: (0, m, 0, j)
            ),
        ),
        compiler_params=pltpu.CompilerParams(
            dimension_semantics=("arbitrary", "arbitrary"), vmem_limit_bytes=40 << 20
        ),
        cost_estimate=pl.CostEstimate(
            flops=2 * slots * rows * micro * groups * heads * width * 384,
            transcendentals=slots * rows * micro * groups * heads * width,
            bytes_accessed=2 * kv.size + 6 * q_lin.size,
        ),
        name="attend",
    )(place, q_lin, kv, rope_keys, seg_query, seg_key, cos, sin)


def attend_back(
    heads,
    groups,
    width,
    scale,
    place,
    q_lin,
    kv,
    rope_keys,
    seg_query,
    seg_key,
    cos,
    sin,
    d_o,
    normed,
    latents,
    w_query,
    w_expand,
):
    slots, micro, rows, q_all = q_lin.shape
    length = kv.shape[1]
    tokens, model = normed.shape
    q_width, kv_width = q_all // groups, kv.shape[2] // groups
    latent_width = KVRANK + ROPE

    def last(j, m, place):
        return (jnp.where(j == groups - 1, m, 0), 0, 0)

    def whole(shape):
        return pl.BlockSpec(shape, lambda j, m, place: (0, 0), pipeline_mode=pl.Buffered(1))

    def sent(total, columns):
        return [
            (jax.ShapeDtypeStruct((n * total // 8, columns * groups), bf16), n * total // 8, columns)
            for n in (2, 2, 4)
        ]

    grads = sent(model, q_width) + sent(KVRANK, kv_width)
    return pl.pallas_call(
        functools.partial(attend_back_kernel, heads, width, scale, groups),
        out_shape=[
            *(shape for shape, _, _ in grads),
            *[jax.ShapeDtypeStruct((micro, length // 2, latent_width), bf16)] * 2,
            *[jax.ShapeDtypeStruct((micro, rows, model), bf16)] * slots,
        ],
        grid_spec=pltpu.PrefetchScalarGridSpec(
            num_scalar_prefetch=1,
            grid=(groups, micro),
            in_specs=attention_specs(heads, slots, rows, length, width, q_width, 1)
            + [
                pl.BlockSpec((slots, 1, rows, heads * VHEAD), lambda j, m, place: (0, m, 0, j)),
                whole(normed.shape),
                whole(latents.shape),
                whole(w_query.shape),
                whole(w_expand.shape),
            ],
            out_specs=[
                *(
                    pl.BlockSpec((height, columns), lambda j, m, place: (0, j))
                    for _, height, columns in grads
                ),
                *[pl.BlockSpec((1, length // 2, latent_width), last)] * 2,
                *[pl.BlockSpec((1, rows, model), last)] * slots,
            ],
            scratch_shapes=[
                pltpu.VMEM((length, kv_width), f32),
                pltpu.VMEM((micro, length, LANES), f32),
                pltpu.VMEM(kv.shape, bf16),
                pltpu.VMEM((tokens, q_all), bf16),
                pltpu.VMEM((KVRANK, kv_width), bf16),
            ],
        ),
        compiler_params=pltpu.CompilerParams(
            dimension_semantics=("arbitrary", "arbitrary"), vmem_limit_bytes=60 << 20
        ),
        cost_estimate=pl.CostEstimate(
            flops=2 * slots * rows * micro * groups * heads * width * 1024
            + 4 * tokens * model * q_all
            + 4 * micro * length * KVRANK * kv.shape[2],
            transcendentals=slots * rows * micro * groups * heads * width,
            bytes_accessed=2 * kv.size + 4 * q_lin.size + 8 * w_query.size,
        ),
        name="attend_back",
    )(
        place,
        q_lin,
        kv,
        rope_keys,
        seg_query,
        seg_key,
        cos,
        sin,
        d_o,
        normed,
        latents,
        w_query,
        w_expand,
    )


def spans(total, step):
    return [(at, min(step, total - at)) for at in range(0, total, step)]


def feed_kernel(part, rows, offset, place, *refs):
    given, refs = refs[:20], refs[20:]
    refs = refs[4:] if offset else refs
    back_own, back_other, out_own, out_other, act_all, hid_all, norm_all, grad_all = refs[:8]
    w_hid, w_down, norm, grad, d_act, act, hid, sems = refs[8:]
    norm_own, norm_other, grad_own, grad_other = given[:4]
    slice_rows = given[4].shape[0]

    def at_core(i):
        core = place[0] if i < 4 else 1 - place[0]
        return pl.ds(pl.multiple_of((2 * (i % 4) + core) * slice_rows, slice_rows), slice_rows)

    early = [
        pltpu.make_async_copy(grad_own, grad.at[pl.ds(0, rows)], sems.at[0]),
        pltpu.make_async_copy(grad_other, grad.at[pl.ds(rows, rows)], sems.at[1]),
    ] + [
        pltpu.make_async_copy(given[12 + i], w_down.at[at_core(i)], sems.at[2 + i])
        for i in range(8)
    ]
    later = [
        pltpu.make_async_copy(norm_own, norm.at[pl.ds(0, rows)], sems.at[10]),
        pltpu.make_async_copy(norm_other, norm.at[pl.ds(rows, rows)], sems.at[11]),
    ] + [
        pltpu.make_async_copy(given[4 + i], w_hid.at[at_core(i)], sems.at[12 + i])
        for i in range(8)
    ]
    for copy in early + later:
        copy.start()
    for copy in early:
        copy.wait()

    def for_chunks(total, body):
        whole = total // 256

        def step(i, carry):
            body(pl.multiple_of(i * 256, 256), 256)
            return carry

        lax.fori_loop(0, whole, step, 0)
        if total % 256:
            body(whole * 256, total % 256)

    def act_back(start, size):
        d_act[:, pl.ds(start, size)] = dot(grad[...], w_down[:, pl.ds(start, size)])

    for_chunks(part, act_back)
    for copy in later:
        copy.wait()

    def forward(start, size):
        gate = dot(norm[...], w_hid[:, pl.ds(start, size)])
        up_at = start + part
        if not isinstance(start, int):
            up_at = pl.multiple_of(up_at, LANES)
        up = dot(norm[...], w_hid[:, pl.ds(up_at, size)])
        back = d_act[:, pl.ds(start, size)]
        sigma = jax.nn.sigmoid(gate)
        swish = gate * sigma
        act[:, pl.ds(start, size)] = (swish * up).astype(bf16)
        hid[:, pl.ds(start, size)] = (
            back * up * sigma * (1.0 + gate * (1.0 - sigma))
        ).astype(bf16)
        hid[:, pl.ds(up_at, size)] = (back * swish).astype(bf16)

    for_chunks(part, forward)
    here = pl.ds(offset * 2 * rows, 2 * rows)
    saves = [
        pltpu.make_async_copy(source, target.at[here], sems.at[20 + i])
        for i, (source, target) in enumerate(
            ((act, act_all), (hid, hid_all), (norm, norm_all), (grad, grad_all))
        )
    ]
    for copy in saves:
        copy.start()

    def backward(start, size):
        back = dot_rt(hid[...], w_hid[pl.ds(start, size), :], bf16)
        back_own[:, pl.ds(start, size)] = back[:rows]
        back_other[:, pl.ds(start, size)] = back[rows:]
        out = dot_rt(act[...], w_down[pl.ds(start, size), :], bf16)
        out_own[:, pl.ds(start, size)] = out[:rows]
        out_other[:, pl.ds(start, size)] = out[rows:]

    for_chunks(w_hid.shape[0], backward)
    for copy in saves:
        copy.wait()


def feed(place, offset, blocks, tokens, hidden_pieces, down_pieces, whole):
    rows, width = tokens[0].shape
    part = down_pieces[0].shape[1]
    anywhere = pl.BlockSpec(memory_space=pl.ANY)
    in_vmem = pl.BlockSpec(memory_space=pltpu.VMEM)
    total = 2 * rows * blocks
    operands = [*tokens, *hidden_pieces, *down_pieces, *whole]
    return pl.pallas_call(
        functools.partial(feed_kernel, part, rows, offset),
        out_shape=[jax.ShapeDtypeStruct((rows, width), bf16)] * 4
        + [
            jax.ShapeDtypeStruct((total, columns), bf16)
            for columns in (part, 2 * part, width, width)
        ],
        grid_spec=pltpu.PrefetchScalarGridSpec(
            num_scalar_prefetch=1,
            in_specs=[anywhere] * len(operands),
            out_specs=[in_vmem] * 4 + [anywhere] * 4,
            scratch_shapes=[
                pltpu.VMEM((width, 2 * part), bf16),
                pltpu.VMEM((width, part), bf16),
                pltpu.VMEM((2 * rows, width), bf16),
                pltpu.VMEM((2 * rows, width), bf16),
                pltpu.VMEM((2 * rows, part), f32),
                pltpu.VMEM((2 * rows, part), bf16),
                pltpu.VMEM((2 * rows, 2 * part), bf16),
                pltpu.SemaphoreType.DMA((24,)),
            ],
        ),
        input_output_aliases={21 + i: 4 + i for i in range(len(whole))},
        compiler_params=pltpu.CompilerParams(vmem_limit_bytes=58 << 20),
        cost_estimate=pl.CostEstimate(
            flops=2 * 2 * rows * width * part * 6,
            transcendentals=2 * rows * part,
            bytes_accessed=2 * (3 * width * part + 2 * rows * (6 * width + 3 * part)),
        ),
        name="feed",
    )(place, *operands)


def pack_kernel(part, place, gate, up, down, hid_mine, hid_other, down_mine, down_other):
    slice_rows, hidden_here = gate.shape
    rest = hidden_here - part

    def put(at, low, high, value):
        low[:, at : at + part] = value[:, :part]
        if rest < part:
            edge = rest // LANES * LANES
            high[:, at + edge : at + part] = jnp.zeros((slice_rows, part - edge), bf16)
        high[:, at : at + rest] = value[:, part:]

    def write(hid_low, hid_high, down_low, down_high):
        put(0, hid_low, hid_high, gate[...])
        put(part, hid_low, hid_high, up[...])
        put(0, down_low, down_high, down[...].T)

    @pl.when(place[0] == 0)
    def _():
        write(hid_mine, hid_other, down_mine, down_other)

    @pl.when(place[0] != 0)
    def _():
        write(hid_other, hid_mine, down_other, down_mine)


def pack(place, part, gate, up, down):
    slice_rows = gate.shape[0]
    in_vmem = pl.BlockSpec(memory_space=pltpu.VMEM)
    return pl.pallas_call(
        functools.partial(pack_kernel, part),
        out_shape=[jax.ShapeDtypeStruct((slice_rows, n * part), bf16) for n in (2, 2, 1, 1)],
        grid_spec=pltpu.PrefetchScalarGridSpec(
            num_scalar_prefetch=1, in_specs=[in_vmem] * 3, out_specs=[in_vmem] * 4
        ),
        compiler_params=pltpu.CompilerParams(vmem_limit_bytes=48 << 20),
        cost_estimate=pl.CostEstimate(
            flops=0, transcendentals=0, bytes_accessed=24 * slice_rows * part
        ),
        name="pack",
    )(place, gate, up, down)


def weight_grad_kernel(packs, place, left, right_ref, *refs):
    packed, (turned, buffer, sems) = refs[:-3], refs[-3:]
    slice_rows, tokens = packed[0].shape[0] // len(packs[0]), turned.shape[1]
    blocks = [block for pack in packs for block in pack]
    outs = [
        out.at[pl.ds(i * slice_rows, slice_rows)]
        for out, pack in zip(packed, packs)
        for i in range(len(pack))
    ]

    def fetch(i):
        k, half = blocks[i]
        core = place[0] if half == 0 else 1 - place[0]
        start = pl.multiple_of((2 * k + core) * slice_rows, slice_rows)
        return pltpu.make_async_copy(
            left.at[:, pl.ds(start, slice_rows)], buffer.at[i % 2], sems.at[i % 2]
        )

    @pl.when(pl.program_id(0) == 0)
    def _():
        fetch(0).start()
        for i in range(len(outs)):
            fetch(i).wait()
            if i + 1 < len(outs):
                fetch(i + 1).start()

            def turn(j, carry, i=i):
                at = pl.ds(pl.multiple_of(j * 256, 256), 256)
                turned[pl.ds(i * slice_rows, slice_rows), at] = buffer[i % 2, at, :].T
                return carry

            lax.fori_loop(0, tokens // 256, turn, 0)

    for half in range(0, len(outs), 4):
        rows = pl.ds(half * slice_rows, 4 * slice_rows)
        grads = dot(turned[rows, :], right_ref[...], bf16)
        for i in range(4):
            outs[half + i][...] = grads[i * slice_rows : (i + 1) * slice_rows]


def weight_grad(place, packs, slice_rows, left, right):
    tokens, columns = right.shape
    count = sum(len(pack) for pack in packs)
    heights = [len(pack) * slice_rows for pack in packs]
    return pl.pallas_call(
        functools.partial(weight_grad_kernel, packs),
        out_shape=[jax.ShapeDtypeStruct((height, columns), bf16) for height in heights],
        grid_spec=pltpu.PrefetchScalarGridSpec(
            num_scalar_prefetch=1,
            grid=(-(-columns // 256),),
            in_specs=[
                pl.BlockSpec(memory_space=pl.ANY),
                pl.BlockSpec((tokens, 256), lambda n, place: (0, n)),
            ],
            out_specs=[pl.BlockSpec((height, 256), lambda n, place: (0, n)) for height in heights],
            scratch_shapes=[
                pltpu.VMEM((count * slice_rows, tokens), bf16),
                pltpu.VMEM((2, tokens, slice_rows), bf16),
                pltpu.SemaphoreType.DMA((2,)),
            ],
        ),
        compiler_params=pltpu.CompilerParams(
            dimension_semantics=("arbitrary",), vmem_limit_bytes=48 << 20
        ),
        cost_estimate=pl.CostEstimate(
            flops=2 * tokens * columns * count * slice_rows,
            transcendentals=0,
            bytes_accessed=2 * (tokens * columns + count * slice_rows * (tokens + columns)),
        ),
        name="weight_grad",
    )(place, left, right)


def shards(
    hidden,
    segments,
    cotangent,
    attn_gain,
    q_weight,
    latent_weight,
    latent_gain,
    expand_weight,
    out_weight,
    mlp_gain,
    gate_weight,
    up_weight,
    down_weight,
):
    micro, _, rows, width = hidden.shape
    length = segments.shape[2]
    tp_size, cores = lax.axis_size("tp"), lax.axis_size("ctx")
    shard, core, place_z = lax.axis_index("shard"), lax.axis_index("ctx"), lax.axis_index("tp")
    span = rows * tp_size
    own = micro * rows
    block = width // 4
    slice_rows = q_weight.shape[0]
    heads_here = q_weight.shape[1] // (NOPE + ROPE)
    split = heads_here % cores == 0
    heads = heads_here // cores if split else heads_here
    slots = cores if split else 1
    rope_width = -(-heads * ROPE // LANES) * LANES
    q_width = heads * NOPE + rope_width
    scale = (NOPE + ROPE) ** (-0.5)
    hidden_here = gate_weight.shape[1]
    part = -(-hidden_here // (cores * LANES)) * LANES
    window = min(length, -(-(DOC_MOST + rows) // LANES) * LANES)

    line_x, line_y, line_z, line_c = Line(), Line(), Line(), Line()

    def features(values):
        size = values.shape[-1] // 4
        return jnp.concatenate(
            [
                lax.dynamic_slice_in_dim(values, (shard ^ k) * size, size, values.ndim - 1)
                for k in range(4)
            ],
            axis=-1,
        )

    def columns(values, k):
        return values[:, block * k : block * (k + 1)]

    def mine(values, axis):
        return lax.dynamic_index_in_dim(values, core, axis, keepdims=False)

    def others(values, axis):
        return lax.dynamic_index_in_dim(values, 1 - core, axis, keepdims=False)

    def to_core(value):
        return line_c.send(swap_core, value)

    small_rows = latent_weight.shape[0]
    gain_rows, latent_gains = attn_gain.shape[0], latent_gain.shape[0]
    kv_cols = latent_weight.shape[1]
    gains_row = jnp.concatenate([attn_gain, mlp_gain, latent_gain])
    gains_row = jnp.pad(gains_row, (0, kv_cols - gains_row.shape[0]))
    small = jnp.concatenate([latent_weight, jnp.pad(gains_row[None], ((0, 15), (0, 0)))])
    small_all = lax.all_gather(small, ("shard", "ctx", "tp"), axis=0)
    devices = 4 * cores * tp_size

    def own_first(values):
        size = values.shape[0] // 4
        return jnp.concatenate(
            [lax.dynamic_slice_in_dim(values, (shard ^ k) * size, size, 0) for k in range(4)]
        )

    w_latent = own_first(small_all[:, :small_rows].reshape(width, kv_cols))
    gain_all = small_all[:, small_rows].astype(f32)
    gain_one = own_first(gain_all[:, :gain_rows].reshape(width))
    gain_two = own_first(gain_all[:, gain_rows : 2 * gain_rows].reshape(width))
    gain_kv = gain_all[:, 2 * gain_rows : 2 * gain_rows + latent_gains].reshape(KVRANK)
    del devices

    def q_order(values):
        groups = values.shape[1] // (heads * (NOPE + ROPE))
        by_head = values.reshape(values.shape[0], groups, heads, NOPE + ROPE)
        plain = by_head[..., :NOPE].reshape(values.shape[0], groups, heads * NOPE)
        rope = by_head[..., NOPE:].reshape(values.shape[0], groups, heads * ROPE)
        rope = jnp.pad(rope, ((0, 0), (0, 0), (0, rope_width - heads * ROPE)))
        return jnp.concatenate([plain, rope], axis=-1)

    def q_disorder(values):
        lead = values.shape[:2]
        plain = values[..., : heads * NOPE].reshape(*lead, heads, NOPE)
        rope = values[..., heads * NOPE : heads * (NOPE + ROPE)].reshape(*lead, heads, ROPE)
        return jnp.concatenate([plain, rope], axis=-1).reshape(lead[0], -1)

    expand_rows = expand_weight.shape[0]
    kv_width = heads * (NOPE + VHEAD)
    out_width = heads * VHEAD
    stack = slice_rows // expand_rows
    blocks_kv = kv_width // LANES
    expand_cols = -(-blocks_kv // stack)
    groups = cores if split else 1

    def expand_stack(values):
        tiles = [values[:, LANES * i : LANES * (i + 1)] for i in range(blocks_kv)]
        tiles += [jnp.zeros_like(tiles[0])] * (expand_cols * stack - blocks_kv)
        return jnp.concatenate(
            [jnp.concatenate(tiles[stack * i : stack * (i + 1)]) for i in range(expand_cols)],
            axis=1,
        )

    q_local = q_order(q_weight)
    out_local = out_weight.T
    packs = jnp.stack(
        [
            jnp.concatenate(
                [
                    q_local[:, g],
                    out_local[:, out_width * g : out_width * (g + 1)],
                    expand_stack(expand_weight[:, kv_width * g : kv_width * (g + 1)]),
                ],
                axis=1,
            )
            for g in range(groups)
        ]
    )
    pack_mine, pack_other = (mine(packs, 0), others(packs, 0)) if split else (packs[0], packs[0])
    attn_piece = jnp.concatenate([pack_mine, to_core(pack_other)])

    shift = jnp.stack([core, shard]).astype(jnp.int32)

    tokens = ()

    def now(value):
        return after(value, *tokens) if tokens else value

    def send(line, move, value, free=False):
        return line.send(move, now(value), free=free)

    def close(*arrived):
        nonlocal tokens
        tokens = arrived

    attn_z, held = [attn_piece], {}
    wanted = []
    for j in range(tp_size):
        lead, tail = (1, 2) if j % 2 == 0 else (2, 1)
        wanted.append((j, lead, 0, lead == 1, True))
        wanted.append((j, tail, 0, tail == 1, False))
        wanted.append((j, 3, lead, lead == 2, False))

    def attention_round():
        for j, piece in enumerate(attn_z):
            held.setdefault((j, 0), piece)
        keys, arrived = [], []
        for over_x in (True, False):
            ready = [w for w in wanted if w[3] == over_x and (w[0], w[2]) in held]
            ready.sort(key=lambda w: not w[4])
            if ready:
                j, k, source = ready[0][:3]
                wanted.remove(ready[0])
                line, move = (line_x, swap_x) if over_x else (line_y, swap_y)
                arrived.append(send(line, move, held[j, source]))
                keys.append((j, k))
        held.update(zip(keys, arrived))
        if len(attn_z) < tp_size:
            attn_z.append(send(line_z, step_z, attn_z[-1]))
            arrived.append(attn_z[-1])
        return arrived

    close(*attention_round())
    arrived = attention_round()
    hid_a, hid_other, down_a, down_other = pack(
        now(shift), part, gate_weight, up_weight, down_weight
    )
    down_b, hid_b = to_core(down_other), to_core(hid_other)
    grad_own = features(now(cotangent).reshape(own, width))
    inputs16 = features(now(hidden).reshape(own, width))
    inputs = inputs16.astype(f32)
    seg_all = now(segments)[:, 0]
    bases = [core * span + place_z * rows, (1 - core) * span + place_z * rows][:slots]
    starts = [jnp.maximum(base + rows - window, 0) for base in bases]
    place = jnp.stack(
        [jnp.stack([a, b]) for a, b in zip(starts + [shard], bases + [core])]
    ).astype(jnp.int32)
    seg_query = jnp.concatenate(
        [lax.dynamic_slice_in_dim(seg_all, base, rows, 1) for base in bases], axis=1
    )
    seg_key = jnp.stack(
        [lax.dynamic_slice_in_dim(seg_all, start, window, 1) for start in starts], axis=1
    )
    query_index = jnp.concatenate([base + jnp.arange(rows, dtype=jnp.int32) for base in bases])
    first_index = jnp.sum(
        (seg_all[:, None, :] < seg_query[:, :, None]).astype(jnp.int32), axis=-1
    )
    positions = (query_index[None] - first_index).reshape(micro, slots, rows)
    positions = positions.transpose(1, 0, 2)
    freqs = THETA_BASE ** (-2.0 * jnp.arange(ROPE // 2, dtype=f32) / ROPE)
    angles = positions.astype(f32)[..., None] * freqs
    cos_rows, sin_rows = jnp.cos(angles), jnp.sin(angles)
    cos_own = cos_rows[0].reshape(own, ROPE // 2)
    sin_own = sin_rows[0].reshape(own, ROPE // 2)
    cos_lanes = jnp.concatenate([cos_rows] * 4, axis=-1)
    sin_lanes = jnp.concatenate([-sin_rows, sin_rows] * 2, axis=-1)
    tables = (seg_query[..., None], seg_key, cos_lanes, sin_lanes)

    close(*arrived, down_b, hid_b, grad_own, inputs16)
    while len(attn_z) < tp_size - 1:
        close(*attention_round())
    arrived = attention_round()
    down_a1 = send(line_x, swap_x, down_a, free=True)
    down_b2 = send(line_y, swap_y, down_b, free=True)
    factor_one = norm_scale(now(inputs))
    normed_own = (inputs * factor_one * gain_one).astype(bf16)
    latent_raw = dot(normed_own, w_latent)
    latent_part = latent_raw[:, :KVRANK]
    factor_latent = norm_scale(latent_part)
    latent_own = (latent_part * factor_latent * gain_kv).astype(bf16)
    rope_own = rotate(latent_raw[:, KVRANK:], cos_own, sin_own).astype(bf16)
    latent_pack = jnp.concatenate([latent_own, rope_own], axis=1).reshape(micro, rows, kv_cols)
    close(*arrived, down_a1, down_b2, latent_pack)
    latent_z, grad_z = [latent_pack], [grad_own]

    def latents_ahead():
        if len(latent_z) < tp_size:
            latent_z.append(send(line_z, step_z, latent_z[-1]))
        return latent_z[-1]

    def grads_ahead(count):
        for _ in range(count):
            grad_z.append(send(line_z, step_z, grad_z[-1]))

    arrived = attention_round()
    down_b1 = send(line_x, swap_x, down_b, free=True)
    down_a2 = send(line_y, swap_y, down_a, free=True)
    close(*arrived, down_b1, down_a2, latents_ahead())
    arrived = attention_round()
    down_b3 = send(line_x, swap_x, down_b2, free=True)
    down_a3 = send(line_y, swap_y, down_a1, free=True)
    close(*arrived, down_b3, down_a3, latents_ahead())
    while len(wanted) > 2:
        close(*attention_round(), latents_ahead())
    arrived = attention_round()
    normed_chip = normed_own
    if split:
        normed_chip = jnp.concatenate([normed_own, send(line_c, swap_core, normed_own)])
    half_tp = tp_size // 2
    latent_far = [send(line_c, swap_core, jnp.concatenate(latent_z[:half_tp]))]
    while len(latent_z) < tp_size:
        latents_ahead()
    close(*arrived, normed_chip, latent_far[0], latent_z[-1])
    attn_xy = [[held[j, k] for k in range(4)] for j in range(tp_size)]

    hid_a1, hid_b2 = send(line_x, swap_x, hid_a), send(line_y, swap_y, hid_b)
    grads_ahead(1)
    latent_far.append(send(line_c, swap_core, jnp.concatenate(latent_z[half_tp:])))
    q_cols, out_cols = q_width, q_width + out_width

    def core_row(k, half):
        def row(ref):
            at = ref[0] if half == 0 else 1 - ref[0]
            return (2 * k + at) * slice_rows

        return (slice_rows, row)

    def expand_row(k, half):
        def row(ref):
            at = ref[0] if half == 0 else 1 - ref[0]
            return (2 * (ref[1] ^ k) + at) * expand_rows

        return (expand_rows, row)

    moves = []
    for j in range(tp_size):
        for k in range(4):
            for half in range(2):
                source, top = 4 * j + k, half * slice_rows
                moves.append(
                    (source, top, slice_rows, 0, q_width, 0, core_row(k, half), j * q_width)
                )
                moves.append(
                    (source, top, slice_rows, q_cols, out_width, 1, core_row(k, half), j * out_width)
                )
                for i in range(blocks_kv):
                    moves.append(
                        (
                            source,
                            top + i % stack * expand_rows,
                            expand_rows,
                            out_cols + i // stack * LANES,
                            LANES,
                            2,
                            expand_row(k, half),
                            j * kv_width + i * LANES,
                        )
                    )
    w_query, w_out, w_expand = assemble(
        [piece for pieces in attn_xy for piece in pieces],
        moves,
        [(width, tp_size * q_width), (width, tp_size * out_width), (KVRANK, tp_size * kv_width)],
        now(shift),
    )
    q_lin = dot(normed_chip, w_query).reshape(slots, micro, rows, tp_size * q_width)
    latent_rows = [
        [(at * span + (place_z - j) % tp_size * rows) for j in range(tp_size)]
        for at in (core, 1 - core)
    ]
    latent_all, rope_keys = lay_out(
        jnp.stack([row for each in latent_rows for row in each]).astype(jnp.int32),
        latent_z + latent_far,
        micro,
        length,
    )
    latent_all = latent_all.reshape(micro * length, KVRANK)
    kv_all = dot(latent_all, w_expand, bf16).reshape(micro, length, tp_size * kv_width)
    close(hid_a1, hid_b2, grad_z[-1], q_lin, kv_all)

    hid_b1, hid_a2 = send(line_x, swap_x, hid_b), send(line_y, swap_y, hid_a)
    more = tp_size - 3
    grads_ahead(more)
    grad_far = [send(line_c, swap_core, piece, free=True) for piece in grad_z[:2]]
    mixed = attend(heads, tp_size, window, scale, now(place), q_lin, kv_all, rope_keys, *tables)
    mixed = mixed.reshape(slots * own, tp_size * out_width)
    close(hid_b1, hid_a2, grad_z[-1], *grad_far, mixed)

    hid_b3, hid_a3 = send(line_x, swap_x, hid_b2), send(line_y, swap_y, hid_a1)
    mixed = now(mixed)
    if split:
        mixed_out = dot_rt(mixed, w_out, bf16)
        middle = inputs + mixed_out[:own].astype(f32) + to_core(mixed_out[own:]).astype(f32)
    else:
        middle = inputs + dot_rt(mixed, w_out)
    factor_two = norm_scale(middle)
    normed_two = (middle * factor_two * gain_two).astype(bf16)
    norm_z = [normed_two, send(line_z, step_z, normed_two)]
    norm_far = [send(line_c, swap_core, normed_two)]
    for piece in grad_z[2:]:
        grad_far.append(send(line_c, swap_core, piece))
    close(hid_b3, hid_a3, norm_z[-1], *norm_far, *grad_far[2:])

    hidden_pieces = [hid_a, hid_a1, hid_a2, hid_a3, hid_b, hid_b1, hid_b2, hid_b3]
    down_pieces = [down_a, down_a1, down_a2, down_a3, down_b, down_b1, down_b2, down_b3]
    whole, back_parts, out_parts = [], [], []

    class Ring:
        def __init__(self, parts):
            self.parts, self.at, self.total, self.seen = parts, 0, None, {}

        def block(self, j):
            if j not in self.seen:
                own_part, far_part = self.parts[j]
                self.seen[j] = add16(own_part, send(line_c, swap_core, far_part))
            return self.seen[j]

        def step(self):
            if self.at == tp_size - 1:
                return ()
            self.at += 1
            total = self.block(self.at)
            if self.total is not None:
                total = add16(total, self.total)
            self.total = send(line_z, step_z, total)
            return (self.total,)

        def result(self):
            while self.step():
                pass
            return self.total.astype(f32) + self.block(0).astype(f32)

    back_ring, out_ring = Ring(back_parts), Ring(out_parts)
    for j in range(tp_size):
        arrived = []
        if len(norm_z) < tp_size:
            norm_z.append(send(line_z, step_z, norm_z[-1]))
            arrived.append(norm_z[-1])
        elif len(grad_z) < tp_size:
            grads_ahead(1 if j + 2 < tp_size else tp_size - len(grad_z))
            arrived.append(grad_z[-1])
        elif back_ring.at + 1 < len(back_parts):
            arrived += back_ring.step()
        if j + 1 < tp_size:
            norm_far.append(send(line_c, swap_core, norm_z[j + 1]))
            arrived.append(norm_far[-1])
        while len(grad_far) <= j:
            grad_far.append(send(line_c, swap_core, grad_z[len(grad_far)], free=True))
        made = feed(
            now(shift),
            j,
            tp_size,
            [norm_z[j], norm_far[j], grad_z[j], grad_far[j]],
            hidden_pieces,
            down_pieces,
            whole,
        )
        back_parts.append(made[:2])
        out_parts.append(made[2:4])
        whole = made[4:]
        close(*arrived, made[0])
    act_all, hidden_all, normed_all, grad_all = whole

    first, second = ((3, 0), (2, 0), (3, 1), (1, 1)), ((1, 0), (0, 0), (2, 1), (0, 1))
    arrived = back_ring.step()
    down_y, down_x, down_kept = weight_grad(
        now(shift), SENT_BLOCKS, slice_rows, grad_all, act_all
    )
    close(*arrived, down_y)

    down_y, down_x = send(line_y, swap_y, down_y), send(line_x, swap_x, down_x)
    arrived = []
    while back_ring.at < tp_size - 1:
        arrived += back_ring.step()
    back_ring.block(0)
    own3, own2, far3, far1 = weight_grad(
        now(shift), [(block,) for block in first], slice_rows, normed_all, hidden_all
    )
    close(*arrived, down_y, down_x, own3)

    own3, far3 = send(line_y, swap_y, own3), send(line_x, swap_x, far3)
    arrived = out_ring.step()
    grad_normed_two = back_ring.result()
    own1, own0, far2, far0 = weight_grad(
        now(shift), [(block,) for block in second], slice_rows, normed_all, hidden_all
    )
    close(*arrived, own3, far3, own1)

    own2, far1 = send(line_y, swap_y, own2), send(line_x, swap_x, far1)

    grad_mid_norm, grad_gain_two = norm_back(middle, factor_two, gain_two, now(grad_normed_two))
    grad_middle = grad_own.astype(f32) + grad_mid_norm
    grad_attn = grad_middle.astype(bf16)
    if split:
        grad_attn = jnp.concatenate([grad_attn, to_core(grad_attn)])
    grad_mixed = dot(grad_attn, w_out, bf16)
    out_blocks = [dot_lt(columns(grad_attn, k), mixed, bf16) for k in range(4)]
    close(own2, far1, grad_mixed, *out_blocks)

    def cut(value):
        middle_row = value.shape[0] // 2
        return value[:middle_row], value[middle_row:]

    def block_of(blocks, k, half):
        return cut(blocks[k])[half]

    def sent_of(blocks):
        return [jnp.concatenate([block_of(blocks, *at) for at in pair]) for pair in SENT_BLOCKS[:2]]

    def kept_of(blocks):
        return jnp.concatenate([block_of(blocks, *at) for at in SENT_BLOCKS[2]])

    def stage_one(over_y, over_x):
        return send(line_y, swap_y, over_y, free=True), send(line_x, swap_x, over_x, free=True)

    def stage_two(kept, sent):
        (top1, top0), (low2, low0) = (cut(each) for each in cut(kept))
        (top3, top2), (low3, low1) = cut(now(sent[0])), cut(now(sent[1]))
        top1 = send(line_x, swap_x, add16(top1, top3), free=True)
        low2 = send(line_y, swap_y, add16(low2, low3), free=True)
        return (top0, top2, top1), (low0, low1, low2)

    def stage_sum(tops, lows):
        return jnp.concatenate([add16(*tops), add16(*lows)])

    (down3, down2), (downf3, downf1) = cut(down_y), cut(down_x)
    (down1, down0), (downf2, downf0) = (cut(each) for each in cut(down_kept))
    over_x = send(
        line_x, swap_x, jnp.concatenate([add16(own1, now(own3)), add16(down1, down3)], axis=1)
    )
    over_y = send(
        line_y, swap_y, jnp.concatenate([add16(far2, now(far3)), add16(downf2, downf3)], axis=1)
    )
    arrived = out_ring.step()
    out_sent = stage_one(*sent_of(out_blocks))
    made = attend_back(
        heads,
        tp_size,
        window,
        scale,
        now(place),
        q_lin,
        kv_all,
        rope_keys,
        *tables,
        grad_mixed.reshape(slots, micro, rows, tp_size * out_width),
        normed_chip,
        latent_all,
        w_query,
        w_expand,
    )
    sums, (latent_mine, latent_others), parts = made[:6], made[6:8], made[8:]
    close(over_x, over_y, *arrived, *out_sent, sums[0])

    query_sent = stage_one(*sums[:2])
    latent_far = send(line_c, swap_core, latent_others)
    arrived = []
    while out_ring.at < tp_size - 1:
        arrived += out_ring.step()
    close(*query_sent, *arrived, latent_far)

    latent_sum = add16(latent_mine, now(latent_far))

    def latent_block(j):
        return lax.dynamic_slice_in_dim(latent_sum, (place_z - j) % tp_size * rows, rows, 1)

    latent_step = send(line_z, step_z, latent_block(1))
    out_sums = stage_two(kept_of(out_blocks), out_sent)
    grad_normed_one = parts[0].reshape(own, width).astype(f32)
    if split:
        far = send(line_c, swap_core, parts[1].reshape(own, width), free=True)
        grad_normed_one = grad_normed_one + far.astype(f32)
    close(latent_step, out_sums[0][2], out_sums[1][2])

    for j in range(2, tp_size - 1):
        latent_step = send(line_z, step_z, add16(now(latent_step), latent_block(j)))
    expand_sent = stage_one(*sums[3:5])
    close(latent_step, *expand_sent)

    latent_step = send(line_z, step_z, add16(now(latent_step), latent_block(tp_size - 1)))
    query_sums = stage_two(sums[2], query_sent)
    close(latent_step, query_sums[0][2], query_sums[1][2])

    expand_sums = stage_two(sums[5], expand_sent)
    grad_latent_own = (now(latent_step).astype(f32) + latent_block(0).astype(f32)).reshape(
        own, kv_cols
    )
    output = (middle + out_ring.result()).astype(bf16)
    hid_own = add16(own0, own2, over_x[:, : 2 * part])
    hid_other = add16(far0, far1, over_y[:, : 2 * part])
    down_own = add16(down0, down2, over_x[:, 2 * part :])
    down_other = add16(downf0, downf1, over_y[:, 2 * part :])
    hid_far, down_far = to_core(hid_other), to_core(down_other)
    grad_wgate, grad_wup, grad_wdown = (
        in_order(core, near, far, 1)[:, :hidden_here].astype(f32)
        for near, far in (
            (hid_own[:, :part], hid_far[:, :part]),
            (hid_own[:, part:], hid_far[:, part:]),
            (down_own, down_far),
        )
    )
    grad_wdown = grad_wdown.T

    def over_z(value, columns):
        return scatter_z(Line(), lambda j: value[:, columns * j : columns * (j + 1)])

    out_here = over_z(stage_sum(*out_sums), out_width)
    query_here = over_z(stage_sum(*query_sums), q_width)
    expand_here = over_z(stage_sum(*expand_sums), kv_width)
    out_cores = out_here.reshape(cores, slice_rows, out_width)
    query_cores = query_here.reshape(cores, slice_rows, q_width)
    expand_cores = expand_here.reshape(cores, expand_rows, kv_width)

    def finish(by_core):
        kept, given = mine(by_core, 0), to_core(others(by_core, 0))
        if split:
            return in_order(core, kept[:, None], given[:, None], 1).astype(f32)
        return (kept.astype(f32) + given.astype(f32))[:, None]

    grad_wout = finish(out_cores).reshape(slice_rows, -1).T
    grad_wexpand = finish(expand_cores).reshape(expand_rows, -1)
    grad_wquery = q_disorder(finish(query_cores))

    grad_latent_part, grad_gain_latent = norm_back(
        latent_part, factor_latent, gain_kv, grad_latent_own[:, :KVRANK]
    )
    grad_raw = jnp.concatenate(
        [grad_latent_part, rotate(grad_latent_own[:, KVRANK:], cos_own, -sin_own)], axis=-1
    ).astype(bf16)
    grad_normed_one = grad_normed_one + dot_rt(grad_raw, w_latent)
    grad_in_norm, grad_gain_one = norm_back(inputs, factor_one, gain_one, grad_normed_one)
    input_grad = (grad_middle + grad_in_norm).astype(bf16)

    core_rows = width // 4 // cores

    def core_features(values, at, size):
        return jnp.concatenate(
            [
                lax.dynamic_slice_in_dim(values, (cores * k + at) * size, size, values.ndim - 1)
                for k in range(4)
            ],
            axis=-1,
        )

    def gains_of(at):
        pieces = [
            core_features(grads, at, grads.shape[0] // (4 * cores)).reshape(4, tp_size, -1)
            for grads in (grad_gain_one, grad_gain_two, features(grad_gain_latent))
        ]
        return jnp.concatenate(pieces, axis=-1)

    def over_all(kept, given, rounded):
        kept = kept.astype(f32) + swap_core(given.astype(rounded)).astype(f32)
        sent = kept.astype(rounded)
        total = kept[0]
        for k in (1, 2, 3):
            gone = lax.ppermute(sent[k], "shard", [(i, i ^ k) for i in range(4)])
            total = total + gone.astype(f32)
        sent = total.astype(rounded)
        here = lax.dynamic_index_in_dim(total, place_z, 0, keepdims=False)
        for j in range(1, tp_size):
            gone = lax.dynamic_index_in_dim(sent, (place_z + j) % tp_size, 0, keepdims=False)
            gone = lax.ppermute(gone, "tp", [(i, (i + j) % tp_size) for i in range(tp_size)])
            here = here + gone.astype(f32)
        return here

    grad_wlatent = over_all(
        *(
            dot_lt(core_features(normed_own, at, core_rows), grad_raw).reshape(
                4, tp_size, small_rows, kv_cols
            )
            for at in (core, 1 - core)
        ),
        bf16,
    )
    gain_grads = over_all(gains_of(core), gains_of(1 - core), f32)
    like = (micro, 1, rows, width)
    return (
        features(output).reshape(like),
        features(input_grad).reshape(like),
        gain_grads[:gain_rows],
        grad_wquery,
        grad_wlatent,
        gain_grads[2 * gain_rows :],
        grad_wexpand,
        grad_wout,
        gain_grads[gain_rows : 2 * gain_rows],
        grad_wgate,
        grad_wup,
        grad_wdown,
    )


def solution(mesh):
    tokens = P(None, "shard", ("ctx", "tp"), None)
    everywhere = P(("shard", "ctx", "tp"))
    down_split = P(("shard", "ctx"), "tp")
    up_split = P("tp", ("shard", "ctx"))
    whole_rows = P(("shard", "ctx", "tp"), None)
    return jax.shard_map(
        shards,
        mesh=mesh,
        in_specs=(
            tokens,
            P(None, "shard", None),
            tokens,
            everywhere,
            down_split,
            whole_rows,
            everywhere,
            down_split,
            up_split,
            everywhere,
            down_split,
            down_split,
            up_split,
        ),
        out_specs=(
            tokens,
            tokens,
            everywhere,
            down_split,
            whole_rows,
            everywhere,
            down_split,
            up_split,
            everywhere,
            down_split,
            down_split,
            up_split,
        ),
        check_vma=False,
    )
```

```python
import functools

import jax
import jax.numpy as jnp
from jax import lax
from jax.experimental import pallas as pl
from jax.experimental.pallas import tpu as pltpu
from jax.sharding import PartitionSpec as P

NOPE = 128
ROPE = 64
VHEAD = 128
KVRANK = 512
DOC_MOST = 512
LANES = 128

EPSILON = 1e-06
THETA_BASE = 10000.0
NEG_FILL = -1e30

f32 = jnp.float32
bf16 = jnp.bfloat16


def norm_scale(values):
    return lax.rsqrt(jnp.mean(values * values, axis=-1, keepdims=True) + EPSILON)


def norm_back(values, factor, gain_vec, grad_out):
    scaled = grad_out * gain_vec
    grad_in = factor * scaled - values * factor**3 * jnp.mean(
        scaled * values, axis=-1, keepdims=True
    )
    return (grad_in, jnp.sum(grad_out * values * factor, axis=0))


def rotate(values, cos_table, sin_table):
    half_width = values.shape[-1] // 2
    first_half = values[..., :half_width]
    second_half = values[..., half_width:]
    return jnp.concatenate(
        [
            first_half * cos_table - second_half * sin_table,
            second_half * cos_table + first_half * sin_table,
        ],
        axis=-1,
    )


def dot(left, right, kind=f32):
    return jnp.dot(left, right, preferred_element_type=f32).astype(kind)


def dot_rt(left, right, kind=f32):
    return lax.dot_general(
        left, right, (((1,), (1,)), ((), ())), preferred_element_type=f32
    ).astype(kind)


def dot_lt(left, right, kind=f32):
    return lax.dot_general(
        left, right, (((0,), (0,)), ((), ())), preferred_element_type=f32
    ).astype(kind)


def add16(*terms):
    total = terms[0].astype(f32)
    for term in terms[1:]:
        total = total + term.astype(f32)
    return total.astype(bf16)


def after(value, *others):
    return lax.optimization_barrier((value, *others))[0]


class Line:
    def __init__(self):
        self.last = None

    def send(self, move, value, *needs, free=False):
        if self.last is not None and not free:
            needs = (*needs, self.last)
        if needs:
            value = after(value, *needs)
        self.last = move(value)
        return self.last


def swap_core(value):
    return lax.ppermute(value, "ctx", [(0, 1), (1, 0)])


def swap_x(value):
    return lax.ppermute(value, "shard", [(i, i ^ 1) for i in range(4)])


def swap_y(value):
    return lax.ppermute(value, "shard", [(i, i ^ 2) for i in range(4)])


def step_z(value):
    size = lax.axis_size("tp")
    return lax.ppermute(value, "tp", [(i, (i + 1) % size) for i in range(size)])


def scatter_z(line_z, block_of, last=bf16, add=add16):
    size = lax.axis_size("tp")
    total = block_of(1)
    for j in range(2, size):
        total = add(line_z.send(step_z, total), block_of(j))
    return (line_z.send(step_z, total).astype(f32) + block_of(0).astype(f32)).astype(last)


def in_order(core, mine, other, axis):
    return jnp.where(
        core == 0,
        jnp.concatenate([mine, other], axis=axis),
        jnp.concatenate([other, mine], axis=axis),
    )


def assemble(sources, moves, shapes, place):
    depth = min(32, len(moves))

    def kernel(place_ref, *refs):
        given, made, sems = refs[: len(sources)], refs[len(sources) : -1], refs[-1]
        flight = []
        for i, (src, row, rows, column, columns, dst, to_row, to_column) in enumerate(moves):
            if i >= depth:
                flight[i - depth].wait()
            if not isinstance(to_row, int):
                to_row = pl.multiple_of(to_row[1](place_ref), to_row[0])
            copy = pltpu.make_async_copy(
                given[src].at[pl.ds(row, rows), pl.ds(column, columns)],
                made[dst].at[pl.ds(to_row, rows), pl.ds(to_column, columns)],
                sems.at[i % depth],
            )
            copy.start()
            flight.append(copy)
        for copy in flight[-depth:]:
            copy.wait()

    return pl.pallas_call(
        kernel,
        out_shape=[jax.ShapeDtypeStruct(shape, bf16) for shape in shapes],
        grid_spec=pltpu.PrefetchScalarGridSpec(
            num_scalar_prefetch=1,
            in_specs=[pl.BlockSpec(memory_space=pl.ANY)] * len(sources),
            out_specs=[pl.BlockSpec(memory_space=pltpu.VMEM)] * len(shapes),
            scratch_shapes=[pltpu.SemaphoreType.DMA((depth,))],
        ),
        compiler_params=pltpu.CompilerParams(vmem_limit_bytes=48 << 20),
        cost_estimate=pl.CostEstimate(
            flops=0,
            transcendentals=0,
            bytes_accessed=4 * sum(a * b for a, b in shapes),
        ),
        name="assemble",
    )(place, *sources)


def lay_out_kernel(places, *refs):
    given, (latent, rope) = refs[:-2], refs[-2:]
    micro, rows = latent.shape[0], given[0].shape[1]
    pieces = [each[i : i + micro] for each in given for i in range(0, each.shape[0], micro)]
    for place, piece in zip(range(len(pieces)), pieces):
        at = pl.ds(pl.multiple_of(places[place], rows), rows)
        latent[:, at, :] = piece[:, :, :KVRANK]
        keys = piece[:, :, KVRANK:]
        rope[:, at, :] = jnp.concatenate([keys, keys], axis=-1)


def lay_out(places, pieces, micro, length):
    in_vmem = pl.BlockSpec(memory_space=pltpu.VMEM)
    return pl.pallas_call(
        lay_out_kernel,
        out_shape=[
            jax.ShapeDtypeStruct((micro, length, KVRANK), bf16),
            jax.ShapeDtypeStruct((micro, length, 2 * ROPE), bf16),
        ],
        grid_spec=pltpu.PrefetchScalarGridSpec(
            num_scalar_prefetch=1,
            in_specs=[in_vmem] * len(pieces),
            out_specs=[in_vmem] * 2,
        ),
        cost_estimate=pl.CostEstimate(
            flops=0, transcendentals=0, bytes_accessed=4 * micro * length * (KVRANK + 2 * ROPE)
        ),
        name="lay_out",
    )(places, *pieces)


def begin_kernel(place, hidden, gain, w_latent, gain_kv, cos_ref, sin_ref, normed, raw, packed, scale_one, scale_kv):
    values = hidden[...].astype(f32)
    factor = norm_scale(values)
    scale_one[...] = factor
    normed[...] = (values * factor * gain[...]).astype(bf16)
    latent = dot(normed[...], w_latent[...])
    own = latent[:, :KVRANK]
    raw[...] = own
    factor = norm_scale(own)
    scale_kv[...] = factor
    ropes = latent[:, KVRANK:]
    ropes = jnp.concatenate([ropes, ropes], axis=1)
    lane = lax.broadcasted_iota(jnp.int32, ropes.shape, 1)
    ropes = ropes * cos_ref[...] + swap_halves(ropes, lane) * sin_ref[...]
    packed[:, :KVRANK] = (own * factor * gain_kv[...]).astype(bf16)
    packed[:, KVRANK:] = ropes[:, :ROPE].astype(bf16)


def in_one(kernel, name, outs, place, *operands, scratch=()):
    in_vmem = pl.BlockSpec(memory_space=pltpu.VMEM)
    moved = sum(x.size * x.dtype.itemsize for x in operands)
    return pl.pallas_call(
        kernel,
        out_shape=[jax.ShapeDtypeStruct(shape, kind) for shape, kind in outs],
        grid_spec=pltpu.PrefetchScalarGridSpec(
            num_scalar_prefetch=1,
            in_specs=[in_vmem] * len(operands),
            out_specs=[in_vmem] * len(outs),
            scratch_shapes=[pltpu.VMEM(shape, kind) for shape, kind in scratch],
        ),
        compiler_params=pltpu.CompilerParams(vmem_limit_bytes=58 << 20),
        cost_estimate=pl.CostEstimate(flops=0, transcendentals=0, bytes_accessed=moved),
        name=name,
    )(place, *operands)


def finish_kernel(
    place,
    latent_far,
    latent_here,
    raw,
    scale_kv,
    gain_kv,
    cos_ref,
    sin_ref,
    own_part,
    far_part,
    w_latent,
    hidden,
    scale_one,
    gain,
    grad_middle,
    normed,
    grad_gain_two,
    input_grad,
    w_mine,
    w_other,
    grad_gain,
    grad_gain_kv,
    grad_w,
):
    grads = latent_far[...].astype(f32) + latent_here[...].astype(f32)
    grad_part, total = norm_back(raw[...], scale_kv[...], gain_kv[...], grads[:, :KVRANK])
    grad_gain_kv[...] = total[None]
    ropes = grads[:, KVRANK:]
    ropes = jnp.concatenate([ropes, ropes], axis=1)
    lane = lax.broadcasted_iota(jnp.int32, ropes.shape, 1)
    ropes = ropes * cos_ref[...] - swap_halves(ropes, lane) * sin_ref[...]
    grad_raw = jnp.concatenate([grad_part, ropes[:, :ROPE]], axis=1).astype(bf16)
    grad_w[...] = dot_lt(normed[...], grad_raw, bf16)
    grad_normed = dot_rt(grad_raw, w_latent[...]) + own_part[...].astype(f32)
    if far_part is not None:
        grad_normed = grad_normed + far_part[...].astype(f32)
    grad_in, total = norm_back(
        hidden[...].astype(f32), scale_one[...], gain[...], grad_normed
    )
    grad_gain[...] = total[None]
    input_grad[...] = (grad_middle[...] + grad_in).astype(bf16)
    size, kv_size = grad_w.shape[0] // 8, KVRANK // 8
    for out, half in ((w_mine, place[0]), (w_other, 1 - place[0])):
        for k in range(4):
            at = pl.multiple_of((2 * k + half) * size, size)
            top = k * (size + 16)
            out[top : top + size, :] = grad_w[pl.ds(at, size), :]
            both = pl.multiple_of((place[1] ^ k) * 2 * kv_size, 2 * kv_size)
            kv_row = jnp.broadcast_to(grad_gain_kv[:, pl.ds(both, 2 * kv_size)], (16, 2 * kv_size))
            kv_row = jnp.where(half == 0, kv_row, pltpu.roll(kv_row, kv_size, 1))[:, :kv_size]
            row = [
                jnp.broadcast_to(gains[:, pl.ds(at, size)], (16, size))
                for gains in (grad_gain, grad_gain_two)
            ]
            out[top + size : top + size + 16, :] = jnp.concatenate([*row, kv_row], axis=1).astype(
                bf16
            )


SENT_BLOCKS = (((3, 0), (2, 0)), ((3, 1), (1, 1)), ((1, 0), (0, 0), (2, 1), (0, 1)))


def swap_halves(values, lane):
    return jnp.where(
        lane % ROPE < ROPE // 2,
        pltpu.roll(values, LANES - ROPE // 2, 1),
        pltpu.roll(values, ROPE // 2, 1),
    )


def window_mask(start, base, rows, width, seg_query, seg_key):
    query_index = base + lax.broadcasted_iota(jnp.int32, (rows, width), 0)
    key_index = start + lax.broadcasted_iota(jnp.int32, (rows, width), 1)
    same_doc = (seg_query == seg_key) & (key_index <= query_index) & (seg_key != 0)
    return same_doc | (key_index == query_index)


def head_operands(q_ref, kv_ref, rope_key, slot, window, head, heads, cos_table, sin_table):
    rows = q_ref.shape[2]
    lane = lax.broadcasted_iota(jnp.int32, (rows, LANES), 1)
    first = heads * NOPE + head // 2 * LANES
    rope_lin = q_ref[slot, 0, :, first : first + LANES]
    turned = rope_lin * cos_table + swap_halves(rope_lin, lane) * sin_table
    turned = jnp.where(lane // ROPE == head % 2, turned, 0.0)
    plain = q_ref[slot, 0, :, head * NOPE : (head + 1) * NOPE]
    query = jnp.concatenate([plain, turned], axis=1).astype(bf16)
    at = head * (NOPE + VHEAD)
    key = jnp.concatenate([kv_ref[0, window, at : at + NOPE], rope_key], axis=1)
    value = kv_ref[0, window, at + NOPE : at + NOPE + VHEAD]
    return query, key, value


def attend_kernel(
    heads, width, scale, place, q_ref, kv_ref, kr_ref, segq_ref, segk_ref, cos_ref, sin_ref, o_ref
):
    slots, rows = q_ref.shape[0], q_ref.shape[2]
    for slot in range(slots):
        start = pl.multiple_of(place[slot, 0], rows)
        window = pl.ds(start, width)
        allowed = window_mask(
            start,
            place[slot, 1],
            rows,
            width,
            segq_ref[0, slot * rows : (slot + 1) * rows, :],
            segk_ref[0, slot : slot + 1, :],
        )
        rope_key = kr_ref[0, window, :]
        for head in range(heads):
            query, key, value = head_operands(
                q_ref, kv_ref, rope_key, slot, window, head, heads, cos_ref[slot, 0], sin_ref[slot, 0]
            )
            scores = jnp.where(allowed, dot_rt(query, key) * scale, NEG_FILL)
            expd = jnp.exp(scores - jnp.max(scores, axis=-1, keepdims=True))
            probs = expd / jnp.sum(expd, axis=-1, keepdims=True)
            o_ref[slot, 0, :, head * VHEAD : (head + 1) * VHEAD] = dot(
                probs.astype(bf16), value, bf16
            )


def attend_back_kernel(
    heads,
    width,
    scale,
    groups,
    place,
    q_ref,
    kv_ref,
    kr_ref,
    segq_ref,
    segk_ref,
    cos_ref,
    sin_ref,
    do_ref,
    norm_ref,
    latent_ref,
    wq_ref,
    wkv_ref,
    *refs,
):
    slots, rows = q_ref.shape[0], q_ref.shape[2]
    q_width, kv_width = q_ref.shape[3], kv_ref.shape[2]
    query_outs, expand_outs, latent_outs = refs[:3], refs[3:6], refs[6:8]
    parts, (total, rope_total, kv_grads, q_grads, expand_grads) = refs[8:-5], refs[-5:]
    group, m = pl.program_id(0), pl.program_id(1)
    micro = pl.num_programs(1)
    lane = lax.broadcasted_iota(jnp.int32, (rows, LANES), 1)
    q_first = pl.multiple_of(group * q_width, LANES)
    kv_first = pl.multiple_of(group * kv_width, LANES)

    def q_rows(slot):
        return pl.ds(pl.multiple_of((slot * micro + m) * rows, rows), rows)

    @pl.when(group == 0)
    def _():
        rope_total[m] = jnp.zeros(rope_total.shape[1:], f32)

    total[...] = jnp.zeros_like(total)
    for slot in range(slots):
        start = pl.multiple_of(place[slot, 0], rows)
        window = pl.ds(start, width)
        allowed = window_mask(
            start,
            place[slot, 1],
            rows,
            width,
            segq_ref[0, slot * rows : (slot + 1) * rows, :],
            segk_ref[0, slot : slot + 1, :],
        )
        rope_key = kr_ref[0, window, :]
        rope_grads = None
        for head in range(heads):
            query, key, value = head_operands(
                q_ref, kv_ref, rope_key, slot, window, head, heads, cos_ref[slot, 0], sin_ref[slot, 0]
            )
            grad_mixed = do_ref[slot, 0, :, head * VHEAD : (head + 1) * VHEAD]
            scores = jnp.where(allowed, dot_rt(query, key) * scale, NEG_FILL)
            expd = jnp.exp(scores - jnp.max(scores, axis=-1, keepdims=True))
            probs = expd / jnp.sum(expd, axis=-1, keepdims=True)
            grad_probs = dot_rt(grad_mixed, value)
            inner = jnp.sum(probs * grad_probs, axis=-1, keepdims=True)
            grad_scores = (scale * probs * (grad_probs - inner)).astype(bf16)
            grad_query = dot(grad_scores, key)
            grad_key = dot_lt(grad_scores, query)
            at = head * (NOPE + VHEAD)
            total[window, at : at + NOPE] += grad_key[:, :NOPE]
            rope_total[m, window, :] += grad_key[:, NOPE:]
            total[window, at + NOPE : at + NOPE + VHEAD] += dot_lt(probs.astype(bf16), grad_mixed)
            q_grads[q_rows(slot), pl.ds(q_first + head * NOPE, NOPE)] = grad_query[:, :NOPE].astype(
                bf16
            )
            if head % 2 == 0:
                rope_grads = jnp.where(lane < ROPE, grad_query[:, NOPE:], 0.0)
            else:
                rope_grads = jnp.where(lane < ROPE, rope_grads, grad_query[:, NOPE:])
            if head % 2 == 1 or head == heads - 1:
                turned = rope_grads * cos_ref[slot, 0] - swap_halves(rope_grads, lane) * sin_ref[slot, 0]
                first = q_first + heads * NOPE + head // 2 * LANES
                q_grads[q_rows(slot), pl.ds(first, LANES)] = turned.astype(bf16)
    kv_grads[m, :, pl.ds(kv_first, kv_width)] = total[...].astype(bf16)

    @pl.when(m == micro - 1)
    def _():
        grads = dot_lt(norm_ref[...], q_grads[:, pl.ds(q_first, q_width)], bf16)
        size = grads.shape[0] // 8
        for out, blocks in zip(query_outs, SENT_BLOCKS):
            for i, (k, half) in enumerate(blocks):
                out[i * size : (i + 1) * size, :] = grads[(2 * k + half) * size :][:size]
        back = kv_grads[:, :, pl.ds(kv_first, kv_width)]
        expand_grads[...] = dot_lt(
            latent_ref[...], back.reshape(latent_ref.shape[0], kv_width), bf16
        )
        size = expand_grads.shape[0] // 8
        shard = place[slots, 0]
        for out, blocks in zip(expand_outs, SENT_BLOCKS):
            for i, (k, half) in enumerate(blocks):
                at = pl.multiple_of((2 * (shard ^ k) + half) * size, size)
                out[i * size : (i + 1) * size, :] = expand_grads[pl.ds(at, size), :]

    @pl.when(group == groups - 1)
    def _():
        span = latent_outs[0].shape[1]
        for out, half in zip(latent_outs, (place[slots, 1], 1 - place[slots, 1])):
            at = pl.ds(pl.multiple_of(half * span, span), span)
            out[0, :, :KVRANK] = dot_rt(kv_grads[m, at, :], wkv_ref[...], bf16)
            ropes = rope_total[m, at, :]
            ropes = ropes + pltpu.roll(ropes, ROPE, 1)
            out[0, :, KVRANK:] = ropes[:, :ROPE].astype(bf16)
        for slot, out in enumerate(parts):
            out[0] = dot_rt(q_grads[q_rows(slot), :], wq_ref[...], bf16)


def attention_specs(heads, slots, rows, length, width, q_width, order):
    def at(*index):
        return lambda a, b, place: tuple(
            {"m": (a, b)[order], "j": (a, b)[1 - order]}.get(i, i) for i in index
        )

    return [
        pl.BlockSpec((slots, 1, rows, q_width), at(0, "m", 0, "j")),
        pl.BlockSpec((1, length, heads * (NOPE + VHEAD)), at("m", 0, "j")),
        pl.BlockSpec((1, length, LANES), at("m", 0, 0)),
        pl.BlockSpec((1, slots * rows, 1), at("m", 0, 0)),
        pl.BlockSpec((1, slots, width), at("m", 0, 0)),
        pl.BlockSpec((slots, 1, rows, LANES), at(0, "m", 0, 0)),
        pl.BlockSpec((slots, 1, rows, LANES), at(0, "m", 0, 0)),
    ]


def attend(heads, groups, width, scale, place, q_lin, kv, rope_keys, seg_query, seg_key, cos, sin):
    slots, micro, rows, q_all = q_lin.shape
    length = kv.shape[1]
    return pl.pallas_call(
        functools.partial(attend_kernel, heads, width, scale),
        out_shape=jax.ShapeDtypeStruct((slots, micro, rows, groups * heads * VHEAD), bf16),
        grid_spec=pltpu.PrefetchScalarGridSpec(
            num_scalar_prefetch=1,
            grid=(micro, groups),
            in_specs=attention_specs(heads, slots, rows, length, width, q_all // groups, 0),
            out_specs=pl.BlockSpec(
                (slots, 1, rows, heads * VHEAD), lambda m, j, place: (0, m, 0, j)
            ),
        ),
        compiler_params=pltpu.CompilerParams(
            dimension_semantics=("arbitrary", "arbitrary"), vmem_limit_bytes=40 << 20
        ),
        cost_estimate=pl.CostEstimate(
            flops=2 * slots * rows * micro * groups * heads * width * 384,
            transcendentals=slots * rows * micro * groups * heads * width,
            bytes_accessed=2 * kv.size + 6 * q_lin.size,
        ),
        name="attend",
    )(place, q_lin, kv, rope_keys, seg_query, seg_key, cos, sin)


def attend_back(
    heads,
    groups,
    width,
    scale,
    place,
    q_lin,
    kv,
    rope_keys,
    seg_query,
    seg_key,
    cos,
    sin,
    d_o,
    normed,
    latents,
    w_query,
    w_expand,
):
    slots, micro, rows, q_all = q_lin.shape
    length = kv.shape[1]
    tokens, model = normed.shape
    q_width, kv_width = q_all // groups, kv.shape[2] // groups
    latent_width = KVRANK + ROPE

    def last(j, m, place):
        return (jnp.where(j == groups - 1, m, 0), 0, 0)

    def whole(shape):
        return pl.BlockSpec(shape, lambda j, m, place: (0, 0), pipeline_mode=pl.Buffered(1))

    def sent(total, columns):
        return [
            (jax.ShapeDtypeStruct((n * total // 8, columns * groups), bf16), n * total // 8, columns)
            for n in (2, 2, 4)
        ]

    grads = sent(model, q_width) + sent(KVRANK, kv_width)
    return pl.pallas_call(
        functools.partial(attend_back_kernel, heads, width, scale, groups),
        out_shape=[
            *(shape for shape, _, _ in grads),
            *[jax.ShapeDtypeStruct((micro, length // 2, latent_width), bf16)] * 2,
            *[jax.ShapeDtypeStruct((micro, rows, model), bf16)] * slots,
        ],
        grid_spec=pltpu.PrefetchScalarGridSpec(
            num_scalar_prefetch=1,
            grid=(groups, micro),
            in_specs=attention_specs(heads, slots, rows, length, width, q_width, 1)
            + [
                pl.BlockSpec((slots, 1, rows, heads * VHEAD), lambda j, m, place: (0, m, 0, j)),
                whole(normed.shape),
                whole(latents.shape),
                whole(w_query.shape),
                whole(w_expand.shape),
            ],
            out_specs=[
                *(
                    pl.BlockSpec((height, columns), lambda j, m, place: (0, j))
                    for _, height, columns in grads
                ),
                *[pl.BlockSpec((1, length // 2, latent_width), last)] * 2,
                *[pl.BlockSpec((1, rows, model), last)] * slots,
            ],
            scratch_shapes=[
                pltpu.VMEM((length, kv_width), f32),
                pltpu.VMEM((micro, length, LANES), f32),
                pltpu.VMEM(kv.shape, bf16),
                pltpu.VMEM((tokens, q_all), bf16),
                pltpu.VMEM((KVRANK, kv_width), bf16),
            ],
        ),
        compiler_params=pltpu.CompilerParams(
            dimension_semantics=("arbitrary", "arbitrary"), vmem_limit_bytes=60 << 20
        ),
        cost_estimate=pl.CostEstimate(
            flops=2 * slots * rows * micro * groups * heads * width * 1024
            + 4 * tokens * model * q_all
            + 4 * micro * length * KVRANK * kv.shape[2],
            transcendentals=slots * rows * micro * groups * heads * width,
            bytes_accessed=2 * kv.size + 4 * q_lin.size + 8 * w_query.size,
        ),
        name="attend_back",
    )(
        place,
        q_lin,
        kv,
        rope_keys,
        seg_query,
        seg_key,
        cos,
        sin,
        d_o,
        normed,
        latents,
        w_query,
        w_expand,
    )


def spans(total, step):
    return [(at, min(step, total - at)) for at in range(0, total, step)]


def feed_kernel(part, rows, offset, place, *refs):
    given, refs = refs[:20], refs[20:]
    refs = refs[4:] if offset else refs
    back_own, back_other, out_own, out_other, act_all, hid_all, norm_all, grad_all = refs[:8]
    w_hid, w_down, norm, grad, d_act, act, hid, sems = refs[8:]
    norm_own, norm_other, grad_own, grad_other = given[:4]
    slice_rows = given[4].shape[0]

    def at_core(i):
        core = place[0] if i < 4 else 1 - place[0]
        return pl.ds(pl.multiple_of((2 * (i % 4) + core) * slice_rows, slice_rows), slice_rows)

    early = [
        pltpu.make_async_copy(grad_own, grad.at[pl.ds(0, rows)], sems.at[0]),
        pltpu.make_async_copy(grad_other, grad.at[pl.ds(rows, rows)], sems.at[1]),
    ] + [
        pltpu.make_async_copy(given[12 + i], w_down.at[at_core(i)], sems.at[2 + i])
        for i in range(8)
    ]
    later = [
        pltpu.make_async_copy(norm_own, norm.at[pl.ds(0, rows)], sems.at[10]),
        pltpu.make_async_copy(norm_other, norm.at[pl.ds(rows, rows)], sems.at[11]),
    ] + [
        pltpu.make_async_copy(given[4 + i], w_hid.at[at_core(i)], sems.at[12 + i])
        for i in range(8)
    ]
    for copy in early + later:
        copy.start()
    for copy in early:
        copy.wait()

    def for_chunks(total, body):
        whole = total // 256

        def step(i, carry):
            body(pl.multiple_of(i * 256, 256), 256)
            return carry

        lax.fori_loop(0, whole, step, 0)
        if total % 256:
            body(whole * 256, total % 256)

    def act_back(start, size):
        d_act[:, pl.ds(start, size)] = dot(grad[...], w_down[:, pl.ds(start, size)])

    for_chunks(part, act_back)
    for copy in later:
        copy.wait()

    def forward(start, size):
        gate = dot(norm[...], w_hid[:, pl.ds(start, size)])
        up_at = start + part
        if not isinstance(start, int):
            up_at = pl.multiple_of(up_at, LANES)
        up = dot(norm[...], w_hid[:, pl.ds(up_at, size)])
        back = d_act[:, pl.ds(start, size)]
        sigma = jax.nn.sigmoid(gate)
        swish = gate * sigma
        act[:, pl.ds(start, size)] = (swish * up).astype(bf16)
        hid[:, pl.ds(start, size)] = (
            back * up * sigma * (1.0 + gate * (1.0 - sigma))
        ).astype(bf16)
        hid[:, pl.ds(up_at, size)] = (back * swish).astype(bf16)

    for_chunks(part, forward)
    here = pl.ds(offset * 2 * rows, 2 * rows)
    saves = [
        pltpu.make_async_copy(source, target.at[here], sems.at[20 + i])
        for i, (source, target) in enumerate(
            ((act, act_all), (hid, hid_all), (norm, norm_all), (grad, grad_all))
        )
    ]
    for copy in saves:
        copy.start()

    def backward(start, size):
        back = dot_rt(hid[...], w_hid[pl.ds(start, size), :], bf16)
        back_own[:, pl.ds(start, size)] = back[:rows]
        back_other[:, pl.ds(start, size)] = back[rows:]
        out = dot_rt(act[...], w_down[pl.ds(start, size), :], bf16)
        out_own[:, pl.ds(start, size)] = out[:rows]
        out_other[:, pl.ds(start, size)] = out[rows:]

    for_chunks(w_hid.shape[0], backward)
    for copy in saves:
        copy.wait()


def feed(place, offset, blocks, tokens, hidden_pieces, down_pieces, whole):
    rows, width = tokens[0].shape
    part = down_pieces[0].shape[1]
    anywhere = pl.BlockSpec(memory_space=pl.ANY)
    in_vmem = pl.BlockSpec(memory_space=pltpu.VMEM)
    total = 2 * rows * blocks
    operands = [*tokens, *hidden_pieces, *down_pieces, *whole]
    return pl.pallas_call(
        functools.partial(feed_kernel, part, rows, offset),
        out_shape=[jax.ShapeDtypeStruct((rows, width), bf16)] * 4
        + [
            jax.ShapeDtypeStruct((total, columns), bf16)
            for columns in (part, 2 * part, width, width)
        ],
        grid_spec=pltpu.PrefetchScalarGridSpec(
            num_scalar_prefetch=1,
            in_specs=[anywhere] * len(operands),
            out_specs=[in_vmem] * 4 + [anywhere] * 4,
            scratch_shapes=[
                pltpu.VMEM((width, 2 * part), bf16),
                pltpu.VMEM((width, part), bf16),
                pltpu.VMEM((2 * rows, width), bf16),
                pltpu.VMEM((2 * rows, width), bf16),
                pltpu.VMEM((2 * rows, part), f32),
                pltpu.VMEM((2 * rows, part), bf16),
                pltpu.VMEM((2 * rows, 2 * part), bf16),
                pltpu.SemaphoreType.DMA((24,)),
            ],
        ),
        input_output_aliases={21 + i: 4 + i for i in range(len(whole))},
        compiler_params=pltpu.CompilerParams(vmem_limit_bytes=58 << 20),
        cost_estimate=pl.CostEstimate(
            flops=2 * 2 * rows * width * part * 6,
            transcendentals=2 * rows * part,
            bytes_accessed=2 * (3 * width * part + 2 * rows * (6 * width + 3 * part)),
        ),
        name="feed",
    )(place, *operands)


def pack_kernel(part, place, gate, up, down, hid_mine, hid_other, down_mine, down_other):
    hidden_here, slice_rows = gate.shape
    rest = hidden_here - part

    def put(at, low, high, value):
        low[:, at : at + part] = value[:, :part]
        if rest < part:
            edge = rest // LANES * LANES
            high[:, at + edge : at + part] = jnp.zeros((slice_rows, part - edge), bf16)
        high[:, at : at + rest] = value[:, part:]

    def write(hid_low, hid_high, down_low, down_high):
        put(0, hid_low, hid_high, gate[...].T)
        put(part, hid_low, hid_high, up[...].T)
        put(0, down_low, down_high, down[...].T)

    @pl.when(place[0] == 0)
    def _():
        write(hid_mine, hid_other, down_mine, down_other)

    @pl.when(place[0] != 0)
    def _():
        write(hid_other, hid_mine, down_other, down_mine)


def pack(place, part, gate, up, down):
    slice_rows = gate.shape[1]
    in_vmem = pl.BlockSpec(memory_space=pltpu.VMEM)
    return pl.pallas_call(
        functools.partial(pack_kernel, part),
        out_shape=[jax.ShapeDtypeStruct((slice_rows, n * part), bf16) for n in (2, 2, 1, 1)],
        grid_spec=pltpu.PrefetchScalarGridSpec(
            num_scalar_prefetch=1, in_specs=[in_vmem] * 3, out_specs=[in_vmem] * 4
        ),
        compiler_params=pltpu.CompilerParams(vmem_limit_bytes=48 << 20),
        cost_estimate=pl.CostEstimate(
            flops=0, transcendentals=0, bytes_accessed=24 * slice_rows * part
        ),
        name="pack",
    )(place, gate, up, down)


def spread_kernel(place, hid_own, hid_far, down_own, down_far, *outs):
    part = down_own.shape[1]
    rest = outs[0].shape[0] - part

    def write(low, high):
        for out, i in zip(outs, (0, 1, 0)):
            hid, down = (low[0], low[1]) if out is not outs[2] else (low[1], low[1])
            out[:part, :] = hid[:, i * part : (i + 1) * part].T.astype(f32)
            hid = high[0] if out is not outs[2] else high[1]
            out[part:, :] = hid[:, i * part : (i + 1) * part].T.astype(f32)[:rest]

    @pl.when(place[0] == 0)
    def _():
        write((hid_own, down_own), (hid_far, down_far))

    @pl.when(place[0] != 0)
    def _():
        write((hid_far, down_far), (hid_own, down_own))


def spread(place, hidden_here, *halves):
    slice_rows = halves[0].shape[0]
    in_vmem = pl.BlockSpec(memory_space=pltpu.VMEM)
    return pl.pallas_call(
        spread_kernel,
        out_shape=[jax.ShapeDtypeStruct((hidden_here, slice_rows), f32)] * 3,
        grid_spec=pltpu.PrefetchScalarGridSpec(
            num_scalar_prefetch=1, in_specs=[in_vmem] * 4, out_specs=[in_vmem] * 3
        ),
        compiler_params=pltpu.CompilerParams(vmem_limit_bytes=48 << 20),
        cost_estimate=pl.CostEstimate(
            flops=0, transcendentals=0, bytes_accessed=20 * slice_rows * hidden_here
        ),
        name="spread",
    )(place, *halves)


def weight_grad_kernel(packs, place, left, right_ref, *refs):
    packed, (turned, buffer, sems) = refs[:-3], refs[-3:]
    slice_rows, tokens = packed[0].shape[0] // len(packs[0]), turned.shape[1]
    blocks = [block for pack in packs for block in pack]
    outs = [
        out.at[pl.ds(i * slice_rows, slice_rows)]
        for out, pack in zip(packed, packs)
        for i in range(len(pack))
    ]

    def fetch(i):
        k, half = blocks[i]
        core = place[0] if half == 0 else 1 - place[0]
        start = pl.multiple_of((2 * k + core) * slice_rows, slice_rows)
        return pltpu.make_async_copy(
            left.at[:, pl.ds(start, slice_rows)], buffer.at[i % 2], sems.at[i % 2]
        )

    @pl.when(pl.program_id(0) == 0)
    def _():
        fetch(0).start()
        for i in range(len(outs)):
            fetch(i).wait()
            if i + 1 < len(outs):
                fetch(i + 1).start()

            def turn(j, carry, i=i):
                at = pl.ds(pl.multiple_of(j * 256, 256), 256)
                turned[pl.ds(i * slice_rows, slice_rows), at] = buffer[i % 2, at, :].T
                return carry

            lax.fori_loop(0, tokens // 256, turn, 0)

    for half in range(0, len(outs), 4):
        rows = pl.ds(half * slice_rows, 4 * slice_rows)
        grads = dot(turned[rows, :], right_ref[...], bf16)
        for i in range(4):
            outs[half + i][...] = grads[i * slice_rows : (i + 1) * slice_rows]


def weight_grad(place, packs, slice_rows, left, right):
    tokens, columns = right.shape
    count = sum(len(pack) for pack in packs)
    heights = [len(pack) * slice_rows for pack in packs]
    return pl.pallas_call(
        functools.partial(weight_grad_kernel, packs),
        out_shape=[jax.ShapeDtypeStruct((height, columns), bf16) for height in heights],
        grid_spec=pltpu.PrefetchScalarGridSpec(
            num_scalar_prefetch=1,
            grid=(-(-columns // 256),),
            in_specs=[
                pl.BlockSpec(memory_space=pl.ANY),
                pl.BlockSpec((tokens, 256), lambda n, place: (0, n)),
            ],
            out_specs=[pl.BlockSpec((height, 256), lambda n, place: (0, n)) for height in heights],
            scratch_shapes=[
                pltpu.VMEM((count * slice_rows, tokens), bf16),
                pltpu.VMEM((2, tokens, slice_rows), bf16),
                pltpu.SemaphoreType.DMA((2,)),
            ],
        ),
        compiler_params=pltpu.CompilerParams(
            dimension_semantics=("arbitrary",), vmem_limit_bytes=48 << 20
        ),
        cost_estimate=pl.CostEstimate(
            flops=2 * tokens * columns * count * slice_rows,
            transcendentals=0,
            bytes_accessed=2 * (tokens * columns + count * slice_rows * (tokens + columns)),
        ),
        name="weight_grad",
    )(place, left, right)


def shards(
    hidden,
    segments,
    cotangent,
    attn_gain,
    q_weight,
    latent_weight,
    latent_gain,
    expand_weight,
    out_weight,
    mlp_gain,
    gate_weight,
    up_weight,
    down_weight,
):
    micro, _, rows, width = hidden.shape
    length = segments.shape[2]
    tp_size, cores = lax.axis_size("tp"), lax.axis_size("ctx")
    shard, core, place_z = lax.axis_index("shard"), lax.axis_index("ctx"), lax.axis_index("tp")
    span = rows * tp_size
    own = micro * rows
    block = width // 4
    slice_rows = q_weight.shape[0]
    heads_here = q_weight.shape[1] // (NOPE + ROPE)
    split = heads_here % cores == 0
    heads = heads_here // cores if split else heads_here
    slots = cores if split else 1
    rope_width = -(-heads * ROPE // LANES) * LANES
    q_width = heads * NOPE + rope_width
    scale = (NOPE + ROPE) ** (-0.5)
    hidden_here = gate_weight.shape[1]
    part = -(-hidden_here // (cores * LANES)) * LANES
    window = min(length, -(-(DOC_MOST + rows) // LANES) * LANES)

    line_x, line_y, line_z, line_c = Line(), Line(), Line(), Line()

    def features(values):
        size = values.shape[-1] // 4
        return jnp.concatenate(
            [
                lax.dynamic_slice_in_dim(values, (shard ^ k) * size, size, values.ndim - 1)
                for k in range(4)
            ],
            axis=-1,
        )

    def columns(values, k):
        return values[:, block * k : block * (k + 1)]

    def mine(values, axis):
        return lax.dynamic_index_in_dim(values, core, axis, keepdims=False)

    def others(values, axis):
        return lax.dynamic_index_in_dim(values, 1 - core, axis, keepdims=False)

    def to_core(value):
        return line_c.send(swap_core, value)

    small_rows = latent_weight.shape[0]
    gain_rows, latent_gains = attn_gain.shape[0], latent_gain.shape[0]
    kv_cols = latent_weight.shape[1]
    gains_row = jnp.concatenate([attn_gain, mlp_gain, latent_gain])
    gains_row = jnp.pad(gains_row, (0, kv_cols - gains_row.shape[0]))
    small = jnp.concatenate([latent_weight, jnp.pad(gains_row[None], ((0, 15), (0, 0)))])
    small_all = lax.all_gather(small, ("shard", "ctx", "tp"), axis=0)
    devices = 4 * cores * tp_size

    def own_first(values):
        size = values.shape[0] // 4
        return jnp.concatenate(
            [lax.dynamic_slice_in_dim(values, (shard ^ k) * size, size, 0) for k in range(4)]
        )

    w_latent = own_first(small_all[:, :small_rows].reshape(width, kv_cols))
    gain_all = small_all[:, small_rows].astype(f32)
    gain_one = own_first(gain_all[:, :gain_rows].reshape(width))
    gain_two = own_first(gain_all[:, gain_rows : 2 * gain_rows].reshape(width))
    gain_kv = gain_all[:, 2 * gain_rows : 2 * gain_rows + latent_gains].reshape(KVRANK)
    del devices

    def q_order(values):
        groups = values.shape[1] // (heads * (NOPE + ROPE))
        by_head = values.reshape(values.shape[0], groups, heads, NOPE + ROPE)
        plain = by_head[..., :NOPE].reshape(values.shape[0], groups, heads * NOPE)
        rope = by_head[..., NOPE:].reshape(values.shape[0], groups, heads * ROPE)
        rope = jnp.pad(rope, ((0, 0), (0, 0), (0, rope_width - heads * ROPE)))
        return jnp.concatenate([plain, rope], axis=-1)

    def q_disorder(values):
        lead = values.shape[:2]
        plain = values[..., : heads * NOPE].reshape(*lead, heads, NOPE)
        rope = values[..., heads * NOPE : heads * (NOPE + ROPE)].reshape(*lead, heads, ROPE)
        return jnp.concatenate([plain, rope], axis=-1).reshape(lead[0], -1)

    expand_rows = expand_weight.shape[0]
    kv_width = heads * (NOPE + VHEAD)
    out_width = heads * VHEAD
    stack = slice_rows // expand_rows
    blocks_kv = kv_width // LANES
    expand_cols = -(-blocks_kv // stack)
    groups = cores if split else 1

    def expand_stack(values):
        tiles = [values[:, LANES * i : LANES * (i + 1)] for i in range(blocks_kv)]
        tiles += [jnp.zeros_like(tiles[0])] * (expand_cols * stack - blocks_kv)
        return jnp.concatenate(
            [jnp.concatenate(tiles[stack * i : stack * (i + 1)]) for i in range(expand_cols)],
            axis=1,
        )

    q_local = q_order(q_weight)
    out_local = out_weight.T
    packs = jnp.stack(
        [
            jnp.concatenate(
                [
                    q_local[:, g],
                    out_local[:, out_width * g : out_width * (g + 1)],
                    expand_stack(expand_weight[:, kv_width * g : kv_width * (g + 1)]),
                ],
                axis=1,
            )
            for g in range(groups)
        ]
    )
    pack_mine, pack_other = (mine(packs, 0), others(packs, 0)) if split else (packs[0], packs[0])
    attn_piece = jnp.concatenate([pack_mine, to_core(pack_other)])

    shift = jnp.stack([core, shard]).astype(jnp.int32)

    tokens, sending = (), []

    def now(value):
        return after(value, *tokens) if tokens else value

    def behind(value):
        return after(value, *tokens, *sending)

    def send(line, move, value, free=False):
        sending.append(now(value))
        return line.send(move, sending[-1], free=free)

    def close(*arrived):
        nonlocal tokens
        tokens = arrived
        sending.clear()

    attn_z, held = [attn_piece], {}
    wanted = []
    for j in range(tp_size):
        lead, tail = (1, 2) if j % 2 == 0 else (2, 1)
        wanted.append((j, lead, 0, lead == 1, True))
        wanted.append((j, tail, 0, tail == 1, False))
        wanted.append((j, 3, lead, lead == 2, False))

    def attention_round():
        for j, piece in enumerate(attn_z):
            held.setdefault((j, 0), piece)
        keys, arrived = [], []
        for over_x in (True, False):
            ready = [w for w in wanted if w[3] == over_x and (w[0], w[2]) in held]
            ready.sort(key=lambda w: not w[4])
            if ready:
                j, k, source = ready[0][:3]
                wanted.remove(ready[0])
                line, move = (line_x, swap_x) if over_x else (line_y, swap_y)
                arrived.append(send(line, move, held[j, source]))
                keys.append((j, k))
        held.update(zip(keys, arrived))
        if len(attn_z) < tp_size:
            attn_z.append(send(line_z, step_z, attn_z[-1]))
            arrived.append(attn_z[-1])
        return arrived

    arrived = attention_round()
    hid_a, hid_other, down_a, down_other = pack(
        behind(shift), part, gate_weight.T, up_weight.T, down_weight
    )
    close(*arrived, hid_a)
    arrived = attention_round()
    down_b = send(line_c, swap_core, down_other)
    hid_b = send(line_c, swap_core, hid_other, free=True)
    grad_own = features(now(cotangent).reshape(own, width))
    inputs16 = features(now(hidden).reshape(own, width))
    inputs = inputs16.astype(f32)
    seg_all = now(segments)[:, 0]
    bases = [core * span + place_z * rows, (1 - core) * span + place_z * rows][:slots]
    starts = [jnp.maximum(base + rows - window, 0) for base in bases]
    place = jnp.stack(
        [jnp.stack([a, b]) for a, b in zip(starts + [shard], bases + [core])]
    ).astype(jnp.int32)
    seg_query = jnp.concatenate(
        [lax.dynamic_slice_in_dim(seg_all, base, rows, 1) for base in bases], axis=1
    )
    seg_key = jnp.stack(
        [lax.dynamic_slice_in_dim(seg_all, start, window, 1) for start in starts], axis=1
    )
    query_index = jnp.concatenate([base + jnp.arange(rows, dtype=jnp.int32) for base in bases])
    first_index = jnp.sum(
        (seg_all[:, None, :] < seg_query[:, :, None]).astype(jnp.int32), axis=-1
    )
    positions = (query_index[None] - first_index).reshape(micro, slots, rows)
    positions = positions.transpose(1, 0, 2)
    freqs = THETA_BASE ** (-2.0 * jnp.arange(ROPE // 2, dtype=f32) / ROPE)
    angles = positions.astype(f32)[..., None] * freqs
    cos_rows, sin_rows = jnp.cos(angles), jnp.sin(angles)
    cos_lanes = jnp.concatenate([cos_rows] * 4, axis=-1)
    sin_lanes = jnp.concatenate([-sin_rows, sin_rows] * 2, axis=-1)
    tables = (seg_query[..., None], seg_key, cos_lanes, sin_lanes)

    close(*arrived, down_b, hid_b, grad_own, inputs16)
    while len(attn_z) < tp_size - 1:
        close(*attention_round())
    arrived = attention_round()
    down_a1 = send(line_x, swap_x, down_a, free=True)
    down_b2 = send(line_y, swap_y, down_b, free=True)
    own_lanes = [lanes[0].reshape(own, LANES) for lanes in (cos_lanes, sin_lanes)]
    normed_own, latent_part, latent_pack, factor_one, factor_latent = in_one(
        begin_kernel,
        "begin",
        [
            ((own, width), bf16),
            ((own, KVRANK), f32),
            ((own, kv_cols), bf16),
            ((own, 1), f32),
            ((own, 1), f32),
        ],
        shift,
        behind(inputs16),
        gain_one[None],
        w_latent,
        gain_kv[None],
        *own_lanes,
    )
    latent_pack = latent_pack.reshape(micro, rows, kv_cols)
    close(*arrived, down_a1, down_b2, latent_pack)
    latent_z, grad_z = [latent_pack], [grad_own]

    def latents_ahead():
        if len(latent_z) < tp_size:
            latent_z.append(send(line_z, step_z, latent_z[-1]))
        return latent_z[-1]

    def grads_ahead(count):
        for _ in range(count):
            grad_z.append(send(line_z, step_z, grad_z[-1]))

    arrived = attention_round()
    down_b1 = send(line_x, swap_x, down_b, free=True)
    down_a2 = send(line_y, swap_y, down_a, free=True)
    close(*arrived, down_b1, down_a2, latents_ahead())
    arrived = attention_round()
    down_b3 = send(line_x, swap_x, down_b2, free=True)
    down_a3 = send(line_y, swap_y, down_a1, free=True)
    close(*arrived, down_b3, down_a3, latents_ahead())
    while len(wanted) > 2:
        close(*attention_round(), latents_ahead())
    arrived = attention_round()
    normed_chip = normed_own
    if split:
        normed_chip = jnp.concatenate([normed_own, send(line_c, swap_core, normed_own)])
    half_tp = tp_size // 2
    latent_far = [send(line_c, swap_core, jnp.concatenate(latent_z[:half_tp]))]
    while len(latent_z) < tp_size:
        latents_ahead()
    close(*arrived, normed_chip, latent_far[0], latent_z[-1])
    attn_xy = [[held[j, k] for k in range(4)] for j in range(tp_size)]

    hid_a1, hid_b2 = send(line_x, swap_x, hid_a), send(line_y, swap_y, hid_b)
    grads_ahead(1)
    latent_far.append(send(line_c, swap_core, jnp.concatenate(latent_z[half_tp:])))
    q_cols, out_cols = q_width, q_width + out_width

    def core_row(k, half):
        def row(ref):
            at = ref[0] if half == 0 else 1 - ref[0]
            return (2 * k + at) * slice_rows

        return (slice_rows, row)

    def expand_row(k, half):
        def row(ref):
            at = ref[0] if half == 0 else 1 - ref[0]
            return (2 * (ref[1] ^ k) + at) * expand_rows

        return (expand_rows, row)

    moves = []
    for j in range(tp_size):
        for k in range(4):
            for half in range(2):
                source, top = 4 * j + k, half * slice_rows
                moves.append(
                    (source, top, slice_rows, 0, q_width, 0, core_row(k, half), j * q_width)
                )
                moves.append(
                    (source, top, slice_rows, q_cols, out_width, 1, core_row(k, half), j * out_width)
                )
                for i in range(blocks_kv):
                    moves.append(
                        (
                            source,
                            top + i % stack * expand_rows,
                            expand_rows,
                            out_cols + i // stack * LANES,
                            LANES,
                            2,
                            expand_row(k, half),
                            j * kv_width + i * LANES,
                        )
                    )
    w_query, w_out, w_expand = assemble(
        [piece for pieces in attn_xy for piece in pieces],
        moves,
        [(width, tp_size * q_width), (width, tp_size * out_width), (KVRANK, tp_size * kv_width)],
        now(shift),
    )
    q_lin = dot(normed_chip, w_query).reshape(slots, micro, rows, tp_size * q_width)
    latent_rows = [
        [(at * span + (place_z - j) % tp_size * rows) for j in range(tp_size)]
        for at in (core, 1 - core)
    ]
    latent_all, rope_keys = lay_out(
        jnp.stack([row for each in latent_rows for row in each]).astype(jnp.int32),
        latent_z + latent_far,
        micro,
        length,
    )
    latent_all = latent_all.reshape(micro * length, KVRANK)
    kv_all = dot(latent_all, w_expand, bf16).reshape(micro, length, tp_size * kv_width)
    close(hid_a1, hid_b2, grad_z[-1], q_lin, kv_all)

    hid_b1, hid_a2 = send(line_x, swap_x, hid_b), send(line_y, swap_y, hid_a)
    more = tp_size - 3
    grads_ahead(more)
    grad_far = [send(line_c, swap_core, piece, free=True) for piece in grad_z[:2]]
    mixed = attend(heads, tp_size, window, scale, behind(place), q_lin, kv_all, rope_keys, *tables)
    mixed = mixed.reshape(slots * own, tp_size * out_width)
    close(hid_b1, hid_a2, grad_z[-1], *grad_far, mixed)

    hid_b3, hid_a3 = send(line_x, swap_x, hid_b2), send(line_y, swap_y, hid_a1)
    mixed = now(mixed)
    if split:
        mixed_out = dot_rt(mixed, w_out, bf16)
        middle = inputs + mixed_out[:own].astype(f32) + to_core(mixed_out[own:]).astype(f32)
    else:
        middle = inputs + dot_rt(mixed, w_out)
    factor_two = norm_scale(middle)
    normed_two = (middle * factor_two * gain_two).astype(bf16)
    norm_z = [normed_two, send(line_z, step_z, normed_two)]
    norm_far = [send(line_c, swap_core, normed_two)]
    for piece in grad_z[2:]:
        grad_far.append(send(line_c, swap_core, piece))
    close(hid_b3, hid_a3, norm_z[-1], *norm_far, *grad_far[2:])

    hidden_pieces = [hid_a, hid_a1, hid_a2, hid_a3, hid_b, hid_b1, hid_b2, hid_b3]
    down_pieces = [down_a, down_a1, down_a2, down_a3, down_b, down_b1, down_b2, down_b3]
    whole, back_parts, out_parts = [], [], []

    class Ring:
        def __init__(self, parts):
            self.parts, self.at, self.total, self.seen = parts, 0, None, {}

        def block(self, j):
            if j not in self.seen:
                own_part, far_part = self.parts[j]
                self.seen[j] = add16(own_part, send(line_c, swap_core, far_part))
            return self.seen[j]

        def step(self):
            if self.at == tp_size - 1:
                return ()
            self.at += 1
            total = self.block(self.at)
            if self.total is not None:
                total = add16(total, self.total)
            self.total = send(line_z, step_z, total)
            return (self.total,)

        def result(self):
            while self.step():
                pass
            return self.total.astype(f32) + self.block(0).astype(f32)

    back_ring, out_ring = Ring(back_parts), Ring(out_parts)
    for j in range(tp_size):
        arrived = []
        if len(norm_z) < tp_size:
            norm_z.append(send(line_z, step_z, norm_z[-1]))
            arrived.append(norm_z[-1])
        elif len(grad_z) < tp_size:
            grads_ahead(1 if j + 2 < tp_size else tp_size - len(grad_z))
            arrived.append(grad_z[-1])
        elif back_ring.at + 1 < len(back_parts):
            arrived += back_ring.step()
        if j + 1 < tp_size:
            norm_far.append(send(line_c, swap_core, norm_z[j + 1]))
            arrived.append(norm_far[-1])
        while len(grad_far) <= j:
            grad_far.append(send(line_c, swap_core, grad_z[len(grad_far)], free=True))
        made = feed(
            behind(shift),
            j,
            tp_size,
            [norm_z[j], norm_far[j], grad_z[j], grad_far[j]],
            hidden_pieces,
            down_pieces,
            whole,
        )
        back_parts.append(made[:2])
        out_parts.append(made[2:4])
        whole = made[4:]
        close(*arrived, made[0])
    act_all, hidden_all, normed_all, grad_all = whole

    first, second = ((3, 0), (2, 0), (3, 1), (1, 1)), ((1, 0), (0, 0), (2, 1), (0, 1))
    arrived = back_ring.step()
    down_y, down_x, down_kept = weight_grad(
        behind(shift), SENT_BLOCKS, slice_rows, grad_all, act_all
    )
    close(*arrived, down_y)

    down_y, down_x = send(line_y, swap_y, down_y), send(line_x, swap_x, down_x)
    arrived = []
    while back_ring.at < tp_size - 1:
        arrived += back_ring.step()
    back_ring.block(0)
    own3, own2, far3, far1 = weight_grad(
        behind(shift), [(block,) for block in first], slice_rows, normed_all, hidden_all
    )
    close(*arrived, down_y, down_x, own3)

    own3, far3 = send(line_y, swap_y, own3), send(line_x, swap_x, far3)
    arrived = out_ring.step()
    grad_mid_norm, grad_gain_two = norm_back(middle, factor_two, gain_two, back_ring.result())
    grad_middle = grad_own.astype(f32) + grad_mid_norm
    grad_attn = grad_middle.astype(bf16)
    attn_far = send(line_c, swap_core, grad_attn, free=True)
    own1, own0, far2, far0 = weight_grad(
        behind(shift), [(block,) for block in second], slice_rows, normed_all, hidden_all
    )
    close(*arrived, own3, far3, attn_far, own1)

    own2, far1 = send(line_y, swap_y, own2), send(line_x, swap_x, far1)

    if split:
        grad_attn = jnp.concatenate([grad_attn, attn_far])
    grad_mixed = dot(grad_attn, w_out, bf16)
    out_blocks = [dot_lt(columns(grad_attn, k), mixed, bf16) for k in range(4)]
    close(own2, far1, grad_mixed, *out_blocks)

    def cut(value):
        middle_row = value.shape[0] // 2
        return value[:middle_row], value[middle_row:]

    def block_of(blocks, k, half):
        return cut(blocks[k])[half]

    def sent_of(blocks):
        return [jnp.concatenate([block_of(blocks, *at) for at in pair]) for pair in SENT_BLOCKS[:2]]

    def kept_of(blocks):
        return jnp.concatenate([block_of(blocks, *at) for at in SENT_BLOCKS[2]])

    def stage_one(over_y, over_x):
        return send(line_y, swap_y, over_y, free=True), send(line_x, swap_x, over_x, free=True)

    def stage_two(kept, sent):
        (top1, top0), (low2, low0) = (cut(each) for each in cut(kept))
        (top3, top2), (low3, low1) = cut(now(sent[0])), cut(now(sent[1]))
        top1 = send(line_x, swap_x, add16(top1, top3), free=True)
        low2 = send(line_y, swap_y, add16(low2, low3), free=True)
        return (top0, top2, top1), (low0, low1, low2)

    def stage_sum(tops, lows):
        return jnp.concatenate([add16(*tops), add16(*lows)])

    (down3, down2), (downf3, downf1) = cut(down_y), cut(down_x)
    (down1, down0), (downf2, downf0) = (cut(each) for each in cut(down_kept))
    over_x = send(
        line_x, swap_x, jnp.concatenate([add16(own1, now(own3)), add16(down1, down3)], axis=1)
    )
    over_y = send(
        line_y, swap_y, jnp.concatenate([add16(far2, now(far3)), add16(downf2, downf3)], axis=1)
    )
    arrived = out_ring.step()
    out_sent = stage_one(*sent_of(out_blocks))
    made = attend_back(
        heads,
        tp_size,
        window,
        scale,
        behind(place),
        q_lin,
        kv_all,
        rope_keys,
        *tables,
        grad_mixed.reshape(slots, micro, rows, tp_size * out_width),
        normed_chip,
        latent_all,
        w_query,
        w_expand,
    )
    sums, (latent_mine, latent_others), parts = made[:6], made[6:8], made[8:]
    close(over_x, over_y, *arrived, *out_sent, sums[0])

    query_sent = stage_one(*sums[:2])
    latent_far = send(line_c, swap_core, latent_others)
    arrived = []
    while out_ring.at < tp_size - 1:
        arrived += out_ring.step()
    hid_own = add16(own0, own2, over_x[:, : 2 * part])
    hid_other = add16(far0, far1, over_y[:, : 2 * part])
    down_own = add16(down0, down2, over_x[:, 2 * part :])
    down_other = add16(downf0, downf1, over_y[:, 2 * part :])
    close(*query_sent, *arrived, latent_far, hid_own, hid_other, down_own, down_other)

    latent_sum = add16(latent_mine, now(latent_far))

    def latent_block(j):
        return lax.dynamic_slice_in_dim(latent_sum, (place_z - j) % tp_size * rows, rows, 1)

    latent_step = send(line_z, step_z, latent_block(1))
    out_sums = stage_two(kept_of(out_blocks), out_sent)
    expand_sent = stage_one(*sums[3:5])
    output = (middle + out_ring.result()).astype(bf16)
    close(latent_step, out_sums[0][2], out_sums[1][2], *expand_sent, output)

    class Columns:
        def __init__(self, sums, count):
            self.value, self.count, self.at = stage_sum(*sums), count, 1
            self.total = self.block(1)

        def block(self, j):
            return self.value[:, self.count * j : self.count * (j + 1)]

        def step(self):
            if self.at > tp_size - 1:
                return ()
            self.total = line_z.send(step_z, now(self.total), free=True)
            self.at += 1
            return (self.total,)

        def add(self):
            if self.at <= tp_size:
                self.total = add16(now(self.total), self.block(self.at % tp_size))
                if self.at == tp_size:
                    self.at += 1

    for j in range(2, tp_size - 1):
        latent_step = send(line_z, step_z, add16(now(latent_step), latent_block(j)))
    expand_sums = stage_two(sums[5], expand_sent)
    out_columns = Columns(out_sums, out_width)
    arrived = out_columns.step()
    hid_far = send(line_c, swap_core, hid_other)
    close(latent_step, expand_sums[0][2], expand_sums[1][2], *arrived, hid_far)

    latent_step = send(line_z, step_z, add16(now(latent_step), latent_block(tp_size - 1)))
    query_sums = stage_two(sums[2], query_sent)
    out_columns.add()
    expand_columns = Columns(expand_sums, kv_width)
    arrived = [*out_columns.step(), *expand_columns.step()]
    far_part = None
    if split:
        far_part = send(line_c, swap_core, parts[1].reshape(own, width))
    down_far = send(line_c, swap_core, down_other, free=True)
    close(latent_step, query_sums[0][2], query_sums[1][2], *arrived, down_far, far_part)

    query_columns = Columns(query_sums, q_width)
    out_columns.add()
    expand_columns.add()
    arrived = [*query_columns.step(), *expand_columns.step(), *out_columns.step()]
    grad_wgate, grad_wup, grad_wdown = spread(
        behind(shift), hidden_here, hid_own, hid_far, down_own, down_far
    )
    grad_wgate, grad_wup = grad_wgate.T, grad_wup.T
    others_of = [] if far_part is None else [far_part]
    kernel = finish_kernel
    if far_part is None:
        kernel = lambda *refs: finish_kernel(*refs[:9], None, *refs[9:])
    gathered_rows = 4 * (width // 8 + 16)
    input_grad, w_mine, w_other = in_one(
        kernel,
        "finish",
        [((own, width), bf16), *[((gathered_rows, kv_cols), bf16)] * 2],
        shift,
        behind(latent_step).reshape(own, kv_cols),
        latent_block(0).reshape(own, kv_cols),
        latent_part,
        factor_latent,
        gain_kv[None],
        *own_lanes,
        parts[0].reshape(own, width),
        *others_of,
        w_latent,
        inputs16,
        factor_one,
        gain_one[None],
        grad_middle,
        normed_own,
        grad_gain_two[None],
        scratch=[((1, width), f32), ((1, KVRANK), f32), ((width, kv_cols), bf16)],
    )
    close(*arrived, input_grad, grad_wdown)

    rings = [query_columns, expand_columns]
    for ring in rings:
        ring.add()
    arrived = [step for ring in rings for step in ring.step()]
    w_sum = add16(w_mine, send(line_c, swap_core, w_other, free=True))
    high = w_sum.shape[0] // 4
    w_far = [
        lax.ppermute(w_sum[high * k : high * (k + 1)], "shard", [(i, i ^ k) for i in range(4)])
        for k in (1, 2, 3)
    ]
    close(*arrived, *w_far)

    w_sum = add16(w_sum[:high], *(now(each) for each in w_far))
    for ring in rings:
        ring.add()
    arrived = [step for ring in rings for step in ring.step()]

    def rows_for(at):
        rows_at = lax.dynamic_slice_in_dim(w_sum, at * small_rows, small_rows, 0)
        return jnp.concatenate([rows_at, w_sum[high - 16 :]])

    w_here = rows_for(place_z).astype(f32)
    for j in range(1, tp_size):
        pairs = [(i, (i + j) % tp_size) for i in range(tp_size)]
        w_here = w_here + lax.ppermute(rows_for((place_z + j) % tp_size), "tp", pairs).astype(f32)
    grad_wlatent, gains = w_here[:small_rows], w_here[small_rows]

    def own_gains(start, count):
        each = count // tp_size
        return lax.dynamic_slice_in_dim(gains[start : start + count], place_z * each, each, 0)

    grad_gain_one, grad_gain_two = own_gains(0, width // 8), own_gains(width // 8, width // 8)
    grad_gain_latent = own_gains(width // 4, KVRANK // 8)
    close(*arrived)
    for ring in (*rings, out_columns):
        while ring.at <= tp_size:
            ring.add()
            if ring.at < tp_size:
                ring.total = step_z(ring.total)
                ring.at += 1
    query_here, expand_here, out_here = (ring.total for ring in (*rings, out_columns))

    def finished(value, here_rows):
        halves = value.reshape(cores, here_rows, value.shape[1])
        kept, given = mine(halves, 0), swap_core(others(halves, 0))
        if split:
            return in_order(core, kept[:, None], given[:, None], 1).astype(f32)
        return (kept.astype(f32) + given.astype(f32))[:, None]

    grad_wout = finished(out_here, slice_rows).reshape(slice_rows, -1).T
    grad_wexpand = finished(expand_here, expand_rows).reshape(expand_rows, -1)
    grad_wquery = q_disorder(finished(query_here, slice_rows))
    like = (micro, 1, rows, width)
    return (
        features(output).reshape(like),
        features(input_grad).reshape(like),
        grad_gain_one,
        grad_wquery,
        grad_wlatent,
        grad_gain_latent,
        grad_wexpand,
        grad_wout,
        grad_gain_two,
        grad_wgate,
        grad_wup,
        grad_wdown,
    )


def solution(mesh):
    tokens = P(None, "shard", ("ctx", "tp"), None)
    everywhere = P(("shard", "ctx", "tp"))
    down_split = P(("shard", "ctx"), "tp")
    up_split = P("tp", ("shard", "ctx"))
    whole_rows = P(("shard", "ctx", "tp"), None)
    return jax.shard_map(
        shards,
        mesh=mesh,
        in_specs=(
            tokens,
            P(None, "shard", None),
            tokens,
            everywhere,
            down_split,
            whole_rows,
            everywhere,
            down_split,
            up_split,
            everywhere,
            down_split,
            down_split,
            up_split,
        ),
        out_specs=(
            tokens,
            tokens,
            everywhere,
            down_split,
            whole_rows,
            everywhere,
            down_split,
            up_split,
            everywhere,
            down_split,
            down_split,
            up_split,
        ),
        check_vma=False,
    )
```

```python
import functools

import jax
import jax.numpy as jnp
from jax import lax
from jax.experimental import pallas as pl
from jax.experimental.pallas import tpu as pltpu
from jax.sharding import PartitionSpec as P

NOPE = 128
ROPE = 64
VHEAD = 128
KVRANK = 512
DOC_MOST = 512
LANES = 128

EPSILON = 1e-06
THETA_BASE = 10000.0
NEG_FILL = -1e30

f32 = jnp.float32
bf16 = jnp.bfloat16


def norm_scale(values):
    return lax.rsqrt(jnp.mean(values * values, axis=-1, keepdims=True) + EPSILON)


def norm_back(values, factor, gain_vec, grad_out):
    scaled = grad_out * gain_vec
    grad_in = factor * scaled - values * factor**3 * jnp.mean(
        scaled * values, axis=-1, keepdims=True
    )
    return (grad_in, jnp.sum(grad_out * values * factor, axis=0))


def rotate(values, cos_table, sin_table):
    half_width = values.shape[-1] // 2
    first_half = values[..., :half_width]
    second_half = values[..., half_width:]
    return jnp.concatenate(
        [
            first_half * cos_table - second_half * sin_table,
            second_half * cos_table + first_half * sin_table,
        ],
        axis=-1,
    )


def dot(left, right, kind=f32):
    return jnp.dot(left, right, preferred_element_type=f32).astype(kind)


def dot_rt(left, right, kind=f32):
    return lax.dot_general(
        left, right, (((1,), (1,)), ((), ())), preferred_element_type=f32
    ).astype(kind)


def dot_lt(left, right, kind=f32):
    return lax.dot_general(
        left, right, (((0,), (0,)), ((), ())), preferred_element_type=f32
    ).astype(kind)


def add16(*terms):
    total = terms[0].astype(f32)
    for term in terms[1:]:
        total = total + term.astype(f32)
    return total.astype(bf16)


def after(value, *others):
    return lax.optimization_barrier((value, *others))[0]


class Line:
    def __init__(self):
        self.last = None

    def send(self, move, value, *needs, free=False):
        if self.last is not None and not free:
            needs = (*needs, self.last)
        if needs:
            value = after(value, *needs)
        self.last = move(value)
        return self.last


def swap_core(value):
    return lax.ppermute(value, "ctx", [(0, 1), (1, 0)])


def swap_x(value):
    return lax.ppermute(value, "shard", [(i, i ^ 1) for i in range(4)])


def swap_y(value):
    return lax.ppermute(value, "shard", [(i, i ^ 2) for i in range(4)])


def step_z(value):
    size = lax.axis_size("tp")
    return lax.ppermute(value, "tp", [(i, (i + 1) % size) for i in range(size)])


def scatter_z(line_z, block_of, last=bf16, add=add16):
    size = lax.axis_size("tp")
    total = block_of(1)
    for j in range(2, size):
        total = add(line_z.send(step_z, total), block_of(j))
    return (line_z.send(step_z, total).astype(f32) + block_of(0).astype(f32)).astype(last)


def in_order(core, mine, other, axis):
    return jnp.where(
        core == 0,
        jnp.concatenate([mine, other], axis=axis),
        jnp.concatenate([other, mine], axis=axis),
    )


def assemble(sources, moves, shapes, place):
    depth = min(32, len(moves))

    def kernel(place_ref, *refs):
        given, made, sems = refs[: len(sources)], refs[len(sources) : -1], refs[-1]
        flight = []
        for i, (src, row, rows, column, columns, dst, to_row, to_column) in enumerate(moves):
            if i >= depth:
                flight[i - depth].wait()
            if not isinstance(to_row, int):
                to_row = pl.multiple_of(to_row[1](place_ref), to_row[0])
            copy = pltpu.make_async_copy(
                given[src].at[pl.ds(row, rows), pl.ds(column, columns)],
                made[dst].at[pl.ds(to_row, rows), pl.ds(to_column, columns)],
                sems.at[i % depth],
            )
            copy.start()
            flight.append(copy)
        for copy in flight[-depth:]:
            copy.wait()

    return pl.pallas_call(
        kernel,
        out_shape=[jax.ShapeDtypeStruct(shape, bf16) for shape in shapes],
        grid_spec=pltpu.PrefetchScalarGridSpec(
            num_scalar_prefetch=1,
            in_specs=[pl.BlockSpec(memory_space=pl.ANY)] * len(sources),
            out_specs=[pl.BlockSpec(memory_space=pltpu.VMEM)] * len(shapes),
            scratch_shapes=[pltpu.SemaphoreType.DMA((depth,))],
        ),
        compiler_params=pltpu.CompilerParams(vmem_limit_bytes=48 << 20),
        cost_estimate=pl.CostEstimate(
            flops=0,
            transcendentals=0,
            bytes_accessed=4 * sum(a * b for a, b in shapes),
        ),
        name="assemble",
    )(place, *sources)


def lay_out_kernel(places, *refs):
    given, (latent, rope) = refs[:-2], refs[-2:]
    micro, rows = latent.shape[0], given[0].shape[1]
    pieces = [each[i : i + micro] for each in given for i in range(0, each.shape[0], micro)]
    for place, piece in zip(range(len(pieces)), pieces):
        at = pl.ds(pl.multiple_of(places[place], rows), rows)
        latent[:, at, :] = piece[:, :, :KVRANK]
        keys = piece[:, :, KVRANK:]
        rope[:, at, :] = jnp.concatenate([keys, keys], axis=-1)


def lay_out(places, pieces, micro, length):
    in_vmem = pl.BlockSpec(memory_space=pltpu.VMEM)
    return pl.pallas_call(
        lay_out_kernel,
        out_shape=[
            jax.ShapeDtypeStruct((micro, length, KVRANK), bf16),
            jax.ShapeDtypeStruct((micro, length, 2 * ROPE), bf16),
        ],
        grid_spec=pltpu.PrefetchScalarGridSpec(
            num_scalar_prefetch=1,
            in_specs=[in_vmem] * len(pieces),
            out_specs=[in_vmem] * 2,
        ),
        cost_estimate=pl.CostEstimate(
            flops=0, transcendentals=0, bytes_accessed=4 * micro * length * (KVRANK + 2 * ROPE)
        ),
        name="lay_out",
    )(places, *pieces)


def begin_kernel(place, hidden, gain, w_latent, gain_kv, cos_ref, sin_ref, normed, raw, packed, scale_one, scale_kv):
    values = hidden[...].astype(f32)
    factor = norm_scale(values)
    scale_one[...] = factor
    normed[...] = (values * factor * gain[...]).astype(bf16)
    latent = dot(normed[...], w_latent[...])
    own = latent[:, :KVRANK]
    raw[...] = own
    factor = norm_scale(own)
    scale_kv[...] = factor
    ropes = latent[:, KVRANK:]
    ropes = jnp.concatenate([ropes, ropes], axis=1)
    lane = lax.broadcasted_iota(jnp.int32, ropes.shape, 1)
    ropes = ropes * cos_ref[...] + swap_halves(ropes, lane) * sin_ref[...]
    packed[:, :KVRANK] = (own * factor * gain_kv[...]).astype(bf16)
    packed[:, KVRANK:] = ropes[:, :ROPE].astype(bf16)


def in_one(kernel, name, outs, place, *operands, scratch=()):
    in_vmem = pl.BlockSpec(memory_space=pltpu.VMEM)
    moved = sum(x.size * x.dtype.itemsize for x in operands)
    return pl.pallas_call(
        kernel,
        out_shape=[jax.ShapeDtypeStruct(shape, kind) for shape, kind in outs],
        grid_spec=pltpu.PrefetchScalarGridSpec(
            num_scalar_prefetch=1,
            in_specs=[in_vmem] * len(operands),
            out_specs=[in_vmem] * len(outs),
            scratch_shapes=[pltpu.VMEM(shape, kind) for shape, kind in scratch],
        ),
        compiler_params=pltpu.CompilerParams(vmem_limit_bytes=58 << 20),
        cost_estimate=pl.CostEstimate(flops=0, transcendentals=0, bytes_accessed=moved),
        name=name,
    )(place, *operands)


def finish_kernel(
    place,
    latent_far,
    latent_here,
    raw,
    scale_kv,
    gain_kv,
    cos_ref,
    sin_ref,
    own_part,
    far_part,
    w_latent,
    hidden,
    scale_one,
    gain,
    grad_middle,
    normed,
    grad_gain_two,
    input_grad,
    w_mine,
    w_other,
    grad_gain,
    grad_gain_kv,
    grad_w,
):
    grads = latent_far[...].astype(f32) + latent_here[...].astype(f32)
    grad_part, total = norm_back(raw[...], scale_kv[...], gain_kv[...], grads[:, :KVRANK])
    grad_gain_kv[...] = total[None]
    ropes = grads[:, KVRANK:]
    ropes = jnp.concatenate([ropes, ropes], axis=1)
    lane = lax.broadcasted_iota(jnp.int32, ropes.shape, 1)
    ropes = ropes * cos_ref[...] - swap_halves(ropes, lane) * sin_ref[...]
    grad_raw = jnp.concatenate([grad_part, ropes[:, :ROPE]], axis=1).astype(bf16)
    grad_w[...] = dot_lt(normed[...], grad_raw, bf16)
    grad_normed = dot_rt(grad_raw, w_latent[...]) + own_part[...].astype(f32)
    if far_part is not None:
        grad_normed = grad_normed + far_part[...].astype(f32)
    grad_in, total = norm_back(
        hidden[...].astype(f32), scale_one[...], gain[...], grad_normed
    )
    grad_gain[...] = total[None]
    input_grad[...] = (grad_middle[...] + grad_in).astype(bf16)
    size, kv_size = grad_w.shape[0] // 8, KVRANK // 8
    for out, half in ((w_mine, place[0]), (w_other, 1 - place[0])):
        for k in range(4):
            at = pl.multiple_of((2 * k + half) * size, size)
            top = k * (size + 16)
            out[top : top + size, :] = grad_w[pl.ds(at, size), :]
            both = pl.multiple_of((place[1] ^ k) * 2 * kv_size, 2 * kv_size)
            kv_row = jnp.broadcast_to(grad_gain_kv[:, pl.ds(both, 2 * kv_size)], (16, 2 * kv_size))
            kv_row = jnp.where(half == 0, kv_row, pltpu.roll(kv_row, kv_size, 1))[:, :kv_size]
            row = [
                jnp.broadcast_to(gains[:, pl.ds(at, size)], (16, size))
                for gains in (grad_gain, grad_gain_two)
            ]
            out[top + size : top + size + 16, :] = jnp.concatenate([*row, kv_row], axis=1).astype(
                bf16
            )


SENT_BLOCKS = (((3, 0), (2, 0)), ((3, 1), (1, 1)), ((1, 0), (0, 0), (2, 1), (0, 1)))


def swap_halves(values, lane):
    return jnp.where(
        lane % ROPE < ROPE // 2,
        pltpu.roll(values, LANES - ROPE // 2, 1),
        pltpu.roll(values, ROPE // 2, 1),
    )


def window_mask(start, base, rows, width, seg_query, seg_key):
    query_index = base + lax.broadcasted_iota(jnp.int32, (rows, width), 0)
    key_index = start + lax.broadcasted_iota(jnp.int32, (rows, width), 1)
    same_doc = (seg_query == seg_key) & (key_index <= query_index) & (seg_key != 0)
    return same_doc | (key_index == query_index)


def head_operands(q_ref, kv_ref, rope_key, slot, window, head, heads, cos_table, sin_table):
    rows = q_ref.shape[2]
    lane = lax.broadcasted_iota(jnp.int32, (rows, LANES), 1)
    first = heads * NOPE + head // 2 * LANES
    rope_lin = q_ref[slot, 0, :, first : first + LANES]
    turned = rope_lin * cos_table + swap_halves(rope_lin, lane) * sin_table
    turned = jnp.where(lane // ROPE == head % 2, turned, 0.0)
    plain = q_ref[slot, 0, :, head * NOPE : (head + 1) * NOPE]
    query = jnp.concatenate([plain, turned], axis=1).astype(bf16)
    at = head * (NOPE + VHEAD)
    key = jnp.concatenate([kv_ref[0, window, at : at + NOPE], rope_key], axis=1)
    value = kv_ref[0, window, at + NOPE : at + NOPE + VHEAD]
    return query, key, value


def attend_kernel(
    heads, width, scale, place, q_ref, kv_ref, kr_ref, segq_ref, segk_ref, cos_ref, sin_ref, o_ref
):
    slots, rows = q_ref.shape[0], q_ref.shape[2]
    for slot in range(slots):
        start = pl.multiple_of(place[slot, 0], rows)
        window = pl.ds(start, width)
        allowed = window_mask(
            start,
            place[slot, 1],
            rows,
            width,
            segq_ref[0, slot * rows : (slot + 1) * rows, :],
            segk_ref[0, slot : slot + 1, :],
        )
        rope_key = kr_ref[0, window, :]
        for head in range(heads):
            query, key, value = head_operands(
                q_ref, kv_ref, rope_key, slot, window, head, heads, cos_ref[slot, 0], sin_ref[slot, 0]
            )
            scores = jnp.where(allowed, dot_rt(query, key) * scale, NEG_FILL)
            expd = jnp.exp(scores - jnp.max(scores, axis=-1, keepdims=True))
            probs = expd / jnp.sum(expd, axis=-1, keepdims=True)
            o_ref[slot, 0, :, head * VHEAD : (head + 1) * VHEAD] = dot(
                probs.astype(bf16), value, bf16
            )


def attend_back_kernel(
    heads,
    width,
    scale,
    groups,
    place,
    q_ref,
    kv_ref,
    kr_ref,
    segq_ref,
    segk_ref,
    cos_ref,
    sin_ref,
    do_ref,
    norm_ref,
    latent_ref,
    wq_ref,
    wkv_ref,
    *refs,
):
    slots, rows = q_ref.shape[0], q_ref.shape[2]
    q_width, kv_width = q_ref.shape[3], kv_ref.shape[2]
    query_outs, expand_outs, latent_outs = refs[:3], refs[3:6], refs[6:8]
    parts, (total, rope_total, kv_grads, q_grads, expand_grads) = refs[8:-5], refs[-5:]
    group, m = pl.program_id(0), pl.program_id(1)
    micro = pl.num_programs(1)
    lane = lax.broadcasted_iota(jnp.int32, (rows, LANES), 1)
    q_first = pl.multiple_of(group * q_width, LANES)
    kv_first = pl.multiple_of(group * kv_width, LANES)

    def q_rows(slot):
        return pl.ds(pl.multiple_of((slot * micro + m) * rows, rows), rows)

    @pl.when(group == 0)
    def _():
        rope_total[m] = jnp.zeros(rope_total.shape[1:], f32)

    total[...] = jnp.zeros_like(total)
    for slot in range(slots):
        start = pl.multiple_of(place[slot, 0], rows)
        window = pl.ds(start, width)
        allowed = window_mask(
            start,
            place[slot, 1],
            rows,
            width,
            segq_ref[0, slot * rows : (slot + 1) * rows, :],
            segk_ref[0, slot : slot + 1, :],
        )
        rope_key = kr_ref[0, window, :]
        rope_grads = None
        for head in range(heads):
            query, key, value = head_operands(
                q_ref, kv_ref, rope_key, slot, window, head, heads, cos_ref[slot, 0], sin_ref[slot, 0]
            )
            grad_mixed = do_ref[slot, 0, :, head * VHEAD : (head + 1) * VHEAD]
            scores = jnp.where(allowed, dot_rt(query, key) * scale, NEG_FILL)
            expd = jnp.exp(scores - jnp.max(scores, axis=-1, keepdims=True))
            probs = expd / jnp.sum(expd, axis=-1, keepdims=True)
            grad_probs = dot_rt(grad_mixed, value)
            inner = jnp.sum(probs * grad_probs, axis=-1, keepdims=True)
            grad_scores = (scale * probs * (grad_probs - inner)).astype(bf16)
            grad_query = dot(grad_scores, key)
            grad_key = dot_lt(grad_scores, query)
            at = head * (NOPE + VHEAD)
            total[window, at : at + NOPE] += grad_key[:, :NOPE]
            rope_total[m, window, :] += grad_key[:, NOPE:]
            total[window, at + NOPE : at + NOPE + VHEAD] += dot_lt(probs.astype(bf16), grad_mixed)
            q_grads[q_rows(slot), pl.ds(q_first + head * NOPE, NOPE)] = grad_query[:, :NOPE].astype(
                bf16
            )
            if head % 2 == 0:
                rope_grads = jnp.where(lane < ROPE, grad_query[:, NOPE:], 0.0)
            else:
                rope_grads = jnp.where(lane < ROPE, rope_grads, grad_query[:, NOPE:])
            if head % 2 == 1 or head == heads - 1:
                turned = rope_grads * cos_ref[slot, 0] - swap_halves(rope_grads, lane) * sin_ref[slot, 0]
                first = q_first + heads * NOPE + head // 2 * LANES
                q_grads[q_rows(slot), pl.ds(first, LANES)] = turned.astype(bf16)
    kv_grads[m, :, pl.ds(kv_first, kv_width)] = total[...].astype(bf16)

    @pl.when(m == micro - 1)
    def _():
        grads = dot_lt(norm_ref[...], q_grads[:, pl.ds(q_first, q_width)], bf16)
        size = grads.shape[0] // 8
        for out, blocks in zip(query_outs, SENT_BLOCKS):
            for i, (k, half) in enumerate(blocks):
                out[i * size : (i + 1) * size, :] = grads[(2 * k + half) * size :][:size]
        back = kv_grads[:, :, pl.ds(kv_first, kv_width)]
        expand_grads[...] = dot_lt(
            latent_ref[...], back.reshape(latent_ref.shape[0], kv_width), bf16
        )
        size = expand_grads.shape[0] // 8
        shard = place[slots, 0]
        for out, blocks in zip(expand_outs, SENT_BLOCKS):
            for i, (k, half) in enumerate(blocks):
                at = pl.multiple_of((2 * (shard ^ k) + half) * size, size)
                out[i * size : (i + 1) * size, :] = expand_grads[pl.ds(at, size), :]

    @pl.when(group == groups - 1)
    def _():
        span = latent_outs[0].shape[1]
        for out, half in zip(latent_outs, (place[slots, 1], 1 - place[slots, 1])):
            at = pl.ds(pl.multiple_of(half * span, span), span)
            out[0, :, :KVRANK] = dot_rt(kv_grads[m, at, :], wkv_ref[...], bf16)
            ropes = rope_total[m, at, :]
            ropes = ropes + pltpu.roll(ropes, ROPE, 1)
            out[0, :, KVRANK:] = ropes[:, :ROPE].astype(bf16)
        for slot, out in enumerate(parts):
            out[0] = dot_rt(q_grads[q_rows(slot), :], wq_ref[...], bf16)


def attention_specs(heads, slots, rows, length, width, q_width, order):
    def at(*index):
        return lambda a, b, place: tuple(
            {"m": (a, b)[order], "j": (a, b)[1 - order]}.get(i, i) for i in index
        )

    return [
        pl.BlockSpec((slots, 1, rows, q_width), at(0, "m", 0, "j")),
        pl.BlockSpec((1, length, heads * (NOPE + VHEAD)), at("m", 0, "j")),
        pl.BlockSpec((1, length, LANES), at("m", 0, 0)),
        pl.BlockSpec((1, slots * rows, 1), at("m", 0, 0)),
        pl.BlockSpec((1, slots, width), at("m", 0, 0)),
        pl.BlockSpec((slots, 1, rows, LANES), at(0, "m", 0, 0)),
        pl.BlockSpec((slots, 1, rows, LANES), at(0, "m", 0, 0)),
    ]


def attend(heads, groups, width, scale, place, q_lin, kv, rope_keys, seg_query, seg_key, cos, sin):
    slots, micro, rows, q_all = q_lin.shape
    length = kv.shape[1]
    return pl.pallas_call(
        functools.partial(attend_kernel, heads, width, scale),
        out_shape=jax.ShapeDtypeStruct((slots, micro, rows, groups * heads * VHEAD), bf16),
        grid_spec=pltpu.PrefetchScalarGridSpec(
            num_scalar_prefetch=1,
            grid=(micro, groups),
            in_specs=attention_specs(heads, slots, rows, length, width, q_all // groups, 0),
            out_specs=pl.BlockSpec(
                (slots, 1, rows, heads * VHEAD), lambda m, j, place: (0, m, 0, j)
            ),
        ),
        compiler_params=pltpu.CompilerParams(
            dimension_semantics=("arbitrary", "arbitrary"), vmem_limit_bytes=40 << 20
        ),
        cost_estimate=pl.CostEstimate(
            flops=2 * slots * rows * micro * groups * heads * width * 384,
            transcendentals=slots * rows * micro * groups * heads * width,
            bytes_accessed=2 * kv.size + 6 * q_lin.size,
        ),
        name="attend",
    )(place, q_lin, kv, rope_keys, seg_query, seg_key, cos, sin)


def attend_back(
    heads,
    groups,
    width,
    scale,
    place,
    q_lin,
    kv,
    rope_keys,
    seg_query,
    seg_key,
    cos,
    sin,
    d_o,
    normed,
    latents,
    w_query,
    w_expand,
):
    slots, micro, rows, q_all = q_lin.shape
    length = kv.shape[1]
    tokens, model = normed.shape
    q_width, kv_width = q_all // groups, kv.shape[2] // groups
    latent_width = KVRANK + ROPE

    def last(j, m, place):
        return (jnp.where(j == groups - 1, m, 0), 0, 0)

    def whole(shape):
        return pl.BlockSpec(shape, lambda j, m, place: (0, 0), pipeline_mode=pl.Buffered(1))

    def sent(total, columns):
        return [
            (jax.ShapeDtypeStruct((n * total // 8, columns * groups), bf16), n * total // 8, columns)
            for n in (2, 2, 4)
        ]

    grads = sent(model, q_width) + sent(KVRANK, kv_width)
    return pl.pallas_call(
        functools.partial(attend_back_kernel, heads, width, scale, groups),
        out_shape=[
            *(shape for shape, _, _ in grads),
            *[jax.ShapeDtypeStruct((micro, length // 2, latent_width), bf16)] * 2,
            *[jax.ShapeDtypeStruct((micro, rows, model), bf16)] * slots,
        ],
        grid_spec=pltpu.PrefetchScalarGridSpec(
            num_scalar_prefetch=1,
            grid=(groups, micro),
            in_specs=attention_specs(heads, slots, rows, length, width, q_width, 1)
            + [
                pl.BlockSpec((slots, 1, rows, heads * VHEAD), lambda j, m, place: (0, m, 0, j)),
                whole(normed.shape),
                whole(latents.shape),
                whole(w_query.shape),
                whole(w_expand.shape),
            ],
            out_specs=[
                *(
                    pl.BlockSpec((height, columns), lambda j, m, place: (0, j))
                    for _, height, columns in grads
                ),
                *[pl.BlockSpec((1, length // 2, latent_width), last)] * 2,
                *[pl.BlockSpec((1, rows, model), last)] * slots,
            ],
            scratch_shapes=[
                pltpu.VMEM((length, kv_width), f32),
                pltpu.VMEM((micro, length, LANES), f32),
                pltpu.VMEM(kv.shape, bf16),
                pltpu.VMEM((tokens, q_all), bf16),
                pltpu.VMEM((KVRANK, kv_width), bf16),
            ],
        ),
        compiler_params=pltpu.CompilerParams(
            dimension_semantics=("arbitrary", "arbitrary"), vmem_limit_bytes=60 << 20
        ),
        cost_estimate=pl.CostEstimate(
            flops=2 * slots * rows * micro * groups * heads * width * 1024
            + 4 * tokens * model * q_all
            + 4 * micro * length * KVRANK * kv.shape[2],
            transcendentals=slots * rows * micro * groups * heads * width,
            bytes_accessed=2 * kv.size + 4 * q_lin.size + 8 * w_query.size,
        ),
        name="attend_back",
    )(
        place,
        q_lin,
        kv,
        rope_keys,
        seg_query,
        seg_key,
        cos,
        sin,
        d_o,
        normed,
        latents,
        w_query,
        w_expand,
    )


def spans(total, step):
    return [(at, min(step, total - at)) for at in range(0, total, step)]


def feed_kernel(part, rows, offset, place, *refs):
    given, refs = refs[:20], refs[20:]
    refs = refs[4:] if offset else refs
    back_own, back_other, out_own, out_other, act_all, hid_all, norm_all, grad_all = refs[:8]
    w_hid, w_down, norm, grad, d_act, act, hid, sems = refs[8:]
    norm_own, norm_other, grad_own, grad_other = given[:4]
    slice_rows = given[4].shape[0]

    def at_core(i):
        core = place[0] if i < 4 else 1 - place[0]
        return pl.ds(pl.multiple_of((2 * (i % 4) + core) * slice_rows, slice_rows), slice_rows)

    early = [
        pltpu.make_async_copy(grad_own, grad.at[pl.ds(0, rows)], sems.at[0]),
        pltpu.make_async_copy(grad_other, grad.at[pl.ds(rows, rows)], sems.at[1]),
    ] + [
        pltpu.make_async_copy(given[12 + i], w_down.at[at_core(i)], sems.at[2 + i])
        for i in range(8)
    ]
    later = [
        pltpu.make_async_copy(norm_own, norm.at[pl.ds(0, rows)], sems.at[10]),
        pltpu.make_async_copy(norm_other, norm.at[pl.ds(rows, rows)], sems.at[11]),
    ] + [
        pltpu.make_async_copy(given[4 + i], w_hid.at[at_core(i)], sems.at[12 + i])
        for i in range(8)
    ]
    for copy in early + later:
        copy.start()
    for copy in early:
        copy.wait()

    def for_chunks(total, body):
        whole = total // 256

        def step(i, carry):
            body(pl.multiple_of(i * 256, 256), 256)
            return carry

        lax.fori_loop(0, whole, step, 0)
        if total % 256:
            body(whole * 256, total % 256)

    def act_back(start, size):
        d_act[:, pl.ds(start, size)] = dot(grad[...], w_down[:, pl.ds(start, size)])

    for_chunks(part, act_back)
    for copy in later:
        copy.wait()

    def forward(start, size):
        gate = dot(norm[...], w_hid[:, pl.ds(start, size)])
        up_at = start + part
        if not isinstance(start, int):
            up_at = pl.multiple_of(up_at, LANES)
        up = dot(norm[...], w_hid[:, pl.ds(up_at, size)])
        back = d_act[:, pl.ds(start, size)]
        sigma = jax.nn.sigmoid(gate)
        swish = gate * sigma
        act[:, pl.ds(start, size)] = (swish * up).astype(bf16)
        hid[:, pl.ds(start, size)] = (
            back * up * sigma * (1.0 + gate * (1.0 - sigma))
        ).astype(bf16)
        hid[:, pl.ds(up_at, size)] = (back * swish).astype(bf16)

    for_chunks(part, forward)
    here = pl.ds(offset * 2 * rows, 2 * rows)
    saves = [
        pltpu.make_async_copy(source, target.at[here], sems.at[20 + i])
        for i, (source, target) in enumerate(
            ((act, act_all), (hid, hid_all), (norm, norm_all), (grad, grad_all))
        )
    ]
    for copy in saves:
        copy.start()

    def backward(start, size):
        back = dot_rt(hid[...], w_hid[pl.ds(start, size), :], bf16)
        back_own[:, pl.ds(start, size)] = back[:rows]
        back_other[:, pl.ds(start, size)] = back[rows:]
        out = dot_rt(act[...], w_down[pl.ds(start, size), :], bf16)
        out_own[:, pl.ds(start, size)] = out[:rows]
        out_other[:, pl.ds(start, size)] = out[rows:]

    for_chunks(w_hid.shape[0], backward)
    for copy in saves:
        copy.wait()


def feed(place, offset, blocks, tokens, hidden_pieces, down_pieces, whole):
    rows, width = tokens[0].shape
    part = down_pieces[0].shape[1]
    anywhere = pl.BlockSpec(memory_space=pl.ANY)
    in_vmem = pl.BlockSpec(memory_space=pltpu.VMEM)
    total = 2 * rows * blocks
    operands = [*tokens, *hidden_pieces, *down_pieces, *whole]
    return pl.pallas_call(
        functools.partial(feed_kernel, part, rows, offset),
        out_shape=[jax.ShapeDtypeStruct((rows, width), bf16)] * 4
        + [
            jax.ShapeDtypeStruct((total, columns), bf16)
            for columns in (part, 2 * part, width, width)
        ],
        grid_spec=pltpu.PrefetchScalarGridSpec(
            num_scalar_prefetch=1,
            in_specs=[anywhere] * len(operands),
            out_specs=[in_vmem] * 4 + [anywhere] * 4,
            scratch_shapes=[
                pltpu.VMEM((width, 2 * part), bf16),
                pltpu.VMEM((width, part), bf16),
                pltpu.VMEM((2 * rows, width), bf16),
                pltpu.VMEM((2 * rows, width), bf16),
                pltpu.VMEM((2 * rows, part), f32),
                pltpu.VMEM((2 * rows, part), bf16),
                pltpu.VMEM((2 * rows, 2 * part), bf16),
                pltpu.SemaphoreType.DMA((24,)),
            ],
        ),
        input_output_aliases={21 + i: 4 + i for i in range(len(whole))},
        compiler_params=pltpu.CompilerParams(vmem_limit_bytes=58 << 20),
        cost_estimate=pl.CostEstimate(
            flops=2 * 2 * rows * width * part * 6,
            transcendentals=2 * rows * part,
            bytes_accessed=2 * (3 * width * part + 2 * rows * (6 * width + 3 * part)),
        ),
        name="feed",
    )(place, *operands)


def pack_kernel(part, place, gate, up, down, hid_mine, hid_other, down_mine, down_other):
    hidden_here, slice_rows = gate.shape
    rest = hidden_here - part

    def put(at, low, high, value):
        low[:, at : at + part] = value[:, :part]
        if rest < part:
            edge = rest // LANES * LANES
            high[:, at + edge : at + part] = jnp.zeros((slice_rows, part - edge), bf16)
        high[:, at : at + rest] = value[:, part:]

    def write(hid_low, hid_high, down_low, down_high):
        put(0, hid_low, hid_high, gate[...].T)
        put(part, hid_low, hid_high, up[...].T)
        put(0, down_low, down_high, down[...].T)

    @pl.when(place[0] == 0)
    def _():
        write(hid_mine, hid_other, down_mine, down_other)

    @pl.when(place[0] != 0)
    def _():
        write(hid_other, hid_mine, down_other, down_mine)


def pack(place, part, gate, up, down):
    slice_rows = gate.shape[1]
    in_vmem = pl.BlockSpec(memory_space=pltpu.VMEM)
    return pl.pallas_call(
        functools.partial(pack_kernel, part),
        out_shape=[jax.ShapeDtypeStruct((slice_rows, n * part), bf16) for n in (2, 2, 1, 1)],
        grid_spec=pltpu.PrefetchScalarGridSpec(
            num_scalar_prefetch=1, in_specs=[in_vmem] * 3, out_specs=[in_vmem] * 4
        ),
        compiler_params=pltpu.CompilerParams(vmem_limit_bytes=48 << 20),
        cost_estimate=pl.CostEstimate(
            flops=0, transcendentals=0, bytes_accessed=24 * slice_rows * part
        ),
        name="pack",
    )(place, gate, up, down)


def spread_kernel(place, hid_own, hid_far, down_own, down_far, *outs):
    part = down_own.shape[1]
    rest = outs[0].shape[0] - part

    def write(low, high):
        for out, i in zip(outs, (0, 1, 0)):
            hid, down = (low[0], low[1]) if out is not outs[2] else (low[1], low[1])
            out[:part, :] = hid[:, i * part : (i + 1) * part].T.astype(f32)
            hid = high[0] if out is not outs[2] else high[1]
            out[part:, :] = hid[:, i * part : (i + 1) * part].T.astype(f32)[:rest]

    @pl.when(place[0] == 0)
    def _():
        write((hid_own, down_own), (hid_far, down_far))

    @pl.when(place[0] != 0)
    def _():
        write((hid_far, down_far), (hid_own, down_own))


def spread(place, hidden_here, *halves):
    slice_rows = halves[0].shape[0]
    in_vmem = pl.BlockSpec(memory_space=pltpu.VMEM)
    return pl.pallas_call(
        spread_kernel,
        out_shape=[jax.ShapeDtypeStruct((hidden_here, slice_rows), f32)] * 3,
        grid_spec=pltpu.PrefetchScalarGridSpec(
            num_scalar_prefetch=1, in_specs=[in_vmem] * 4, out_specs=[in_vmem] * 3
        ),
        compiler_params=pltpu.CompilerParams(vmem_limit_bytes=48 << 20),
        cost_estimate=pl.CostEstimate(
            flops=0, transcendentals=0, bytes_accessed=20 * slice_rows * hidden_here
        ),
        name="spread",
    )(place, *halves)


def weight_grad_kernel(packs, place, left, right_ref, *refs):
    packed, (turned, buffer, sems) = refs[:-3], refs[-3:]
    slice_rows, tokens = packed[0].shape[0] // len(packs[0]), turned.shape[1]
    blocks = [block for pack in packs for block in pack]
    outs = [
        out.at[pl.ds(i * slice_rows, slice_rows)]
        for out, pack in zip(packed, packs)
        for i in range(len(pack))
    ]

    def fetch(i):
        k, half = blocks[i]
        core = place[0] if half == 0 else 1 - place[0]
        start = pl.multiple_of((2 * k + core) * slice_rows, slice_rows)
        return pltpu.make_async_copy(
            left.at[:, pl.ds(start, slice_rows)], buffer.at[i % 2], sems.at[i % 2]
        )

    @pl.when(pl.program_id(0) == 0)
    def _():
        fetch(0).start()
        for i in range(len(outs)):
            fetch(i).wait()
            if i + 1 < len(outs):
                fetch(i + 1).start()

            def turn(j, carry, i=i):
                at = pl.ds(pl.multiple_of(j * 256, 256), 256)
                turned[pl.ds(i * slice_rows, slice_rows), at] = buffer[i % 2, at, :].T
                return carry

            lax.fori_loop(0, tokens // 256, turn, 0)

    for half in range(0, len(outs), 4):
        rows = pl.ds(half * slice_rows, 4 * slice_rows)
        grads = dot(turned[rows, :], right_ref[...], bf16)
        for i in range(4):
            outs[half + i][...] = grads[i * slice_rows : (i + 1) * slice_rows]


def weight_grad(place, packs, slice_rows, left, right):
    tokens, columns = right.shape
    count = sum(len(pack) for pack in packs)
    heights = [len(pack) * slice_rows for pack in packs]
    return pl.pallas_call(
        functools.partial(weight_grad_kernel, packs),
        out_shape=[jax.ShapeDtypeStruct((height, columns), bf16) for height in heights],
        grid_spec=pltpu.PrefetchScalarGridSpec(
            num_scalar_prefetch=1,
            grid=(-(-columns // 256),),
            in_specs=[
                pl.BlockSpec(memory_space=pl.ANY),
                pl.BlockSpec((tokens, 256), lambda n, place: (0, n)),
            ],
            out_specs=[pl.BlockSpec((height, 256), lambda n, place: (0, n)) for height in heights],
            scratch_shapes=[
                pltpu.VMEM((count * slice_rows, tokens), bf16),
                pltpu.VMEM((2, tokens, slice_rows), bf16),
                pltpu.SemaphoreType.DMA((2,)),
            ],
        ),
        compiler_params=pltpu.CompilerParams(
            dimension_semantics=("arbitrary",), vmem_limit_bytes=48 << 20
        ),
        cost_estimate=pl.CostEstimate(
            flops=2 * tokens * columns * count * slice_rows,
            transcendentals=0,
            bytes_accessed=2 * (tokens * columns + count * slice_rows * (tokens + columns)),
        ),
        name="weight_grad",
    )(place, left, right)


def shards(
    hidden,
    segments,
    cotangent,
    attn_gain,
    q_weight,
    latent_weight,
    latent_gain,
    expand_weight,
    out_weight,
    mlp_gain,
    gate_weight,
    up_weight,
    down_weight,
):
    micro, _, rows, width = hidden.shape
    length = segments.shape[2]
    tp_size, cores = lax.axis_size("tp"), lax.axis_size("ctx")
    shard, core, place_z = lax.axis_index("shard"), lax.axis_index("ctx"), lax.axis_index("tp")
    span = rows * tp_size
    own = micro * rows
    block = width // 4
    slice_rows = q_weight.shape[0]
    heads_here = q_weight.shape[1] // (NOPE + ROPE)
    split = heads_here % cores == 0
    heads = heads_here // cores if split else heads_here
    slots = cores if split else 1
    rope_width = -(-heads * ROPE // LANES) * LANES
    q_width = heads * NOPE + rope_width
    scale = (NOPE + ROPE) ** (-0.5)
    hidden_here = gate_weight.shape[1]
    part = -(-hidden_here // (cores * LANES)) * LANES
    window = min(length, -(-(DOC_MOST + rows) // LANES) * LANES)

    line_x, line_y, line_z, line_c = Line(), Line(), Line(), Line()

    def features(values):
        size = values.shape[-1] // 4
        return jnp.concatenate(
            [
                lax.dynamic_slice_in_dim(values, (shard ^ k) * size, size, values.ndim - 1)
                for k in range(4)
            ],
            axis=-1,
        )

    def columns(values, k):
        return values[:, block * k : block * (k + 1)]

    def mine(values, axis):
        return lax.dynamic_index_in_dim(values, core, axis, keepdims=False)

    def others(values, axis):
        return lax.dynamic_index_in_dim(values, 1 - core, axis, keepdims=False)

    def to_core(value):
        return line_c.send(swap_core, value)

    small_rows = latent_weight.shape[0]
    gain_rows, latent_gains = attn_gain.shape[0], latent_gain.shape[0]
    kv_cols = latent_weight.shape[1]
    gains_row = jnp.concatenate([attn_gain, mlp_gain, latent_gain])
    gains_row = jnp.pad(gains_row, (0, kv_cols - gains_row.shape[0]))
    small = jnp.concatenate([latent_weight, jnp.pad(gains_row[None], ((0, 15), (0, 0)))])
    small_all = lax.all_gather(small, ("shard", "ctx", "tp"), axis=0)
    devices = 4 * cores * tp_size

    def own_first(values):
        size = values.shape[0] // 4
        return jnp.concatenate(
            [lax.dynamic_slice_in_dim(values, (shard ^ k) * size, size, 0) for k in range(4)]
        )

    w_latent = own_first(small_all[:, :small_rows].reshape(width, kv_cols))
    gain_all = small_all[:, small_rows].astype(f32)
    gain_one = own_first(gain_all[:, :gain_rows].reshape(width))
    gain_two = own_first(gain_all[:, gain_rows : 2 * gain_rows].reshape(width))
    gain_kv = gain_all[:, 2 * gain_rows : 2 * gain_rows + latent_gains].reshape(KVRANK)
    del devices

    def q_order(values):
        groups = values.shape[1] // (heads * (NOPE + ROPE))
        by_head = values.reshape(values.shape[0], groups, heads, NOPE + ROPE)
        plain = by_head[..., :NOPE].reshape(values.shape[0], groups, heads * NOPE)
        rope = by_head[..., NOPE:].reshape(values.shape[0], groups, heads * ROPE)
        rope = jnp.pad(rope, ((0, 0), (0, 0), (0, rope_width - heads * ROPE)))
        return jnp.concatenate([plain, rope], axis=-1)

    def q_disorder(values):
        lead = values.shape[:2]
        plain = values[..., : heads * NOPE].reshape(*lead, heads, NOPE)
        rope = values[..., heads * NOPE : heads * (NOPE + ROPE)].reshape(*lead, heads, ROPE)
        return jnp.concatenate([plain, rope], axis=-1).reshape(lead[0], -1)

    expand_rows = expand_weight.shape[0]
    kv_width = heads * (NOPE + VHEAD)
    out_width = heads * VHEAD
    stack = slice_rows // expand_rows
    blocks_kv = kv_width // LANES
    expand_cols = -(-blocks_kv // stack)
    groups = cores if split else 1

    def expand_stack(values):
        tiles = [values[:, LANES * i : LANES * (i + 1)] for i in range(blocks_kv)]
        tiles += [jnp.zeros_like(tiles[0])] * (expand_cols * stack - blocks_kv)
        return jnp.concatenate(
            [jnp.concatenate(tiles[stack * i : stack * (i + 1)]) for i in range(expand_cols)],
            axis=1,
        )

    q_local = q_order(q_weight)
    out_local = out_weight.T
    packs = jnp.stack(
        [
            jnp.concatenate(
                [
                    q_local[:, g],
                    out_local[:, out_width * g : out_width * (g + 1)],
                    expand_stack(expand_weight[:, kv_width * g : kv_width * (g + 1)]),
                ],
                axis=1,
            )
            for g in range(groups)
        ]
    )
    pack_mine, pack_other = (mine(packs, 0), others(packs, 0)) if split else (packs[0], packs[0])
    attn_piece = jnp.concatenate([pack_mine, to_core(pack_other)])

    shift = jnp.stack([core, shard]).astype(jnp.int32)

    tokens, sending = (), []

    def now(value):
        return after(value, *tokens) if tokens else value

    def behind(value):
        return after(value, *tokens, *sending)

    def send(line, move, value, free=False):
        sending.append(now(value))
        return line.send(move, sending[-1], free=free)

    def close(*arrived):
        nonlocal tokens
        tokens = arrived
        sending.clear()

    attn_z, held = [attn_piece], {}
    wanted = []
    for j in range(tp_size):
        lead, tail = (1, 2) if j % 2 == 0 else (2, 1)
        wanted.append((j, lead, 0, lead == 1, True))
        wanted.append((j, tail, 0, tail == 1, False))
        wanted.append((j, 3, lead, lead == 2, False))

    def attention_round():
        for j, piece in enumerate(attn_z):
            held.setdefault((j, 0), piece)
        keys, arrived = [], []
        for over_x in (True, False):
            ready = [w for w in wanted if w[3] == over_x and (w[0], w[2]) in held]
            ready.sort(key=lambda w: not w[4])
            if ready:
                j, k, source = ready[0][:3]
                wanted.remove(ready[0])
                line, move = (line_x, swap_x) if over_x else (line_y, swap_y)
                arrived.append(send(line, move, held[j, source]))
                keys.append((j, k))
        held.update(zip(keys, arrived))
        if len(attn_z) < tp_size:
            attn_z.append(send(line_z, step_z, attn_z[-1]))
            arrived.append(attn_z[-1])
        return arrived

    arrived = attention_round()
    hid_a, hid_other, down_a, down_other = pack(
        behind(shift), part, gate_weight.T, up_weight.T, down_weight
    )
    close(*arrived, hid_a)
    arrived = attention_round()
    down_b = send(line_c, swap_core, down_other)
    hid_b = send(line_c, swap_core, hid_other, free=True)
    grad_own = features(now(cotangent).reshape(own, width))
    inputs16 = features(now(hidden).reshape(own, width))
    inputs = inputs16.astype(f32)
    seg_all = now(segments)[:, 0]
    bases = [core * span + place_z * rows, (1 - core) * span + place_z * rows][:slots]
    starts = [jnp.maximum(base + rows - window, 0) for base in bases]
    place = jnp.stack(
        [jnp.stack([a, b]) for a, b in zip(starts + [shard], bases + [core])]
    ).astype(jnp.int32)
    seg_query = jnp.concatenate(
        [lax.dynamic_slice_in_dim(seg_all, base, rows, 1) for base in bases], axis=1
    )
    seg_key = jnp.stack(
        [lax.dynamic_slice_in_dim(seg_all, start, window, 1) for start in starts], axis=1
    )
    query_index = jnp.concatenate([base + jnp.arange(rows, dtype=jnp.int32) for base in bases])
    first_index = jnp.sum(
        (seg_all[:, None, :] < seg_query[:, :, None]).astype(jnp.int32), axis=-1
    )
    positions = (query_index[None] - first_index).reshape(micro, slots, rows)
    positions = positions.transpose(1, 0, 2)
    freqs = THETA_BASE ** (-2.0 * jnp.arange(ROPE // 2, dtype=f32) / ROPE)
    angles = positions.astype(f32)[..., None] * freqs
    cos_rows, sin_rows = jnp.cos(angles), jnp.sin(angles)
    cos_lanes = jnp.concatenate([cos_rows] * 4, axis=-1)
    sin_lanes = jnp.concatenate([-sin_rows, sin_rows] * 2, axis=-1)
    tables = (seg_query[..., None], seg_key, cos_lanes, sin_lanes)

    close(*arrived, down_b, hid_b, grad_own, inputs16)
    while len(attn_z) < tp_size - 1:
        close(*attention_round())
    arrived = attention_round()
    down_a1 = send(line_x, swap_x, down_a, free=True)
    down_b2 = send(line_y, swap_y, down_b, free=True)
    own_lanes = [lanes[0].reshape(own, LANES) for lanes in (cos_lanes, sin_lanes)]
    normed_own, latent_part, latent_pack, factor_one, factor_latent = in_one(
        begin_kernel,
        "begin",
        [
            ((own, width), bf16),
            ((own, KVRANK), f32),
            ((own, kv_cols), bf16),
            ((own, 1), f32),
            ((own, 1), f32),
        ],
        shift,
        behind(inputs16),
        gain_one[None],
        w_latent,
        gain_kv[None],
        *own_lanes,
    )
    latent_pack = latent_pack.reshape(micro, rows, kv_cols)
    close(*arrived, down_a1, down_b2, latent_pack)
    latent_z, grad_z = [latent_pack], [grad_own]

    def latents_ahead():
        if len(latent_z) < tp_size:
            latent_z.append(send(line_z, step_z, latent_z[-1]))
        return latent_z[-1]

    def grads_ahead(count):
        for _ in range(count):
            grad_z.append(send(line_z, step_z, grad_z[-1]))

    arrived = attention_round()
    down_b1 = send(line_x, swap_x, down_b, free=True)
    down_a2 = send(line_y, swap_y, down_a, free=True)
    close(*arrived, down_b1, down_a2, latents_ahead())
    arrived = attention_round()
    down_b3 = send(line_x, swap_x, down_b2, free=True)
    down_a3 = send(line_y, swap_y, down_a1, free=True)
    close(*arrived, down_b3, down_a3, latents_ahead())
    while len(wanted) > 2:
        close(*attention_round(), latents_ahead())
    arrived = attention_round()
    normed_chip = normed_own
    if split:
        normed_chip = jnp.concatenate([normed_own, send(line_c, swap_core, normed_own)])
    half_tp = tp_size // 2
    latent_far = [send(line_c, swap_core, jnp.concatenate(latent_z[:half_tp]))]
    while len(latent_z) < tp_size:
        latents_ahead()
    close(*arrived, normed_chip, latent_far[0], latent_z[-1])
    attn_xy = [[held[j, k] for k in range(4)] for j in range(tp_size)]

    hid_a1, hid_b2 = send(line_x, swap_x, hid_a), send(line_y, swap_y, hid_b)
    grads_ahead(1)
    latent_far.append(send(line_c, swap_core, jnp.concatenate(latent_z[half_tp:])))
    q_cols, out_cols = q_width, q_width + out_width

    def core_row(k, half):
        def row(ref):
            at = ref[0] if half == 0 else 1 - ref[0]
            return (2 * k + at) * slice_rows

        return (slice_rows, row)

    def expand_row(k, half):
        def row(ref):
            at = ref[0] if half == 0 else 1 - ref[0]
            return (2 * (ref[1] ^ k) + at) * expand_rows

        return (expand_rows, row)

    moves = []
    for j in range(tp_size):
        for k in range(4):
            for half in range(2):
                source, top = 4 * j + k, half * slice_rows
                moves.append(
                    (source, top, slice_rows, 0, q_width, 0, core_row(k, half), j * q_width)
                )
                moves.append(
                    (source, top, slice_rows, q_cols, out_width, 1, core_row(k, half), j * out_width)
                )
                for i in range(blocks_kv):
                    moves.append(
                        (
                            source,
                            top + i % stack * expand_rows,
                            expand_rows,
                            out_cols + i // stack * LANES,
                            LANES,
                            2,
                            expand_row(k, half),
                            j * kv_width + i * LANES,
                        )
                    )
    w_query, w_out, w_expand = assemble(
        [piece for pieces in attn_xy for piece in pieces],
        moves,
        [(width, tp_size * q_width), (width, tp_size * out_width), (KVRANK, tp_size * kv_width)],
        now(shift),
    )
    q_lin = dot(normed_chip, w_query).reshape(slots, micro, rows, tp_size * q_width)
    latent_rows = [
        [(at * span + (place_z - j) % tp_size * rows) for j in range(tp_size)]
        for at in (core, 1 - core)
    ]
    latent_all, rope_keys = lay_out(
        jnp.stack([row for each in latent_rows for row in each]).astype(jnp.int32),
        latent_z + latent_far,
        micro,
        length,
    )
    latent_all = latent_all.reshape(micro * length, KVRANK)
    kv_all = dot(latent_all, w_expand, bf16).reshape(micro, length, tp_size * kv_width)
    close(hid_a1, hid_b2, grad_z[-1], q_lin, kv_all)

    hid_b1, hid_a2 = send(line_x, swap_x, hid_b), send(line_y, swap_y, hid_a)
    more = tp_size - 3
    grads_ahead(more)
    grad_far = [send(line_c, swap_core, piece, free=True) for piece in grad_z[:2]]
    mixed = attend(heads, tp_size, window, scale, behind(place), q_lin, kv_all, rope_keys, *tables)
    mixed = mixed.reshape(slots * own, tp_size * out_width)
    close(hid_b1, hid_a2, grad_z[-1], *grad_far, mixed)

    hid_b3, hid_a3 = send(line_x, swap_x, hid_b2), send(line_y, swap_y, hid_a1)
    mixed = now(mixed)
    if split:
        mixed_out = dot_rt(mixed, w_out, bf16)
        middle = inputs + mixed_out[:own].astype(f32) + to_core(mixed_out[own:]).astype(f32)
    else:
        middle = inputs + dot_rt(mixed, w_out)
    factor_two = norm_scale(middle)
    normed_two = (middle * factor_two * gain_two).astype(bf16)
    norm_z = [normed_two, send(line_z, step_z, normed_two)]
    norm_far = [send(line_c, swap_core, normed_two)]
    for piece in grad_z[2:]:
        grad_far.append(send(line_c, swap_core, piece))
    close(hid_b3, hid_a3, norm_z[-1], *norm_far, *grad_far[2:])

    hidden_pieces = [hid_a, hid_a1, hid_a2, hid_a3, hid_b, hid_b1, hid_b2, hid_b3]
    down_pieces = [down_a, down_a1, down_a2, down_a3, down_b, down_b1, down_b2, down_b3]
    whole, back_parts, out_parts = [], [], []

    class Ring:
        def __init__(self, parts):
            self.parts, self.at, self.total, self.seen = parts, 0, None, {}

        def block(self, j):
            if j not in self.seen:
                own_part, far_part = self.parts[j]
                self.seen[j] = add16(own_part, send(line_c, swap_core, far_part))
            return self.seen[j]

        def step(self):
            if self.at == tp_size - 1:
                return ()
            self.at += 1
            total = self.block(self.at)
            if self.total is not None:
                total = add16(total, self.total)
            self.total = send(line_z, step_z, total)
            return (self.total,)

        def result(self):
            while self.step():
                pass
            return self.total.astype(f32) + self.block(0).astype(f32)

    back_ring, out_ring = Ring(back_parts), Ring(out_parts)
    for j in range(tp_size):
        arrived = []
        if len(norm_z) < tp_size:
            norm_z.append(send(line_z, step_z, norm_z[-1]))
            arrived.append(norm_z[-1])
        elif len(grad_z) < tp_size:
            grads_ahead(1 if j + 2 < tp_size else tp_size - len(grad_z))
            arrived.append(grad_z[-1])
        elif back_ring.at + 1 < len(back_parts):
            arrived += back_ring.step()
        if j + 1 < tp_size:
            norm_far.append(send(line_c, swap_core, norm_z[j + 1]))
            arrived.append(norm_far[-1])
        while len(grad_far) <= j:
            grad_far.append(send(line_c, swap_core, grad_z[len(grad_far)], free=True))
        made = feed(
            behind(shift),
            j,
            tp_size,
            [norm_z[j], norm_far[j], grad_z[j], grad_far[j]],
            hidden_pieces,
            down_pieces,
            whole,
        )
        back_parts.append(made[:2])
        out_parts.append(made[2:4])
        whole = made[4:]
        close(*arrived, made[0])
    act_all, hidden_all, normed_all, grad_all = whole

    first, second = ((3, 0), (2, 0), (3, 1), (1, 1)), ((1, 0), (0, 0), (2, 1), (0, 1))
    arrived = back_ring.step()
    down_y, down_x, down_kept = weight_grad(
        behind(shift), SENT_BLOCKS, slice_rows, grad_all, act_all
    )
    close(*arrived, down_y)

    down_y, down_x = send(line_y, swap_y, down_y), send(line_x, swap_x, down_x)
    arrived = []
    while back_ring.at < tp_size - 1:
        arrived += back_ring.step()
    back_ring.block(0)
    own3, own2, far3, far1 = weight_grad(
        behind(shift), [(block,) for block in first], slice_rows, normed_all, hidden_all
    )
    close(*arrived, down_y, down_x, own3)

    own3, far3 = send(line_y, swap_y, own3), send(line_x, swap_x, far3)
    arrived = out_ring.step()
    grad_mid_norm, grad_gain_two = norm_back(middle, factor_two, gain_two, back_ring.result())
    grad_middle = grad_own.astype(f32) + grad_mid_norm
    grad_attn = grad_middle.astype(bf16)
    attn_far = send(line_c, swap_core, grad_attn, free=True)
    own1, own0, far2, far0 = weight_grad(
        behind(shift), [(block,) for block in second], slice_rows, normed_all, hidden_all
    )
    close(*arrived, own3, far3, attn_far, own1)

    own2, far1 = send(line_y, swap_y, own2), send(line_x, swap_x, far1)

    if split:
        grad_attn = jnp.concatenate([grad_attn, attn_far])
    grad_mixed = dot(grad_attn, w_out, bf16)
    out_blocks = [dot_lt(columns(grad_attn, k), mixed, bf16) for k in range(4)]
    close(own2, far1, grad_mixed, *out_blocks)

    def cut(value):
        middle_row = value.shape[0] // 2
        return value[:middle_row], value[middle_row:]

    def block_of(blocks, k, half):
        return cut(blocks[k])[half]

    def sent_of(blocks):
        return [jnp.concatenate([block_of(blocks, *at) for at in pair]) for pair in SENT_BLOCKS[:2]]

    def kept_of(blocks):
        return jnp.concatenate([block_of(blocks, *at) for at in SENT_BLOCKS[2]])

    def stage_one(over_y, over_x):
        return send(line_y, swap_y, over_y, free=True), send(line_x, swap_x, over_x, free=True)

    def stage_two(kept, sent):
        (top1, top0), (low2, low0) = (cut(each) for each in cut(kept))
        (top3, top2), (low3, low1) = cut(now(sent[0])), cut(now(sent[1]))
        top1 = send(line_x, swap_x, add16(top1, top3), free=True)
        low2 = send(line_y, swap_y, add16(low2, low3), free=True)
        return (top0, top2, top1), (low0, low1, low2)

    def stage_sum(tops, lows):
        return jnp.concatenate([add16(*tops), add16(*lows)])

    (down3, down2), (downf3, downf1) = cut(down_y), cut(down_x)
    (down1, down0), (downf2, downf0) = (cut(each) for each in cut(down_kept))
    over_x = send(
        line_x, swap_x, jnp.concatenate([add16(own1, now(own3)), add16(down1, down3)], axis=1)
    )
    over_y = send(
        line_y, swap_y, jnp.concatenate([add16(far2, now(far3)), add16(downf2, downf3)], axis=1)
    )
    arrived = out_ring.step()
    out_sent = stage_one(*sent_of(out_blocks))
    made = attend_back(
        heads,
        tp_size,
        window,
        scale,
        behind(place),
        q_lin,
        kv_all,
        rope_keys,
        *tables,
        grad_mixed.reshape(slots, micro, rows, tp_size * out_width),
        normed_chip,
        latent_all,
        w_query,
        w_expand,
    )
    sums, (latent_mine, latent_others), parts = made[:6], made[6:8], made[8:]
    close(over_x, over_y, *arrived, *out_sent, sums[0])

    query_sent = stage_one(*sums[:2])
    latent_far = send(line_c, swap_core, latent_others)
    arrived = []
    while out_ring.at < tp_size - 1:
        arrived += out_ring.step()
    hid_own = add16(own0, own2, over_x[:, : 2 * part])
    hid_other = add16(far0, far1, over_y[:, : 2 * part])
    down_own = add16(down0, down2, over_x[:, 2 * part :])
    down_other = add16(downf0, downf1, over_y[:, 2 * part :])
    close(*query_sent, *arrived, latent_far, hid_own, hid_other, down_own, down_other)

    latent_sum = add16(latent_mine, now(latent_far))

    def latent_block(j):
        return lax.dynamic_slice_in_dim(latent_sum, (place_z - j) % tp_size * rows, rows, 1)

    latent_step = send(line_z, step_z, latent_block(1))
    out_sums = stage_two(kept_of(out_blocks), out_sent)
    expand_sent = stage_one(*sums[3:5])
    output = (middle + out_ring.result()).astype(bf16)
    close(latent_step, out_sums[0][2], out_sums[1][2], *expand_sent, output)

    class Columns:
        def __init__(self, sums, count):
            self.value, self.count, self.at = stage_sum(*sums), count, 1
            self.total = self.block(1)

        def block(self, j):
            return self.value[:, self.count * j : self.count * (j + 1)]

        def step(self):
            if self.at > tp_size - 1:
                return ()
            self.total = line_z.send(step_z, now(self.total), free=True)
            self.at += 1
            return (self.total,)

        def add(self):
            if self.at <= tp_size:
                self.total = add16(now(self.total), self.block(self.at % tp_size))
                if self.at == tp_size:
                    self.at += 1

    for j in range(2, tp_size - 1):
        latent_step = send(line_z, step_z, add16(now(latent_step), latent_block(j)))
    expand_sums = stage_two(sums[5], expand_sent)
    out_columns = Columns(out_sums, out_width)
    arrived = out_columns.step()
    hid_far = send(line_c, swap_core, hid_other)
    close(latent_step, expand_sums[0][2], expand_sums[1][2], *arrived, hid_far)

    latent_step = send(line_z, step_z, add16(now(latent_step), latent_block(tp_size - 1)))
    query_sums = stage_two(sums[2], query_sent)
    out_columns.add()
    expand_columns = Columns(expand_sums, kv_width)
    arrived = [*out_columns.step(), *expand_columns.step()]
    far_part = None
    if split:
        far_part = send(line_c, swap_core, parts[1].reshape(own, width))
    down_far = send(line_c, swap_core, down_other, free=True)
    close(latent_step, query_sums[0][2], query_sums[1][2], *arrived, down_far, far_part)

    query_columns = Columns(query_sums, q_width)
    out_columns.add()
    expand_columns.add()
    arrived = [*query_columns.step(), *expand_columns.step(), *out_columns.step()]
    others_of = [] if far_part is None else [far_part]
    kernel = finish_kernel
    if far_part is None:
        kernel = lambda *refs: finish_kernel(*refs[:9], None, *refs[9:])
    gathered_rows = 4 * (width // 8 + 16)
    input_grad, w_mine, w_other = in_one(
        kernel,
        "finish",
        [((own, width), bf16), *[((gathered_rows, kv_cols), bf16)] * 2],
        shift,
        behind(latent_step).reshape(own, kv_cols),
        latent_block(0).reshape(own, kv_cols),
        latent_part,
        factor_latent,
        gain_kv[None],
        *own_lanes,
        parts[0].reshape(own, width),
        *others_of,
        w_latent,
        inputs16,
        factor_one,
        gain_one[None],
        grad_middle,
        normed_own,
        grad_gain_two[None],
        scratch=[((1, width), f32), ((1, KVRANK), f32), ((width, kv_cols), bf16)],
    )
    close(*arrived, input_grad)

    rings = [query_columns, expand_columns]
    for ring in rings:
        ring.add()
    arrived = [step for ring in rings for step in ring.step()]
    w_sum = add16(w_mine, send(line_c, swap_core, w_other, free=True))
    high = w_sum.shape[0] // 4
    w_far = [
        lax.ppermute(w_sum[high * k : high * (k + 1)], "shard", [(i, i ^ k) for i in range(4)])
        for k in (1, 2, 3)
    ]
    grad_wgate, grad_wup, grad_wdown = spread(
        behind(shift), hidden_here, hid_own, hid_far, down_own, down_far
    )
    grad_wgate, grad_wup = grad_wgate.T, grad_wup.T
    close(*arrived, *w_far, grad_wdown)

    w_sum = add16(w_sum[:high], *(now(each) for each in w_far))
    for ring in rings:
        ring.add()
    arrived = [step for ring in rings for step in ring.step()]

    def rows_for(at):
        rows_at = lax.dynamic_slice_in_dim(w_sum, at * small_rows, small_rows, 0)
        return jnp.concatenate([rows_at, w_sum[high - 16 :]])

    w_here = rows_for(place_z).astype(f32)
    for j in range(1, tp_size):
        pairs = [(i, (i + j) % tp_size) for i in range(tp_size)]
        w_here = w_here + lax.ppermute(rows_for((place_z + j) % tp_size), "tp", pairs).astype(f32)
    grad_wlatent, gains = w_here[:small_rows], w_here[small_rows]

    def own_gains(start, count):
        each = count // tp_size
        return lax.dynamic_slice_in_dim(gains[start : start + count], place_z * each, each, 0)

    grad_gain_one, grad_gain_two = own_gains(0, width // 8), own_gains(width // 8, width // 8)
    grad_gain_latent = own_gains(width // 4, KVRANK // 8)
    close(*arrived)
    for ring in (*rings, out_columns):
        while ring.at <= tp_size:
            ring.add()
            if ring.at < tp_size:
                ring.total = step_z(ring.total)
                ring.at += 1
    query_here, expand_here, out_here = (ring.total for ring in (*rings, out_columns))

    def finished(value, here_rows):
        halves = value.reshape(cores, here_rows, value.shape[1])
        kept, given = mine(halves, 0), swap_core(others(halves, 0))
        if split:
            return in_order(core, kept[:, None], given[:, None], 1).astype(f32)
        return (kept.astype(f32) + given.astype(f32))[:, None]

    grad_wout = finished(out_here, slice_rows).reshape(slice_rows, -1).T
    grad_wexpand = finished(expand_here, expand_rows).reshape(expand_rows, -1)
    grad_wquery = q_disorder(finished(query_here, slice_rows))
    like = (micro, 1, rows, width)
    return (
        features(output).reshape(like),
        features(input_grad).reshape(like),
        grad_gain_one,
        grad_wquery,
        grad_wlatent,
        grad_gain_latent,
        grad_wexpand,
        grad_wout,
        grad_gain_two,
        grad_wgate,
        grad_wup,
        grad_wdown,
    )


def solution(mesh):
    tokens = P(None, "shard", ("ctx", "tp"), None)
    everywhere = P(("shard", "ctx", "tp"))
    down_split = P(("shard", "ctx"), "tp")
    up_split = P("tp", ("shard", "ctx"))
    whole_rows = P(("shard", "ctx", "tp"), None)
    return jax.shard_map(
        shards,
        mesh=mesh,
        in_specs=(
            tokens,
            P(None, "shard", None),
            tokens,
            everywhere,
            down_split,
            whole_rows,
            everywhere,
            down_split,
            up_split,
            everywhere,
            down_split,
            down_split,
            up_split,
        ),
        out_specs=(
            tokens,
            tokens,
            everywhere,
            down_split,
            whole_rows,
            everywhere,
            down_split,
            up_split,
            everywhere,
            down_split,
            down_split,
            up_split,
        ),
        check_vma=False,
    )
```
